256 devices in a mesh: band: 32 (over z, y_lo, core), hid: 8 (over x, y_hi).
Axes of the slice: x: 4, y: 4 (y_hi: 2, y_lo: 2; y = y_hi * 2 + y_lo), z: 8, core: 2. Of those that a mesh axis runs over, the one named last changes fastest.
Arguments:
- pair: float32 [768, 768, 128], P('band', 'hid'), may hold values from -40 to 40
- residue_mask: int32 [768], replicated, may hold values 0 or 1
- hotspot: int32 [768], replicated, may hold values 0 or 1
- interface: int32 [768, 768], P('band', 'hid'), may hold values 0 or 1
- proj_weight: float32 [2, 128, 512], replicated, may hold values from -0.5 to 0.5
- gate_weight: float32 [2, 128, 128], replicated, may hold values from -0.5 to 0.5
- out_weight: float32 [2, 128, 128], replicated, may hold values from -0.5 to 0.5
Outputs:
- pair_out: float32 [768, 768, 128], P('band', 'hid')
The draws below stay inside these ranges and needn't reach their ends.
All inputs are finite; a program needn't handle non-finite values. No bound on the sum of `interface` on one device may be relied on, other than what follows from the above.
Results may differ from the reference program's by a relative error of at most 0.0021.
Values may be sent and summed in bfloat16 or wider, within the bound.
No kernel may reach another device: no remote copies, remote signals or barrier semaphores. Data moves between devices by JAX's collectives and lax.ppermute only.
A program may use at most 128 MiB of HBM per device.

```python
import math
import jax
import jax.numpy as jnp
from jax import lax

C = 128
CH = 128
N = 768


def draw_pair(key, part):
    key_base, key_chan = jax.random.split(key, 2)
    channel_scale = jnp.exp(jax.random.uniform(key_chan, (C,), jnp.float32, math.log(0.3), math.log(3.0)))
    base = jax.random.normal(key_base, (N, N, C), jnp.float32)
    values = base * channel_scale
    return jnp.clip(values, -40.0, 40.0)


def place_ends(array, own_key, least, largest):
    index_at = [jax.random.randint(jax.random.fold_in(own_key, axis), (), 0, length) for axis, length in enumerate(array.shape)]
    main_axis = array.shape.index(max(array.shape))
    beside = index_at[:main_axis] + [(index_at[main_axis] + 1) % array.shape[main_axis]] + index_at[main_axis + 1:]
    return array.at[tuple(index_at)].set(least).at[tuple(beside)].set(largest)


def normal_values(stream_key, dims, deviation, bound, dtype=jnp.bfloat16):
    return jnp.clip(deviation * jax.random.normal(stream_key, dims, jnp.float32), -bound, bound).astype(dtype)


def setup_inputs(seed: int = 0) -> dict:
    key_list = jax.random.split(jax.random.key(seed), 8)
    pair = draw_pair(jax.random.fold_in(key_list[7], 71), 0)
    residue_mask = place_ends((jax.random.randint(key_list[1], (N,), 0, 16) < 15).astype(jnp.int32), jax.random.fold_in(key_list[1], 1), 0, 1)
    hotspot = place_ends((jax.random.randint(key_list[2], (N,), 0, 8) < 1).astype(jnp.int32), jax.random.fold_in(key_list[2], 1), 0, 1)
    interface = place_ends((jax.random.randint(key_list[3], (N, N), 0, 4) < 3).astype(jnp.int32), jax.random.fold_in(key_list[3], 1), 0, 1)
    proj_weight = normal_values(key_list[4], (2, C, 4 * CH), C ** -0.5, 0.5, jnp.float32)
    gate_weight = normal_values(key_list[5], (2, C, C), C ** -0.5, 0.5, jnp.float32)
    out_weight = normal_values(key_list[6], (2, CH, C), CH ** -0.5, 0.5, jnp.float32)
    return dict(pair=pair, residue_mask=residue_mask, hotspot=hotspot, interface=interface, proj_weight=proj_weight, gate_weight=gate_weight, out_weight=out_weight)


EPS = 1e-05
HIGH = lax.Precision.HIGHEST

def normalize(values):
    average = lax.optimization_barrier(jnp.mean(values, axis=-1, keepdims=True))
    centred = values - average
    variance = lax.optimization_barrier(jnp.mean(centred * centred, axis=-1, keepdims=True))
    return centred * lax.rsqrt(variance + EPS)

def reference(pair, residue_mask, hotspot, interface, proj_weight, gate_weight, out_weight):
    flags = jnp.maximum(interface, jnp.maximum(hotspot[:, None], hotspot[None, :]))
    edge = (residue_mask[:, None] * residue_mask[None, :] * flags).astype(jnp.float32)
    state = pair
    for layer in range(2):
        normed = normalize(state)
        proj = jnp.einsum('ikc,cf->fik', normed, proj_weight[layer], precision=HIGH)
        left = (edge * jax.nn.sigmoid(proj[CH:2 * CH]) * proj[:CH]).astype(jnp.bfloat16)
        right = (edge * jax.nn.sigmoid(proj[3 * CH:]) * proj[2 * CH:3 * CH]).astype(jnp.bfloat16)
        left_f = left.astype(jnp.float32)
        right_f = right.astype(jnp.float32)
        if layer == 0:
            tri = jnp.einsum('hik,hjk->hij', left_f, right_f, precision=HIGH)
        else:
            tri = jnp.einsum('hki,hkj->hij', left_f, right_f, precision=HIGH)
        average = lax.optimization_barrier(jnp.mean(tri, axis=0))
        variance = lax.optimization_barrier(jnp.mean(tri * tri, axis=0)) - average * average
        scaled = (tri - average) * lax.rsqrt(variance + EPS)
        projected = jnp.einsum('hij,hc->ijc', scaled, out_weight[layer], precision=HIGH)
        gating = jax.nn.sigmoid(jnp.einsum('ijd,dc->ijc', normed, gate_weight[layer], precision=HIGH))
        state = state + gating * projected
    return state
```

```python
import jax
import jax.numpy as jnp
from jax import lax
from jax.experimental import pallas as pl
from jax.experimental.pallas import tpu as pltpu
from jax.sharding import Mesh, PartitionSpec as P

EPS = 1e-05
F32 = jnp.float32
BF16 = jnp.bfloat16
ROWS = 24
COLS = 96
PIX = ROWS * COLS
CH = 128
MSG = 40
CHIPS = ("z", "yl", "x", "yh")


def split_bf16(value):
    high = value.astype(BF16)
    low = (value - high.astype(F32)).astype(BF16)
    return high, low


def lanes(shape):
    return lax.broadcasted_iota(jnp.int32, shape, len(shape) - 1)


def matmul(a, b, dims):
    return lax.dot_general(a, b, (dims, ((), ())), preferred_element_type=F32)


def edge_rows(mask_sm, hot_sm, mask_ref, hot_ref, inter_ref, edge_ref):
    band = (lax.axis_index("z") * 2 + lax.axis_index("yl")) * 2 + lax.axis_index("core")
    hid = lax.axis_index("x") * 2 + lax.axis_index("yh")
    shift = (8 - hid) * COLS
    col_mask = pltpu.roll(jnp.broadcast_to(mask_ref[...], (8, 768)), shift, 1)[0:1, 0:128]
    col_hot = pltpu.roll(jnp.broadcast_to(hot_ref[...], (8, 768)), shift, 1)[0:1, 0:128]
    col_mask = jnp.where(lanes((1, 128)) < COLS, col_mask, 0)
    for r in range(ROWS):
        flags = jnp.maximum(inter_ref[r : r + 1, :], jnp.maximum(col_hot[:, :COLS], hot_sm[band * ROWS + r]))
        value = flags * col_mask[:, :COLS] * mask_sm[band * ROWS + r]
        edge_ref[r : r + 1, :] = jnp.zeros((1, 128), F32)
        edge_ref[r : r + 1, 0:COLS] = value.astype(F32)


def project(state_ref, proj_ref, gatew_ref, edge_ref, norm_ref, mix_ref, keep_ref, send_ref, gate_ref):
    gate_hi, gate_lo = split_bf16(gatew_ref[...])
    gate_cat = jnp.concatenate([gate_hi, gate_lo, gate_hi], axis=0)

    def normalize(r, carry):
        at = pl.ds(pl.multiple_of(r * COLS, COLS), COLS)
        x = state_ref[at, :]
        centred = x - jnp.mean(x, axis=-1, keepdims=True)
        variance = jnp.mean(centred * centred, axis=-1, keepdims=True)
        high, low = split_bf16(centred * lax.rsqrt(variance + EPS))
        cat = jnp.concatenate([high, high, low], axis=1)
        norm_ref[at, :] = cat
        gate_ref[at, :] = jax.nn.sigmoid(matmul(cat, gate_cat, ((1,), (0,))))
        return carry

    lax.fori_loop(0, ROWS, normalize, 0, unroll=2)
    norm_ref[PIX : PIX + 32, :] = jnp.zeros((32, 384), BF16)
    w_hi, w_lo = split_bf16(proj_ref[...].T)
    w_cat = jnp.concatenate([w_hi, w_lo, w_hi], axis=1)

    def pair_row(r):
        at = pl.ds(pl.multiple_of(r * COLS, COLS), 128)
        values = matmul(w_cat, norm_ref[at, :], ((1,), (1,)))
        edge = edge_ref[pl.ds(r, 1), :]
        left = edge * jax.nn.sigmoid(values[CH : 2 * CH]) * values[:CH]
        right = edge * jax.nn.sigmoid(values[3 * CH :]) * values[2 * CH : 3 * CH]
        return left, right

    lane = lanes((CH, 128))

    def last(q, carry):
        left, right = pair_row(q + 16)
        keep_ref[q] = right
        mix_ref[pl.ds(q + 16, CH, stride=MSG), :] = jnp.where(lane < COLS, left, pltpu.roll(right, 32, 1))
        return carry

    def first(r, carry):
        left, right = pair_row(r)
        third = r // 8
        tail = pltpu.roll(keep_ref[r - 8 * third], 96 - 32 * third, 1)
        mix_ref[pl.ds(r, CH, stride=MSG), :] = jnp.where(lane < COLS, left, tail)
        mix_ref[pl.ds(r + 24, CH, stride=MSG), :] = right
        return carry

    lax.fori_loop(0, 8, last, 0)
    lax.fori_loop(0, 16, first, 0)

    def pack(h, carry):
        at = pl.ds(pl.multiple_of(h * MSG, MSG), MSG)
        send_ref[h] = mix_ref[at, :].astype(BF16)
        return carry

    lax.fori_loop(0, CH, pack, 0, unroll=8)


def first_kernel(mask_sm, hot_sm, mask_ref, hot_ref, inter_ref, state_ref, proj_ref, gatew_ref,
                 send_ref, gate_ref, edge_ref, norm_ref, mix_ref, keep_ref):
    edge_rows(mask_sm, hot_sm, mask_ref, hot_ref, inter_ref, edge_ref)
    project(state_ref, proj_ref, gatew_ref, edge_ref, norm_ref, mix_ref, keep_ref, send_ref, gate_ref)


def unpack(block):
    lane = lanes((8, 128))
    third = jnp.where(lane < 64, pltpu.roll(block[8:16], 64, 1), pltpu.roll(block[16:24], 96, 1))
    third = jnp.where(lane < 32, pltpu.roll(block[0:8], 32, 1), third)
    third = jnp.where(lane < COLS, third, 0.0)
    return block[0:24], jnp.concatenate([block[24:40], third], axis=0)


def outgoing_kernel(own_ref, other_ref, out_ref, left_ref, right_ref):
    core = lax.axis_index("core")

    def place(b, carry):
        z = b // 2
        base = z * 128 + (b - 2 * z) * 48
        rows = pl.ds(pl.multiple_of(b * 24, 24), 24)
        mine = pl.ds(pl.multiple_of(base + core * 24, 8), 24)
        theirs = pl.ds(pl.multiple_of(base + 24 - core * 24, 8), 24)
        for g in range(8):
            at = slice(128 * g, 128 * g + 128)
            left, right = unpack(own_ref[b * 8 + g].astype(F32))
            left_ref[rows, at] = left
            right_ref[mine, at] = right
            _, right = unpack(other_ref[b * 8 + g].astype(F32))
            right_ref[theirs, at] = right
        return carry

    lax.fori_loop(0, 16, place, 0)
    for z in range(8):
        right_ref[128 * z + 96 : 128 * z + 128, :] = jnp.zeros((32, 1024), F32)
    left = left_ref[...].astype(BF16)
    for g in range(8):
        tri = matmul(left, right_ref[128 * g : 128 * g + 128, :].astype(BF16), ((1,), (1,)))
        for b in range(16):
            out_ref[b * 8 + g] = tri[24 * b : 24 * b + 24].astype(BF16)


def incoming_kernel(own_ref, other_ref, out_ref, left_ref, right_ref, tri_ref):
    core = lax.axis_index("core")

    def place(b, carry):
        rows = pl.ds(pl.multiple_of(b * 24, 24), 24)
        rows2 = pl.ds(pl.multiple_of(384 + b * 24, 24), 24)
        for g in range(8):
            at = slice(128 * g, 128 * g + 128)
            left_ref[rows, at], right_ref[rows, at] = unpack(own_ref[b * 8 + g].astype(F32))
            left_ref[rows2, at], right_ref[rows2, at] = unpack(other_ref[b * 8 + g].astype(F32))
        return carry

    lax.fori_loop(0, 16, place, 0)
    right = right_ref[...].astype(BF16)
    for z in range(8):
        left = left_ref[:, 128 * z : 128 * z + 128].T.astype(BF16)
        tri_ref[...] = matmul(left, right, ((1,), (0,)))
        for y in range(2):
            rows = tri_ref[pl.ds(pl.multiple_of(48 * y + 24 * core, 8), 24), :].astype(BF16)
            for g in range(8):
                out_ref[(2 * z + y) * 8 + g] = rows[:, 128 * g : 128 * g + 128]


def finish(tri_ref, state_ref, gate_ref, outw_ref, scaled_ref, next_ref):
    def stats(h, carry):
        total, square = carry
        t = tri_ref[h].astype(F32)
        return total + t, square + t * t

    zero = jnp.zeros((24, 128), F32)
    total, square = lax.fori_loop(0, CH, stats, (zero, zero), unroll=8)
    average = total * (1.0 / CH)
    scale = lax.rsqrt(square * (1.0 / CH) - average * average + EPS)

    def rescale(h, carry):
        at = pl.ds(pl.multiple_of(h * 24, 24), 24)
        scaled_ref[at, :] = (tri_ref[h].astype(F32) - average) * scale
        return carry

    lax.fori_loop(0, CH, rescale, 0, unroll=8)
    w_hi, w_lo = split_bf16(outw_ref[...])
    w_cat = jnp.concatenate([w_hi, w_lo, w_hi], axis=0)

    def combine(r, carry):
        scaled = scaled_ref[pl.ds(r, CH, stride=24), :].T[:COLS]
        high, low = split_bf16(scaled)
        cat = jnp.concatenate([high, high, low], axis=1)
        at = pl.ds(pl.multiple_of(r * COLS, COLS), COLS)
        next_ref[at, :] = state_ref[at, :] + gate_ref[at, :] * matmul(cat, w_cat, ((1,), (0,)))
        return carry

    lax.fori_loop(0, ROWS, combine, 0, unroll=2)


def middle_kernel(mask_sm, hot_sm, mask_ref, hot_ref, inter_ref, tri_ref, state_ref, gate_ref, outw_ref, proj_ref,
                  gatew_ref, next_ref, send_ref, gate2_ref, edge_ref, norm_ref, mix_ref, keep_ref, scaled_ref):
    finish(tri_ref, state_ref, gate_ref, outw_ref, scaled_ref, next_ref)
    edge_rows(mask_sm, hot_sm, mask_ref, hot_ref, inter_ref, edge_ref)
    project(next_ref, proj_ref, gatew_ref, edge_ref, norm_ref, mix_ref, keep_ref, send_ref, gate2_ref)


def last_kernel(tri_ref, state_ref, gate_ref, outw_ref, next_ref, scaled_ref):
    finish(tri_ref, state_ref, gate_ref, outw_ref, scaled_ref, next_ref)


VM = pl.BlockSpec(memory_space=pltpu.VMEM)
SM = pl.BlockSpec(memory_space=pltpu.SMEM)
STATE = jax.ShapeDtypeStruct((PIX, CH), F32)
SEND = jax.ShapeDtypeStruct((CH, MSG, 128), BF16)
TRI = jax.ShapeDtypeStruct((CH, 24, 128), BF16)
PROJECT_SCRATCH = [
    pltpu.VMEM((24, 128), F32),
    pltpu.VMEM((PIX + 32, 384), BF16),
    pltpu.VMEM((CH * MSG, 128), F32),
    pltpu.VMEM((8, CH, 128), F32),
]


def exchange(message):
    return lax.all_to_all(message, CHIPS, split_axis=0, concat_axis=0, tiled=True)


def triangle(kernel, message, scratch):
    own = exchange(message)
    other = lax.ppermute(own, "core", [(0, 1), (1, 0)])
    tri = pl.pallas_call(kernel, out_shape=TRI, in_specs=[VM, VM], out_specs=VM, scratch_shapes=scratch)(own, other)
    return exchange(tri)


def on_device(pair, residue_mask, hotspot, interface, proj_weight, gate_weight, out_weight):
    state = pair.reshape(PIX, CH)
    flags = (residue_mask, hotspot, residue_mask.reshape(1, 768), hotspot.reshape(1, 768), interface)
    flag_specs = [SM, SM, VM, VM, VM]
    send, gate = pl.pallas_call(
        first_kernel, out_shape=(SEND, STATE), in_specs=flag_specs + [VM] * 3, out_specs=(VM, VM),
        scratch_shapes=PROJECT_SCRATCH,
    )(*flags, state, proj_weight[0], gate_weight[0])
    tri = triangle(outgoing_kernel, send, [pltpu.VMEM((384, 1024), F32), pltpu.VMEM((1024, 1024), F32)])
    state, send, gate = pl.pallas_call(
        middle_kernel, out_shape=(STATE, SEND, STATE), in_specs=flag_specs + [VM] * 6, out_specs=(VM, VM, VM),
        scratch_shapes=PROJECT_SCRATCH + [pltpu.VMEM((CH * 24, 128), F32)],
    )(*flags, tri, state, gate, out_weight[0], proj_weight[1], gate_weight[1])
    tri = triangle(
        incoming_kernel, send,
        [pltpu.VMEM((768, 1024), F32), pltpu.VMEM((768, 1024), F32), pltpu.VMEM((128, 1024), F32)],
    )
    state = pl.pallas_call(
        last_kernel, out_shape=STATE, in_specs=[VM] * 4, out_specs=VM, scratch_shapes=[pltpu.VMEM((CH * 24, 128), F32)],
    )(tri, state, gate, out_weight[1])
    return state.reshape(ROWS, COLS, CH)


def solution(mesh):
    grid = Mesh(mesh.devices.reshape(8, 2, 2, 4, 2), ("z", "yl", "core", "x", "yh"))
    rows = ("z", "yl", "core")
    cols = ("x", "yh")
    return jax.shard_map(
        on_device,
        mesh=grid,
        in_specs=(P(rows, cols, None), P(), P(), P(rows, cols), P(), P(), P()),
        out_specs=P(rows, cols, None),
        check_vma=False,
    )
```

```python
import jax
import jax.numpy as jnp
from jax import lax
from jax.experimental import pallas as pl
from jax.experimental.pallas import tpu as pltpu
from jax.sharding import Mesh, PartitionSpec as P

EPS = 1e-05
F32 = jnp.float32
BF16 = jnp.bfloat16
ROWS = 24
COLS = 96
PIX = ROWS * COLS
CH = 128
PACK = 18
CHIPS = ("z", "yl", "x", "yh")


def split_bf16(value):
    high = value.astype(BF16)
    low = (value - high.astype(F32)).astype(BF16)
    return high, low


def lanes(shape):
    return lax.broadcasted_iota(jnp.int32, shape, len(shape) - 1)


def matmul(a, b, dims):
    return lax.dot_general(a, b, (dims, ((), ())), preferred_element_type=F32)


def aligned(start, size, unit):
    return pl.ds(pl.multiple_of(start, unit), size)


def packed_edge(mask_sm, hot_sm, inter_ref, edge_ref, rows_ref):
    band = (lax.axis_index("z") * 2 + lax.axis_index("yl")) * 2 + lax.axis_index("core")
    hid = lax.axis_index("x") * 2 + lax.axis_index("yh")
    lane = lanes((1, 128))
    col_mask = jnp.zeros((1, 128), jnp.int32)
    col_hot = jnp.zeros((1, 128), jnp.int32)
    for c in range(COLS):
        col_mask = jnp.where(lane == c, mask_sm[hid * COLS + c], col_mask)
        col_hot = jnp.where(lane == c, hot_sm[hid * COLS + c], col_hot)
    rows_ref[...] = jnp.zeros((ROWS, 128), jnp.int32)
    rows_ref[:, 0:COLS] = inter_ref[...]
    for r in range(ROWS):
        at = slice(r, r + 1)
        flags = jnp.maximum(rows_ref[at, :], jnp.maximum(col_hot, hot_sm[band * ROWS + r]))
        rows_ref[at, :] = flags * col_mask * mask_sm[band * ROWS + r]
    for t in range(PACK):
        tail = pltpu.roll(jnp.broadcast_to(rows_ref[18 + t % 6 : 19 + t % 6, :], (8, 128)), 96 - 32 * (t // 6), 1)
        edge_ref[t : t + 1, :] = jnp.where(lane < COLS, rows_ref[t : t + 1, :], tail[0:1, :]).astype(F32)


def tail_pixels(t):
    return aligned((18 + t % 6) * COLS + 32 * (t // 6), 32, 32)


def project(state_ref, weight, edge_ref, norm_ref, mix_ref, send_ref):
    def normalize(t, carry):
        x = jnp.concatenate([state_ref[aligned(t * COLS, COLS, COLS), :], state_ref[tail_pixels(t), :]], axis=0)
        centred = x - jnp.mean(x, axis=-1, keepdims=True)
        variance = jnp.mean(centred * centred, axis=-1, keepdims=True)
        high, low = split_bf16(centred * lax.rsqrt(variance + EPS))
        at = aligned(t * 128, 128, 128)
        norm_ref[at, 0:128] = high
        norm_ref[at, 128:256] = high
        norm_ref[at, 256:384] = low
        return carry

    lax.fori_loop(0, PACK, normalize, 0, unroll=3)
    w_hi, w_lo = split_bf16(weight.T)
    w_cat = jnp.concatenate([w_hi, w_lo, w_hi], axis=1)

    def pair(i, carry):
        values = matmul(w_cat, norm_ref[aligned(i * 256, 256, 256), :], ((1,), (1,)))
        for half in range(2):
            t = 2 * i + half
            part = values[:, 128 * half : 128 * half + 128]
            edge = edge_ref[pl.ds(t, 1), :]
            left = edge * jax.nn.sigmoid(part[CH : 2 * CH]) * part[:CH]
            right = edge * jax.nn.sigmoid(part[3 * CH :]) * part[2 * CH : 3 * CH]
            mix_ref[pl.ds(t, CH, stride=2 * PACK), :] = left
            mix_ref[pl.ds(t + PACK, CH, stride=2 * PACK), :] = right
        return carry

    lax.fori_loop(0, PACK // 2, pair, 0, unroll=3)

    def convert(i, carry):
        at = aligned(i * 256, 256, 256)
        send_ref[at, :] = mix_ref[at, :].astype(BF16)
        return carry

    lax.fori_loop(0, 18, convert, 0)


def first_kernel(mask_sm, hot_sm, inter_ref, state_ref, proj_ref, send_ref, edge_ref, rows_ref, norm_ref, mix_ref):
    packed_edge(mask_sm, hot_sm, inter_ref, edge_ref, rows_ref)
    project(state_ref, proj_ref[0], edge_ref, norm_ref, mix_ref, send_ref)


def gate_kernel(layer):
    def body(state_ref, gatew_ref, gate_ref):
        hi, lo = split_bf16(gatew_ref[layer])
        cat = jnp.concatenate([hi, lo, hi], axis=0)

        def step(i, carry):
            at = aligned(i * 128, 128, 128)
            x = state_ref[at, :]
            centred = x - jnp.mean(x, axis=-1, keepdims=True)
            variance = jnp.mean(centred * centred, axis=-1, keepdims=True)
            high, low = split_bf16(centred * lax.rsqrt(variance + EPS))
            gate_ref[at, :] = jax.nn.sigmoid(matmul(jnp.concatenate([high, high, low], axis=1), cat, ((1,), (0,))))
            return carry

        lax.fori_loop(0, PACK, step, 0, unroll=3)

    return body


PAD = 8


def widen(source_ref, wide_ref):
    def step(i, carry):
        wide_ref[aligned(PAD + i * 256, 256, 8), :] = source_ref[aligned(i * 256, 256, 256), :].astype(F32)
        return carry

    lax.fori_loop(0, 18, step, 0)


def unpack(wide_ref, base):
    lane = lanes((8, 128))
    sub = lax.broadcasted_iota(jnp.int32, (8, 128), 0)

    def rows(at):
        return wide_ref[pl.ds(base + at, 8), :]

    third = jnp.where(lane < 64, pltpu.roll(rows(4), 64, 1), pltpu.roll(rows(10), 96, 1))
    third = jnp.where(lane < 32, pltpu.roll(rows(-2), 32, 1), third)
    return rows(0), rows(8), jnp.where(sub < 2, rows(16), third)


def place(wide_ref, base, target_ref, start, column, clear):
    lane = lanes((8, 128))
    for n, part in enumerate(unpack(wide_ref, base)):
        if clear:
            part = jnp.where(lane < COLS, part, 0.0)
        target_ref[aligned(start + 8 * n, 8, 8), column] = part


def pack_tri(tri_ref, base, wide_ref, target):
    lane = lanes((8, 128))
    sub = lax.broadcasted_iota(jnp.int32, (8, 128), 0)

    def rows(at, shift=0):
        value = tri_ref[pl.ds(base + at, 8), :]
        return pltpu.roll(value, shift, 1) if shift else value

    tails = (
        jnp.where(sub < 6, rows(18, 96), rows(12, 64)),
        jnp.where(sub < 4, rows(20, 64), rows(14, 32)),
        rows(22, 32),
    )
    for n, tail in enumerate(tails):
        value = jnp.where(lane < COLS, rows(8 * n), tail)
        if n < 2:
            wide_ref[pl.ds(target + 8 * n, 8), :] = value
        else:
            wide_ref[pl.ds(target + 16, 2), :] = value[0:2]


def narrow(wide_ref, out_ref):
    def step(i, carry):
        at = aligned(i * 256, 256, 256)
        out_ref[at, :] = wide_ref[at, :].astype(BF16)
        return carry

    lax.fori_loop(0, 9, step, 0)


def outgoing_kernel(own_ref, other_ref, out_ref, own_wide, other_wide, left_ref, right_ref, tri_ref, mix_ref):
    core = lax.axis_index("core")
    widen(own_ref, own_wide)
    widen(other_ref, other_wide)

    def step(b, carry):
        z = b // 2
        base = z * 128 + (b - 2 * z) * 48
        for g in range(8):
            at = slice(128 * g, 128 * g + 128)
            message = PAD + (b * 8 + g) * 2 * PACK
            place(own_wide, message, left_ref, b * 24, at, False)
            place(own_wide, message + PACK, right_ref, base + core * 24, at, True)
            place(other_wide, message + PACK, right_ref, base + 24 - core * 24, at, True)
        return carry

    lax.fori_loop(0, 16, step, 0)
    for z in range(8):
        right_ref[128 * z + 96 : 128 * z + 128, :] = jnp.zeros((32, 1024), F32)
    left = left_ref[...].astype(BF16)
    for g in range(8):
        at = slice(128 * g, 128 * g + 128)
        tri_ref[g, 0:384, :] = matmul(left, right_ref[at, :].astype(BF16), ((1,), (1,)))

    def send(b, carry):
        for g in range(8):
            pack_tri(tri_ref.at[g], b * 24, mix_ref, (b * 8 + g) * PACK)
        return carry

    lax.fori_loop(0, 16, send, 0)
    narrow(mix_ref, out_ref)


def incoming_kernel(own_ref, other_ref, out_ref, own_wide, other_wide, left_ref, right_ref, tri_ref, mix_ref):
    core = lax.axis_index("core")
    widen(own_ref, own_wide)
    widen(other_ref, other_wide)

    def step(b, carry):
        for g in range(8):
            at = slice(128 * g, 128 * g + 128)
            message = PAD + (b * 8 + g) * 2 * PACK
            for start, wide_ref in ((0, own_wide), (384, other_wide)):
                place(wide_ref, message, left_ref, start + b * 24, at, False)
                place(wide_ref, message + PACK, right_ref, start + b * 24, at, False)
        return carry

    lax.fori_loop(0, 16, step, 0)
    right = right_ref[...].astype(BF16)
    for z in range(8):
        left = left_ref[:, 128 * z : 128 * z + 128].T.astype(BF16)
        tri = matmul(left, right, ((1,), (0,)))
        for g in range(8):
            tri_ref[z, g] = tri[:, 128 * g : 128 * g + 128]

    def send(b, carry):
        z = b // 2
        base = (b - 2 * z) * 48 + core * 24
        for g in range(8):
            pack_tri(tri_ref.at[z, g], base, mix_ref, (b * 8 + g) * PACK)
        return carry

    lax.fori_loop(0, 16, send, 0)
    narrow(mix_ref, out_ref)


def finish(tri_ref, state_ref, gate_ref, weight, scaled_ref, stat_ref, next_ref):
    def stats(i, carry):
        total, square = carry
        t = tri_ref[aligned(i * 144, 144, 144), :].astype(F32)
        first, second = t[0:72], t[72:144]
        return total + first + second, square + first * first + second * second

    zero = jnp.zeros((72, 128), F32)
    total, square = lax.fori_loop(0, 16, stats, (zero, zero))
    stat_ref[0, 0:72, :] = total
    stat_ref[1, 0:72, :] = square

    def gather(n):
        return sum(stat_ref[n, 18 * q : 18 * q + 18, :] for q in range(4)) * (1.0 / CH)

    average = gather(0)
    scale = lax.rsqrt(gather(1) - average * average + EPS)
    for q in range(4):
        stat_ref[0, 18 * q : 18 * q + 18, :] = average
        stat_ref[1, 18 * q : 18 * q + 18, :] = scale

    def rescale(i, carry):
        t = tri_ref[aligned(i * 144, 144, 144), :].astype(F32)
        for half in range(2):
            part = (t[72 * half : 72 * half + 72] - stat_ref[0, 0:72, :]) * stat_ref[1, 0:72, :]
            scaled_ref[aligned(i * 144 + 72 * half, 72, 72), :] = part
        return carry

    lax.fori_loop(0, 16, rescale, 0)
    w_hi, w_lo = split_bf16(weight.T)
    w_cat = jnp.concatenate([w_hi, w_lo, w_hi], axis=1)

    def combine(i, carry):
        pieces = [split_bf16(scaled_ref[pl.ds(2 * i + half, CH, stride=PACK), :]) for half in range(2)]
        high = jnp.concatenate([pieces[0][0], pieces[1][0]], axis=1)
        low = jnp.concatenate([pieces[0][1], pieces[1][1]], axis=1)
        values = matmul(w_cat, jnp.concatenate([high, high, low], axis=0), ((1,), (0,)))
        for half in range(2):
            t = 2 * i + half
            value = values[:, 128 * half : 128 * half + 128].T
            at = aligned(t * COLS, COLS, COLS)
            next_ref[at, :] = state_ref[at, :] + gate_ref[at, :] * value[:COLS]
            at = tail_pixels(t)
            next_ref[at, :] = state_ref[at, :] + gate_ref[at, :] * value[COLS:]
        return carry

    lax.fori_loop(0, PACK // 2, combine, 0, unroll=3)


def middle_kernel(edge_ref, tri_ref, state_ref, gate_ref, outw_ref, proj_ref, next_ref, send_ref,
                  norm_ref, mix_ref, scaled_ref, stat_ref):
    finish(tri_ref, state_ref, gate_ref, outw_ref[0], scaled_ref, stat_ref, next_ref)
    project(next_ref, proj_ref[1], edge_ref, norm_ref, mix_ref, send_ref)


def last_kernel(tri_ref, state_ref, gate_ref, outw_ref, next_ref, scaled_ref, stat_ref):
    finish(tri_ref, state_ref, gate_ref, outw_ref[1], scaled_ref, stat_ref, next_ref)


VM = pl.BlockSpec(memory_space=pltpu.VMEM)
SM = pl.BlockSpec(memory_space=pltpu.SMEM)
STATE = pltpu.VMEM((PIX, CH), F32)
SEND = pltpu.VMEM((CH * 2 * PACK, 128), BF16)
TRI = pltpu.VMEM((CH * PACK, 128), BF16)
EDGE = pltpu.VMEM((PACK, 128), F32)
PROJECT_SCRATCH = [pltpu.VMEM((PACK * 128, 384), BF16), pltpu.VMEM((CH * 2 * PACK, 128), F32)]
FINISH_SCRATCH = [pltpu.VMEM((CH * PACK, 128), F32), pltpu.VMEM((2, 72, 128), F32)]
WIDE = pltpu.VMEM((CH * 2 * PACK + 16, 128), F32)


PARAMS = pltpu.CompilerParams(vmem_limit_bytes=36 * 1024 * 1024)


def near(value):
    return pltpu.with_memory_space_constraint(value, pltpu.VMEM)


def exchange(message, rows):
    moved = lax.all_to_all(message.reshape(CH, rows // 2, 2, 128), CHIPS, split_axis=0, concat_axis=0, tiled=True)
    return moved.reshape(CH * rows, 128)


def triangle(kernel, message, scratch):
    own = exchange(message, 2 * PACK)
    other = lax.ppermute(own, "core", [(0, 1), (1, 0)])
    tri = pl.pallas_call(
        kernel, out_shape=TRI, compiler_params=PARAMS, in_specs=[VM, VM], out_specs=VM,
        scratch_shapes=[WIDE, WIDE] + scratch + [pltpu.VMEM((CH * PACK, 128), F32)],
    )(near(own), near(other))
    return exchange(tri, PACK)


def gating(layer, state, gate_weight):
    return pl.pallas_call(
        gate_kernel(layer), out_shape=STATE, compiler_params=PARAMS, in_specs=[VM, VM], out_specs=VM,
        cost_estimate=pl.CostEstimate(flops=3 * 2 * PIX * CH * CH, transcendentals=PIX * CH, bytes_accessed=8 * PIX * CH),
    )(near(state), near(gate_weight))


def on_device(pair, residue_mask, hotspot, interface, proj_weight, gate_weight, out_weight):
    state = pair.reshape(PIX, CH)
    send, edge = pl.pallas_call(
        first_kernel, out_shape=(SEND, EDGE), compiler_params=PARAMS, in_specs=[SM, SM, VM, VM, VM], out_specs=(VM, VM),
        scratch_shapes=[pltpu.VMEM((ROWS, 128), jnp.int32)] + PROJECT_SCRATCH,
    )(residue_mask, hotspot, interface, state, proj_weight)
    gate = gating(0, state, gate_weight)
    tri = triangle(
        outgoing_kernel, send,
        [pltpu.VMEM((384, 1024), F32), pltpu.VMEM((1024, 1024), F32), pltpu.VMEM((8, 392, 128), F32)],
    )
    state, send = pl.pallas_call(
        middle_kernel, out_shape=(STATE, SEND), compiler_params=PARAMS, in_specs=[VM] * 6, out_specs=(VM, VM),
        scratch_shapes=PROJECT_SCRATCH + FINISH_SCRATCH,
    )(near(edge), near(tri), near(state), near(gate), near(out_weight), near(proj_weight))
    gate = gating(1, state, gate_weight)
    tri = triangle(
        incoming_kernel, send,
        [pltpu.VMEM((768, 1024), F32), pltpu.VMEM((768, 1024), F32), pltpu.VMEM((8, 8, 128, 128), F32)],
    )
    state = pl.pallas_call(
        last_kernel, out_shape=jax.ShapeDtypeStruct((PIX, CH), F32), compiler_params=PARAMS, in_specs=[VM] * 4, out_specs=VM,
        scratch_shapes=FINISH_SCRATCH,
    )(near(tri), near(state), near(gate), near(out_weight))
    return state.reshape(ROWS, COLS, CH)


def solution(mesh):
    grid = Mesh(mesh.devices.reshape(8, 2, 2, 4, 2), ("z", "yl", "core", "x", "yh"))
    rows = ("z", "yl", "core")
    cols = ("x", "yh")
    return jax.shard_map(
        on_device,
        mesh=grid,
        in_specs=(P(rows, cols, None), P(), P(), P(rows, cols), P(), P(), P()),
        out_specs=P(rows, cols, None),
        check_vma=False,
    )
```

```python
import jax
import jax.numpy as jnp
from jax import lax
from jax.experimental import pallas as pl
from jax.experimental.pallas import tpu as pltpu
from jax.sharding import Mesh, PartitionSpec as P

EPS = 1e-05
F32 = jnp.float32
BF16 = jnp.bfloat16
ROWS = 24
COLS = 96
PIX = ROWS * COLS
CH = 128
PACK = 18
CHIPS = ("z", "yl", "x", "yh")


def split_bf16(value):
    high = value.astype(BF16)
    low = (value - high.astype(F32)).astype(BF16)
    return high, low


def lanes(shape):
    return lax.broadcasted_iota(jnp.int32, shape, len(shape) - 1)


def matmul(a, b, dims):
    return lax.dot_general(a, b, (dims, ((), ())), preferred_element_type=F32)


def stacked(weight, axis):
    high, low = split_bf16(weight)
    return jnp.concatenate([high, low, high], axis=axis)


def aligned(start, size, unit):
    return pl.ds(pl.multiple_of(start, unit), size)


def packed_edge(mask_sm, hot_sm, inter_ref, edge_ref, rows_ref):
    band = (lax.axis_index("z") * 2 + lax.axis_index("yl")) * 2 + lax.axis_index("core")
    hid = lax.axis_index("x") * 2 + lax.axis_index("yh")
    lane = lanes((1, 128))
    col_mask = jnp.zeros((1, 128), jnp.int32)
    col_hot = jnp.zeros((1, 128), jnp.int32)
    for c in range(COLS):
        col_mask = jnp.where(lane == c, mask_sm[hid * COLS + c], col_mask)
        col_hot = jnp.where(lane == c, hot_sm[hid * COLS + c], col_hot)
    rows_ref[...] = jnp.zeros((ROWS, 128), jnp.int32)
    rows_ref[:, 0:COLS] = inter_ref[...]
    for r in range(ROWS):
        at = slice(r, r + 1)
        flags = jnp.maximum(rows_ref[at, :], jnp.maximum(col_hot, hot_sm[band * ROWS + r]))
        rows_ref[at, :] = flags * col_mask * mask_sm[band * ROWS + r]
    for t in range(PACK):
        tail = pltpu.roll(jnp.broadcast_to(rows_ref[18 + t % 6 : 19 + t % 6, :], (8, 128)), 96 - 32 * (t // 6), 1)
        edge_ref[t : t + 1, :] = jnp.where(lane < COLS, rows_ref[t : t + 1, :], tail[0:1, :]).astype(F32)


def tail_pixels(t):
    return aligned((18 + t % 6) * COLS + 32 * (t // 6), 32, 32)


def project(state_ref, w_cat, edge_ref, norm_ref, mix_ref, send_ref):
    def normalize(t, carry):
        x = jnp.concatenate([state_ref[aligned(t * COLS, COLS, COLS), :], state_ref[tail_pixels(t), :]], axis=0)
        centred = x - jnp.mean(x, axis=-1, keepdims=True)
        variance = jnp.mean(centred * centred, axis=-1, keepdims=True)
        high, low = split_bf16(centred * lax.rsqrt(variance + EPS))
        at = aligned(t * 128, 128, 128)
        norm_ref[at, 0:128] = high
        norm_ref[at, 128:256] = high
        norm_ref[at, 256:384] = low
        return carry

    lax.fori_loop(0, PACK, normalize, 0, unroll=3)
    def pair(i, carry):
        values = matmul(w_cat, norm_ref[aligned(i * 256, 256, 256), :], ((1,), (1,)))
        for half in range(2):
            t = 2 * i + half
            part = values[:, 128 * half : 128 * half + 128]
            edge = edge_ref[pl.ds(t, 1), :]
            left = edge * jax.nn.sigmoid(part[CH : 2 * CH]) * part[:CH]
            right = edge * jax.nn.sigmoid(part[3 * CH :]) * part[2 * CH : 3 * CH]
            mix_ref[pl.ds(t, CH, stride=2 * PACK), :] = left
            mix_ref[pl.ds(t + PACK, CH, stride=2 * PACK), :] = right
        return carry

    lax.fori_loop(0, PACK // 2, pair, 0, unroll=3)

    def convert(i, carry):
        at = aligned(i * 256, 256, 256)
        send_ref[at, :] = mix_ref[at, :].astype(BF16)
        return carry

    lax.fori_loop(0, 18, convert, 0)


def first_kernel(mask_sm, hot_sm, inter_ref, state_hbm, proj_hbm, send_ref, edge_ref,
                 rows_ref, state_ref, proj_ref, sems, norm_ref, mix_ref):
    state_copy = pltpu.make_async_copy(state_hbm, state_ref, sems.at[0])
    proj_copy = pltpu.make_async_copy(proj_hbm.at[0], proj_ref, sems.at[1])
    state_copy.start()
    proj_copy.start()
    packed_edge(mask_sm, hot_sm, inter_ref, edge_ref, rows_ref)
    proj_copy.wait()
    w_cat = stacked(proj_ref[...].T, 1)
    state_copy.wait()
    project(state_ref, w_cat, edge_ref, norm_ref, mix_ref, send_ref)


def gate_kernel(layer):
    def body(state_ref, gatew_ref, outw_ref, *refs):
        if layer == 0:
            proj_ref, gate_ref, outcat_ref, projcat_ref = refs
            projcat_ref[...] = stacked(proj_ref[1].T, 1)
        else:
            gate_ref, outcat_ref = refs
        outcat_ref[...] = stacked(outw_ref[layer].T, 1)
        cat = stacked(gatew_ref[layer], 0)

        def step(i, carry):
            at = aligned(i * 128, 128, 128)
            x = state_ref[at, :]
            centred = x - jnp.mean(x, axis=-1, keepdims=True)
            variance = jnp.mean(centred * centred, axis=-1, keepdims=True)
            high, low = split_bf16(centred * lax.rsqrt(variance + EPS))
            gate_ref[at, :] = jax.nn.sigmoid(matmul(jnp.concatenate([high, high, low], axis=1), cat, ((1,), (0,))))
            return carry

        lax.fori_loop(0, PACK, step, 0, unroll=3)

    return body


PAD = 8


def widen(source_ref, wide_ref):
    def step(i, carry):
        wide_ref[aligned(PAD + i * 256, 256, 8), :] = source_ref[aligned(i * 256, 256, 256), :].astype(F32)
        return carry

    lax.fori_loop(0, 18, step, 0)


def unpack(wide_ref, base):
    lane = lanes((8, 128))
    sub = lax.broadcasted_iota(jnp.int32, (8, 128), 0)

    def rows(at):
        return wide_ref[pl.ds(base + at, 8), :]

    third = jnp.where(lane < 64, pltpu.roll(rows(4), 64, 1), pltpu.roll(rows(10), 96, 1))
    third = jnp.where(lane < 32, pltpu.roll(rows(-2), 32, 1), third)
    return rows(0), rows(8), jnp.where(sub < 2, rows(16), third)


def place(wide_ref, base, target_ref, start, column, clear):
    lane = lanes((8, 128))
    for n, part in enumerate(unpack(wide_ref, base)):
        if clear:
            part = jnp.where(lane < COLS, part, 0.0)
        target_ref[aligned(start + 8 * n, 8, 8), column] = part


def pack_tri(tri_ref, base, wide_ref, target):
    lane = lanes((8, 128))
    sub = lax.broadcasted_iota(jnp.int32, (8, 128), 0)

    def rows(at, shift=0):
        value = tri_ref[pl.ds(base + at, 8), :]
        return pltpu.roll(value, shift, 1) if shift else value

    tails = (
        jnp.where(sub < 6, rows(18, 96), rows(12, 64)),
        jnp.where(sub < 4, rows(20, 64), rows(14, 32)),
        rows(22, 32),
    )
    for n, tail in enumerate(tails):
        value = jnp.where(lane < COLS, rows(8 * n), tail)
        if n < 2:
            wide_ref[pl.ds(target + 8 * n, 8), :] = value
        else:
            wide_ref[pl.ds(target + 16, 2), :] = value[0:2]


def narrow(wide_ref, out_ref):
    def step(i, carry):
        at = aligned(i * 256, 256, 256)
        out_ref[at, :] = wide_ref[at, :].astype(BF16)
        return carry

    lax.fori_loop(0, 9, step, 0)


def outgoing_own(own_ref, left_ref, right_ref, wide_ref, keep_ref):
    core = lax.axis_index("core")
    widen(own_ref, wide_ref)

    def step(b, carry):
        start = (b // 2) * 128 + (b % 2) * 48 + core * 24
        for g in range(8):
            at = slice(128 * g, 128 * g + 128)
            message = PAD + (b * 8 + g) * 2 * PACK
            place(wide_ref, message, keep_ref, b * 24, at, False)
            place(wide_ref, message + PACK, right_ref, start, at, True)
        return carry

    lax.fori_loop(0, 16, step, 0, unroll=2)
    for z in range(8):
        right_ref[128 * z + 96 : 128 * z + 128, :] = jnp.zeros((32, 1024), F32)
    left_ref[...] = keep_ref[...].astype(BF16)


def send_tri(tri_ref, mix_ref, out_ref):
    def send(b, carry):
        for g in range(8):
            pack_tri(tri_ref.at[g], b * 24, mix_ref, (b * 8 + g) * PACK)
        return carry

    lax.fori_loop(0, 16, send, 0, unroll=2)
    narrow(mix_ref, out_ref)


def outgoing_kernel(left_ref, _, other_ref, out_ref, right_ref, wide_ref, tri_ref, mix_ref):
    core = lax.axis_index("core")
    widen(other_ref, wide_ref)

    def step(b, carry):
        start = (b // 2) * 128 + (b % 2) * 48 + 24 - core * 24
        for g in range(8):
            message = PAD + (b * 8 + g) * 2 * PACK
            place(wide_ref, message + PACK, right_ref, start, slice(128 * g, 128 * g + 128), True)
        return carry

    lax.fori_loop(0, 16, step, 0, unroll=2)
    left = left_ref[...]
    for n in range(4):
        tri = matmul(left, right_ref[256 * n : 256 * n + 256, :].astype(BF16), ((1,), (1,)))
        tri_ref[2 * n, 0:384, :] = tri[:, 0:128]
        tri_ref[2 * n + 1, 0:384, :] = tri[:, 128:256]
    send_tri(tri_ref, mix_ref, out_ref)


def incoming_half(source_ref, wide_ref, left_ref, right_ref, turn_ref, turned_ref):
    core = lax.axis_index("core")
    widen(source_ref, wide_ref)

    def step(b, carry):
        for g in range(8):
            at = slice(128 * g, 128 * g + 128)
            message = PAD + (b * 8 + g) * 2 * PACK
            place(wide_ref, message, left_ref, b * 24, at, False)
            place(wide_ref, message + PACK, right_ref, b * 24, at, False)
        return carry

    lax.fori_loop(0, 16, step, 0, unroll=2)
    for z in range(8):
        turn_ref[z % 2] = left_ref[:, 128 * z : 128 * z + 128].T
        for y in range(2):
            rows = slice(48 * z + 24 * y, 48 * z + 24 * y + 24)
            turned_ref[rows, :] = turn_ref[z % 2, aligned(48 * y + 24 * core, 24, 8), :]
    left = turned_ref[...].astype(BF16)
    for n in range(4):
        tri = matmul(left, right_ref[:, 256 * n : 256 * n + 256].astype(BF16), ((1,), (0,)))
        yield 2 * n, tri[:, 0:128]
        yield 2 * n + 1, tri[:, 128:256]


def incoming_own(own_ref, part_ref, *scratch):
    for g, tri in incoming_half(own_ref, *scratch):
        part_ref[g] = tri


def incoming_kernel(part_ref, other_ref, out_ref, wide_ref, left_ref, right_ref, turn_ref, turned_ref, tri_ref, mix_ref):
    for g, tri in incoming_half(other_ref, wide_ref, left_ref, right_ref, turn_ref, turned_ref):
        tri_ref[g, 0:384, :] = part_ref[g] + tri
    send_tri(tri_ref, mix_ref, out_ref)


def finish(tri_ref, state_ref, gate_ref, w_cat, scaled_ref, stat_ref, next_ref):
    def stats(i, carry):
        total, square = carry
        t = tri_ref[aligned(i * 144, 144, 144), :].astype(F32)
        first, second = t[0:72], t[72:144]
        return total + first + second, square + first * first + second * second

    zero = jnp.zeros((72, 128), F32)
    total, square = lax.fori_loop(0, 16, stats, (zero, zero))
    stat_ref[0, 0:72, :] = total
    stat_ref[1, 0:72, :] = square

    def gather(n):
        return sum(stat_ref[n, 18 * q : 18 * q + 18, :] for q in range(4)) * (1.0 / CH)

    average = gather(0)
    scale = lax.rsqrt(gather(1) - average * average + EPS)
    for q in range(4):
        stat_ref[0, 18 * q : 18 * q + 18, :] = average
        stat_ref[1, 18 * q : 18 * q + 18, :] = scale

    def rescale(i, carry):
        t = tri_ref[aligned(i * 144, 144, 144), :].astype(F32)
        for half in range(2):
            part = (t[72 * half : 72 * half + 72] - stat_ref[0, 0:72, :]) * stat_ref[1, 0:72, :]
            scaled_ref[aligned(i * 144 + 72 * half, 72, 72), :] = part
        return carry

    lax.fori_loop(0, 16, rescale, 0)
    def combine(i, carry):
        pieces = [split_bf16(scaled_ref[pl.ds(2 * i + half, CH, stride=PACK), :]) for half in range(2)]
        high = jnp.concatenate([pieces[0][0], pieces[1][0]], axis=1)
        low = jnp.concatenate([pieces[0][1], pieces[1][1]], axis=1)
        values = matmul(w_cat, jnp.concatenate([high, high, low], axis=0), ((1,), (0,)))
        for half in range(2):
            t = 2 * i + half
            value = values[:, 128 * half : 128 * half + 128].T
            at = aligned(t * COLS, COLS, COLS)
            next_ref[at, :] = state_ref[at, :] + gate_ref[at, :] * value[:COLS]
            at = tail_pixels(t)
            next_ref[at, :] = state_ref[at, :] + gate_ref[at, :] * value[COLS:]
        return carry

    lax.fori_loop(0, PACK // 2, combine, 0, unroll=3)


def middle_kernel(edge_ref, tri_ref, state_ref, gate_ref, outcat_ref, projcat_ref, next_ref, send_ref,
                  norm_ref, mix_ref, scaled_ref, stat_ref):
    finish(tri_ref, state_ref, gate_ref, outcat_ref[...], scaled_ref, stat_ref, next_ref)
    project(next_ref, projcat_ref[...], edge_ref, norm_ref, mix_ref, send_ref)


def last_kernel(tri_ref, state_ref, gate_ref, outcat_ref, next_ref, scaled_ref, stat_ref):
    finish(tri_ref, state_ref, gate_ref, outcat_ref[...], scaled_ref, stat_ref, next_ref)


VM = pl.BlockSpec(memory_space=pltpu.VMEM)
SM = pl.BlockSpec(memory_space=pltpu.SMEM)
HB = pl.BlockSpec(memory_space=pltpu.HBM)
STATE = pltpu.VMEM((PIX, CH), F32)
SEND = pltpu.VMEM((CH * 2 * PACK, 128), BF16)
TRI = pltpu.VMEM((CH * PACK, 128), BF16)
EDGE = pltpu.VMEM((PACK, 128), F32)
OUTCAT = pltpu.VMEM((CH, 3 * CH), BF16)
PROJCAT = pltpu.VMEM((4 * CH, 3 * CH), BF16)
PROJECT_SCRATCH = [pltpu.VMEM((PACK * 128, 384), BF16), pltpu.VMEM((CH * 2 * PACK, 128), F32)]
FINISH_SCRATCH = [pltpu.VMEM((CH * PACK, 128), F32), pltpu.VMEM((2, 72, 128), F32)]
SEND_SCRATCH = [pltpu.VMEM((8, 392, 128), F32), pltpu.VMEM((CH * PACK, 128), F32)]
WIDE = pltpu.VMEM((CH * 2 * PACK + 16, 128), F32)
HALF = pltpu.VMEM((384, 1024), F32)
RIGHT = pltpu.VMEM((1024, 1024), F32)
HALF_SCRATCH = [WIDE, HALF, HALF, pltpu.VMEM((2, 128, 384), F32), pltpu.VMEM((384, 384), F32)]
PART = pltpu.VMEM((8, 384, 128), F32)


def call(kernel, out_shape, operands, scratch=(), specs=None, mib=16, **options):
    outs = out_shape if isinstance(out_shape, tuple) else None
    return pl.pallas_call(
        kernel,
        out_shape=out_shape,
        in_specs=specs or [VM] * len(operands),
        out_specs=VM if outs is None else (VM,) * len(outs),
        scratch_shapes=list(scratch),
        compiler_params=pltpu.CompilerParams(vmem_limit_bytes=mib * 1024 * 1024),
        **options,
    )(*operands)


def near(value):
    return pltpu.with_memory_space_constraint(value, pltpu.VMEM)


def far(value):
    return pltpu.with_memory_space_constraint(value, pltpu.HBM)


def exchange(message, rows):
    moved = lax.all_to_all(message.reshape(CH, rows // 2, 2, 128), CHIPS, split_axis=0, concat_axis=0, tiled=True)
    return moved.reshape(CH * rows, 128)


def partner(value):
    return lax.ppermute(value, "core", [(0, 1), (1, 0)])


def gating(layer, outs, *operands):
    cost = pl.CostEstimate(flops=3 * 2 * PIX * CH * CH, transcendentals=PIX * CH, bytes_accessed=8 * PIX * CH)
    return call(gate_kernel(layer), outs, operands, cost_estimate=cost)


def on_device(pair, residue_mask, hotspot, interface, proj_weight, gate_weight, out_weight):
    state = pair.reshape(PIX, CH)
    send, edge = call(
        first_kernel, (SEND, EDGE),
        (residue_mask, hotspot, far(interface), far(state), far(proj_weight)),
        [pltpu.VMEM((ROWS, 128), jnp.int32), pltpu.VMEM((PIX, CH), F32), pltpu.VMEM((CH, 4 * CH), F32),
         pltpu.SemaphoreType.DMA((2,))] + PROJECT_SCRATCH,
        [SM, SM, VM, HB, HB],
    )
    own = exchange(send, 2 * PACK)
    other = partner(own)
    left, right = call(outgoing_own, (pltpu.VMEM((384, 1024), BF16), RIGHT), (near(own),), [WIDE, HALF])
    tri, _ = call(
        outgoing_kernel, (TRI, RIGHT), (near(left), near(right), near(other)), [WIDE] + SEND_SCRATCH,
        input_output_aliases={1: 1},
    )
    tri = exchange(tri, PACK)
    gate, outcat, projcat = gating(0, (STATE, OUTCAT, PROJCAT), near(state), gate_weight, out_weight, proj_weight)
    state, send = call(
        middle_kernel, (STATE, SEND),
        (near(edge), near(tri), near(state), near(gate), near(outcat), near(projcat)), PROJECT_SCRATCH + FINISH_SCRATCH,
    )
    own = exchange(send, 2 * PACK)
    other = partner(own)
    part = call(incoming_own, PART, (near(own),), HALF_SCRATCH)
    tri = call(incoming_kernel, TRI, (near(part), near(other)), HALF_SCRATCH + SEND_SCRATCH)
    tri = exchange(tri, PACK)
    gate, outcat = gating(1, (STATE, OUTCAT), near(state), gate_weight, out_weight)
    state = call(
        last_kernel, jax.ShapeDtypeStruct((PIX, CH), F32), (near(tri), near(state), near(gate), near(outcat)),
        FINISH_SCRATCH,
    )
    return state.reshape(ROWS, COLS, CH)


def solution(mesh):
    grid = Mesh(mesh.devices.reshape(8, 2, 2, 4, 2), ("z", "yl", "core", "x", "yh"))
    rows = ("z", "yl", "core")
    cols = ("x", "yh")
    return jax.shard_map(
        on_device,
        mesh=grid,
        in_specs=(P(rows, cols, None), P(), P(), P(rows, cols), P(), P(), P()),
        out_specs=P(rows, cols, None),
        check_vma=False,
    )
```

```python
import jax
import jax.numpy as jnp
from jax import lax
from jax.experimental import pallas as pl
from jax.experimental.pallas import tpu as pltpu
from jax.sharding import Mesh, PartitionSpec as P

EPS = 1e-05
F32 = jnp.float32
BF16 = jnp.bfloat16
ROWS = 24
COLS = 96
PIX = ROWS * COLS
CH = 128
PACK = 18
CHIPS = ("z", "yl", "x", "yh")


def split_bf16(value):
    high = value.astype(BF16)
    low = (value - high.astype(F32)).astype(BF16)
    return high, low


def lanes(shape):
    return lax.broadcasted_iota(jnp.int32, shape, len(shape) - 1)


def matmul(a, b, dims):
    return lax.dot_general(a, b, (dims, ((), ())), preferred_element_type=F32)


def stacked(weight, axis):
    high, low = split_bf16(weight)
    return jnp.concatenate([high, low, high], axis=axis)


def aligned(start, size, unit):
    return pl.ds(pl.multiple_of(start, unit), size)


def packed_edge(mask_sm, hot_sm, inter_ref, edge_ref, rows_ref):
    band = (lax.axis_index("z") * 2 + lax.axis_index("yl")) * 2 + lax.axis_index("core")
    hid = lax.axis_index("x") * 2 + lax.axis_index("yh")
    lane = lanes((1, 128))
    col_mask = jnp.zeros((1, 128), jnp.int32)
    col_hot = jnp.zeros((1, 128), jnp.int32)
    for c in range(COLS):
        col_mask = jnp.where(lane == c, mask_sm[hid * COLS + c], col_mask)
        col_hot = jnp.where(lane == c, hot_sm[hid * COLS + c], col_hot)
    rows_ref[...] = jnp.zeros((ROWS, 128), jnp.int32)
    rows_ref[:, 0:COLS] = inter_ref[...]
    for r in range(ROWS):
        at = slice(r, r + 1)
        flags = jnp.maximum(rows_ref[at, :], jnp.maximum(col_hot, hot_sm[band * ROWS + r]))
        rows_ref[at, :] = flags * col_mask * mask_sm[band * ROWS + r]
    for t in range(PACK):
        tail = pltpu.roll(jnp.broadcast_to(rows_ref[18 + t % 6 : 19 + t % 6, :], (8, 128)), 96 - 32 * (t // 6), 1)
        edge_ref[t : t + 1, :] = jnp.where(lane < COLS, rows_ref[t : t + 1, :], tail[0:1, :]).astype(F32)


def tail_pixels(t):
    return aligned((18 + t % 6) * COLS + 32 * (t // 6), 32, 32)


def project(state_ref, w_cat, edge_ref, norm_ref, mix_ref, send_ref):
    def normalize(t, carry):
        x = jnp.concatenate([state_ref[aligned(t * COLS, COLS, COLS), :], state_ref[tail_pixels(t), :]], axis=0)
        centred = x - jnp.mean(x, axis=-1, keepdims=True)
        variance = jnp.mean(centred * centred, axis=-1, keepdims=True)
        high, low = split_bf16(centred * lax.rsqrt(variance + EPS))
        at = aligned(t * 128, 128, 128)
        norm_ref[at, 0:128] = high
        norm_ref[at, 128:256] = high
        norm_ref[at, 256:384] = low
        return carry

    lax.fori_loop(0, PACK, normalize, 0, unroll=3)
    def pair(i, carry):
        values = matmul(w_cat, norm_ref[aligned(i * 256, 256, 256), :], ((1,), (1,)))
        for half in range(2):
            t = 2 * i + half
            part = values[:, 128 * half : 128 * half + 128]
            edge = edge_ref[pl.ds(t, 1), :]
            left = edge * jax.nn.sigmoid(part[CH : 2 * CH]) * part[:CH]
            right = edge * jax.nn.sigmoid(part[3 * CH :]) * part[2 * CH : 3 * CH]
            mix_ref[pl.ds(t, CH, stride=2 * PACK), :] = left
            mix_ref[pl.ds(t + PACK, CH, stride=2 * PACK), :] = right
        return carry

    lax.fori_loop(0, PACK // 2, pair, 0, unroll=3)

    def convert(i, carry):
        at = aligned(i * 256, 256, 256)
        send_ref[at, :] = mix_ref[at, :].astype(BF16)
        return carry

    lax.fori_loop(0, 18, convert, 0)


def first_kernel(mask_hbm, hot_hbm, inter_hbm, state_hbm, proj_hbm, send_ref, edge_ref, mask_sm, hot_sm,
                 inter_ref, rows_ref, state_ref, proj_ref, sems, norm_ref, mix_ref):
    copies = [
        pltpu.make_async_copy(source, target, sems.at[n])
        for n, (source, target) in enumerate((
            (mask_hbm, mask_sm), (hot_hbm, hot_sm), (inter_hbm, inter_ref), (proj_hbm.at[0], proj_ref),
            (state_hbm, state_ref),
        ))
    ]
    for copy in copies:
        copy.start()
    for copy in copies[:3]:
        copy.wait()
    packed_edge(mask_sm, hot_sm, inter_ref, edge_ref, rows_ref)
    copies[3].wait()
    w_cat = stacked(proj_ref[...].T, 1)
    copies[4].wait()
    project(state_ref, w_cat, edge_ref, norm_ref, mix_ref, send_ref)


def gate_kernel(layer):
    def body(state_ref, gatew_ref, outw_ref, *refs):
        if layer == 0:
            proj_ref, gate_ref, outcat_ref, projcat_ref = refs
            projcat_ref[...] = stacked(proj_ref[1].T, 1)
        else:
            gate_ref, outcat_ref = refs
        outcat_ref[...] = stacked(outw_ref[layer].T, 1)
        cat = stacked(gatew_ref[layer], 0)

        def step(i, carry):
            at = aligned(i * 128, 128, 128)
            x = state_ref[at, :]
            centred = x - jnp.mean(x, axis=-1, keepdims=True)
            variance = jnp.mean(centred * centred, axis=-1, keepdims=True)
            high, low = split_bf16(centred * lax.rsqrt(variance + EPS))
            gate_ref[at, :] = jax.nn.sigmoid(matmul(jnp.concatenate([high, high, low], axis=1), cat, ((1,), (0,))))
            return carry

        lax.fori_loop(0, PACK, step, 0, unroll=3)

    return body


PAD = 8


def widen(source_ref, wide_ref):
    def step(i, carry):
        wide_ref[aligned(PAD + i * 256, 256, 8), :] = source_ref[aligned(i * 256, 256, 256), :].astype(F32)
        return carry

    lax.fori_loop(0, 18, step, 0)


def unpack(wide_ref, base):
    lane = lanes((8, 128))
    sub = lax.broadcasted_iota(jnp.int32, (8, 128), 0)

    def rows(at):
        return wide_ref[pl.ds(base + at, 8), :]

    third = jnp.where(lane < 64, pltpu.roll(rows(4), 64, 1), pltpu.roll(rows(10), 96, 1))
    third = jnp.where(lane < 32, pltpu.roll(rows(-2), 32, 1), third)
    return rows(0), rows(8), jnp.where(sub < 2, rows(16), third)


def place(wide_ref, base, target_ref, start, column, clear):
    lane = lanes((8, 128))
    for n, part in enumerate(unpack(wide_ref, base)):
        if clear:
            part = jnp.where(lane < COLS, part, 0.0)
        target_ref[aligned(start + 8 * n, 8, 8), column] = part


def tail_slot(half, g):
    return 8 + (half * 8 + g) * 24


def send_tri(tri_ref, mix_ref, tail_ref, ready_ref, out_hbm, sems):
    lane = lanes((8, 128))

    def send(i, carry):
        blocks = [(half, g, (2 * i + half) * 24) for half in range(2) for g in range(8)]
        for half, g, base in blocks:
            slot = tail_slot(half, g)
            value = tri_ref[g, aligned(base + 16, 8, 8), :]
            tail_ref[slot + 10 : slot + 18, :] = pltpu.roll(value, 32, 1)
            tail_ref[slot + 4 : slot + 12, :] = pltpu.roll(value, 64, 1)
            tail_ref[slot - 2 : slot + 6, :] = pltpu.roll(value, 96, 1)
        for half, g, base in blocks:
            slot = tail_slot(half, g)
            target = ((2 * i + half) * 8 + g) * PACK
            for n in range(3):
                tail = tail_ref[slot + 8 * n : slot + 8 * n + 8, :]
                value = jnp.where(lane < COLS, tri_ref[g, aligned(base + 8 * n, 8, 8), :], tail)
                if n < 2:
                    mix_ref[pl.ds(target + 8 * n, 8), :] = value
                else:
                    mix_ref[pl.ds(target + 16, 2), :] = value[0:2]
        at = aligned(i * 288, 288, 288)
        ready_ref[at, :] = mix_ref[at, :].astype(BF16)
        return carry

    copies = []
    for n in range(4):
        lax.fori_loop(2 * n, 2 * n + 2, send, 0)
        at = pl.ds(576 * n, 576)
        copies.append(pltpu.make_async_copy(ready_ref.at[at], out_hbm.at[at], sems.at[n]))
        copies[-1].start()
    for copy in copies:
        copy.wait()


def outgoing_own(own_ref, left_ref, right_ref, wide_ref, keep_ref):
    core = lax.axis_index("core")
    widen(own_ref, wide_ref)

    def step(b, carry):
        start = (b // 2) * 128 + (b % 2) * 48 + core * 24
        for g in range(8):
            at = slice(128 * g, 128 * g + 128)
            message = PAD + (b * 8 + g) * 2 * PACK
            place(wide_ref, message, keep_ref, b * 24, at, False)
            place(wide_ref, message + PACK, right_ref, start, at, True)
        return carry

    lax.fori_loop(0, 16, step, 0, unroll=2)
    for z in range(8):
        right_ref[128 * z + 96 : 128 * z + 128, :] = jnp.zeros((32, 1024), F32)
    left_ref[...] = keep_ref[...].astype(BF16)


def outgoing_kernel(left_ref, _, other_ref, out_hbm, right_ref, wide_ref, tri_ref, *scratch):
    core = lax.axis_index("core")
    widen(other_ref, wide_ref)

    def step(b, carry):
        start = (b // 2) * 128 + (b % 2) * 48 + 24 - core * 24
        for g in range(8):
            message = PAD + (b * 8 + g) * 2 * PACK
            place(wide_ref, message + PACK, right_ref, start, slice(128 * g, 128 * g + 128), True)
        return carry

    lax.fori_loop(0, 16, step, 0, unroll=2)
    left = left_ref[...]
    for n in range(4):
        tri = matmul(left, right_ref[256 * n : 256 * n + 256, :].astype(BF16), ((1,), (1,)))
        tri_ref[2 * n, 0:384, :] = tri[:, 0:128]
        tri_ref[2 * n + 1, 0:384, :] = tri[:, 128:256]
    mix_ref, tail_ref, ready_ref, sems = scratch
    send_tri(tri_ref, mix_ref, tail_ref, ready_ref, out_hbm, sems)


def incoming_half(source_ref, wide_ref, left_ref, right_ref, turn_ref, turned_ref):
    core = lax.axis_index("core")
    widen(source_ref, wide_ref)

    def step(b, carry):
        for g in range(8):
            at = slice(128 * g, 128 * g + 128)
            message = PAD + (b * 8 + g) * 2 * PACK
            place(wide_ref, message, left_ref, b * 24, at, False)
            place(wide_ref, message + PACK, right_ref, b * 24, at, False)
        return carry

    lax.fori_loop(0, 16, step, 0, unroll=2)
    for z in range(8):
        turn_ref[z % 2] = left_ref[:, 128 * z : 128 * z + 128].T
        for y in range(2):
            rows = slice(48 * z + 24 * y, 48 * z + 24 * y + 24)
            turned_ref[rows, :] = turn_ref[z % 2, aligned(48 * y + 24 * core, 24, 8), :]
    left = turned_ref[...].astype(BF16)
    for n in range(4):
        tri = matmul(left, right_ref[:, 256 * n : 256 * n + 256].astype(BF16), ((1,), (0,)))
        yield 2 * n, tri[:, 0:128]
        yield 2 * n + 1, tri[:, 128:256]


def incoming_own(own_ref, part_ref, *scratch):
    for g, tri in incoming_half(own_ref, *scratch):
        part_ref[g] = tri


def incoming_kernel(part_ref, other_ref, out_hbm, wide_ref, left_ref, right_ref, turn_ref, turned_ref, tri_ref,
                    mix_ref, tail_ref, ready_ref, sems):
    for g, tri in incoming_half(other_ref, wide_ref, left_ref, right_ref, turn_ref, turned_ref):
        tri_ref[g, 0:384, :] = part_ref[g] + tri
    send_tri(tri_ref, mix_ref, tail_ref, ready_ref, out_hbm, sems)


def finish(tri_ref, state_ref, gate_hbm, outcat_hbm, next_ref, scaled_ref, stat_ref, gate_ref, outcat_ref, fetch_sems,
           done=None):
    fetches = [
        pltpu.make_async_copy(outcat_hbm, outcat_ref, fetch_sems.at[0]),
        pltpu.make_async_copy(gate_hbm, gate_ref, fetch_sems.at[1]),
    ]
    for fetch in fetches:
        fetch.start()

    def stats(i, carry):
        total, square = carry
        t = tri_ref[aligned(i * 144, 144, 144), :].astype(F32)
        first, second = t[0:72], t[72:144]
        return total + first + second, square + first * first + second * second

    zero = jnp.zeros((72, 128), F32)
    total, square = lax.fori_loop(0, 16, stats, (zero, zero))
    stat_ref[0, 0:72, :] = total
    stat_ref[1, 0:72, :] = square

    def gather(n):
        return sum(stat_ref[n, 18 * q : 18 * q + 18, :] for q in range(4)) * (1.0 / CH)

    average = gather(0)
    scale = lax.rsqrt(gather(1) - average * average + EPS)
    for q in range(4):
        stat_ref[0, 18 * q : 18 * q + 18, :] = average
        stat_ref[1, 18 * q : 18 * q + 18, :] = scale

    def rescale(i, carry):
        t = tri_ref[aligned(i * 144, 144, 144), :].astype(F32)
        for half in range(2):
            part = (t[72 * half : 72 * half + 72] - stat_ref[0, 0:72, :]) * stat_ref[1, 0:72, :]
            scaled_ref[aligned(i * 144 + 72 * half, 72, 72), :] = part
        return carry

    lax.fori_loop(0, 16, rescale, 0)
    for fetch in fetches:
        fetch.wait()
    w_cat = outcat_ref[...]

    def combine(i, carry):
        pieces = [split_bf16(scaled_ref[pl.ds(2 * i + half, CH, stride=PACK), :]) for half in range(2)]
        high = jnp.concatenate([pieces[0][0], pieces[1][0]], axis=1)
        low = jnp.concatenate([pieces[0][1], pieces[1][1]], axis=1)
        values = matmul(w_cat, jnp.concatenate([high, high, low], axis=0), ((1,), (0,)))
        for half in range(2):
            t = 2 * i + half
            value = values[:, 128 * half : 128 * half + 128].T
            at = aligned(t * COLS, COLS, COLS)
            next_ref[at, :] = state_ref[at, :] + gate_ref[at, :] * value[:COLS]
            at = tail_pixels(t)
            next_ref[at, :] = state_ref[at, :] + gate_ref[at, :] * value[COLS:]
        return carry

    if done is None:
        lax.fori_loop(0, PACK // 2, combine, 0, unroll=3)
    else:
        for n in range(3):
            for i in range(3):
                combine(3 * n + i, 0)
            done(n)
        done(3)


def middle_kernel(edge_ref, tri_ref, state_ref, gate_hbm, outcat_hbm, projcat_hbm, next_ref, send_ref,
                  projcat_ref, sems, norm_ref, mix_ref, *scratch):
    fetch = pltpu.make_async_copy(projcat_hbm, projcat_ref, sems.at[0])
    fetch.start()
    finish(tri_ref, state_ref, gate_hbm, outcat_hbm, next_ref, *scratch)
    fetch.wait()
    project(next_ref, projcat_ref[...], edge_ref, norm_ref, mix_ref, send_ref)


def last_kernel(tri_ref, state_ref, gate_hbm, outcat_hbm, out_hbm, next_ref, sems, *scratch):
    copies = []

    def done(n):
        at = pl.ds(n * PIX // 4, PIX // 4)
        copies.append(pltpu.make_async_copy(next_ref.at[at], out_hbm.at[at], sems.at[n]))
        copies[-1].start()

    finish(tri_ref, state_ref, gate_hbm, outcat_hbm, next_ref, *scratch, done=done)
    for copy in copies:
        copy.wait()


VM = pl.BlockSpec(memory_space=pltpu.VMEM)
SM = pl.BlockSpec(memory_space=pltpu.SMEM)
HB = pl.BlockSpec(memory_space=pltpu.HBM)
STATE = pltpu.VMEM((PIX, CH), F32)
SEND = pltpu.VMEM((CH * 2 * PACK, 128), BF16)
TRI = pltpu.HBM((CH * PACK, 128), BF16)
GATE = pltpu.HBM((PIX, CH), F32)
EDGE = pltpu.VMEM((PACK, 128), F32)
OUTCAT = pltpu.HBM((CH, 3 * CH), BF16)
PROJCAT = pltpu.HBM((4 * CH, 3 * CH), BF16)
PROJECT_SCRATCH = [pltpu.VMEM((PACK * 128, 384), BF16), pltpu.VMEM((CH * 2 * PACK, 128), F32)]
FINISH_SCRATCH = [
    pltpu.VMEM((CH * PACK, 128), F32), pltpu.VMEM((2, 72, 128), F32), pltpu.VMEM((PIX, CH), F32),
    pltpu.VMEM((CH, 3 * CH), BF16), pltpu.SemaphoreType.DMA((2,)),
]
SEND_SCRATCH = [
    pltpu.VMEM((8, 384, 128), F32), pltpu.VMEM((CH * PACK, 128), F32), pltpu.VMEM((400, 128), F32),
    pltpu.VMEM((CH * PACK, 128), BF16), pltpu.SemaphoreType.DMA((4,)),
]
WIDE = pltpu.VMEM((CH * 2 * PACK + 16, 128), F32)
HALF = pltpu.VMEM((384, 1024), F32)
RIGHT = pltpu.VMEM((1024, 1024), F32)
HALF_SCRATCH = [WIDE, HALF, HALF, pltpu.VMEM((2, 128, 384), F32), pltpu.VMEM((384, 384), F32)]
PART = pltpu.VMEM((8, 384, 128), F32)


def call(kernel, out_shape, operands, scratch=(), specs=None, out_specs=None, mib=16, **options):
    outs = out_shape if isinstance(out_shape, tuple) else None
    return pl.pallas_call(
        kernel,
        out_shape=out_shape,
        in_specs=specs or [VM] * len(operands),
        out_specs=out_specs or (VM if outs is None else (VM,) * len(outs)),
        scratch_shapes=list(scratch),
        compiler_params=pltpu.CompilerParams(vmem_limit_bytes=mib * 1024 * 1024),
        **options,
    )(*operands)


def near(value):
    return pltpu.with_memory_space_constraint(value, pltpu.VMEM)


def far(value):
    return pltpu.with_memory_space_constraint(value, pltpu.HBM)


def exchange(message, rows):
    moved = lax.all_to_all(message.reshape(CH, rows // 2, 2, 128), CHIPS, split_axis=0, concat_axis=0, tiled=True)
    return moved.reshape(CH * rows, 128)


def partner(value):
    return lax.ppermute(value, "core", [(0, 1), (1, 0)])


def gating(layer, outs, *operands):
    cost = pl.CostEstimate(flops=3 * 2 * PIX * CH * CH, transcendentals=PIX * CH, bytes_accessed=8 * PIX * CH)
    return call(gate_kernel(layer), outs, operands, cost_estimate=cost)


def on_device(pair, residue_mask, hotspot, interface, proj_weight, gate_weight, out_weight):
    state = pair.reshape(PIX, CH)
    send, edge = call(
        first_kernel, (SEND, EDGE),
        (far(residue_mask), far(hotspot), far(interface), far(state), far(proj_weight)),
        [pltpu.SMEM((768,), jnp.int32), pltpu.SMEM((768,), jnp.int32), pltpu.VMEM((ROWS, COLS), jnp.int32),
         pltpu.VMEM((ROWS, 128), jnp.int32), pltpu.VMEM((PIX, CH), F32), pltpu.VMEM((CH, 4 * CH), F32),
         pltpu.SemaphoreType.DMA((5,))] + PROJECT_SCRATCH,
        [HB] * 5,
    )
    own = exchange(send, 2 * PACK)
    other = partner(own)
    left, right = call(outgoing_own, (pltpu.VMEM((384, 1024), BF16), RIGHT), (near(own),), [WIDE, HALF])
    tri, _ = call(
        outgoing_kernel, (TRI, RIGHT), (near(left), near(right), near(other)), [WIDE] + SEND_SCRATCH,
        out_specs=(HB, VM), input_output_aliases={1: 1},
    )
    tri = exchange(tri, PACK)
    gate, outcat, projcat = gating(0, (GATE, OUTCAT, PROJCAT), near(state), gate_weight, out_weight, proj_weight)
    state, send = call(
        middle_kernel, (STATE, SEND),
        (near(edge), near(tri), near(state), far(gate), far(outcat), far(projcat)),
        [pltpu.VMEM((4 * CH, 3 * CH), BF16), pltpu.SemaphoreType.DMA((1,))] + PROJECT_SCRATCH + FINISH_SCRATCH,
        [VM, VM, VM, HB, HB, HB],
    )
    own = exchange(send, 2 * PACK)
    other = partner(own)
    part = call(incoming_own, PART, (near(own),), HALF_SCRATCH)
    tri = call(incoming_kernel, TRI, (near(part), near(other)), HALF_SCRATCH + SEND_SCRATCH, out_specs=HB)
    tri = exchange(tri, PACK)
    gate, outcat = gating(1, (GATE, OUTCAT), near(state), gate_weight, out_weight)
    state = call(
        last_kernel, jax.ShapeDtypeStruct((PIX, CH), F32), (near(tri), near(state), far(gate), far(outcat)),
        [pltpu.VMEM((PIX, CH), F32), pltpu.SemaphoreType.DMA((4,))] + FINISH_SCRATCH, [VM, VM, HB, HB], out_specs=HB,
    )
    return state.reshape(ROWS, COLS, CH)


def solution(mesh):
    grid = Mesh(mesh.devices.reshape(8, 2, 2, 4, 2), ("z", "yl", "core", "x", "yh"))
    rows = ("z", "yl", "core")
    cols = ("x", "yh")
    return jax.shard_map(
        on_device,
        mesh=grid,
        in_specs=(P(rows, cols, None), P(), P(), P(rows, cols), P(), P(), P()),
        out_specs=P(rows, cols, None),
        check_vma=False,
    )
```

```python
import jax
import jax.numpy as jnp
from jax import lax
from jax.experimental import pallas as pl
from jax.experimental.pallas import tpu as pltpu
from jax.sharding import Mesh, PartitionSpec as P

EPS = 1e-05
F32 = jnp.float32
BF16 = jnp.bfloat16
ROWS = 24
COLS = 96
PIX = ROWS * COLS
CH = 128
PACK = 18
CHIPS = ("z", "yl", "x", "yh")


def split_bf16(value):
    high = value.astype(BF16)
    low = (value - high.astype(F32)).astype(BF16)
    return high, low


def lanes(shape):
    return lax.broadcasted_iota(jnp.int32, shape, len(shape) - 1)


def matmul(a, b, dims):
    return lax.dot_general(a, b, (dims, ((), ())), preferred_element_type=F32)


def stacked(weight, axis):
    high, low = split_bf16(weight)
    return jnp.concatenate([high, low, high], axis=axis)


def aligned(start, size, unit):
    return pl.ds(pl.multiple_of(start, unit), size)


def packed_edge(mask_sm, hot_sm, inter_ref, edge_ref, rows_ref):
    band = (lax.axis_index("z") * 2 + lax.axis_index("yl")) * 2 + lax.axis_index("core")
    hid = lax.axis_index("x") * 2 + lax.axis_index("yh")
    lane = lanes((1, 128))
    col_mask = jnp.zeros((1, 128), jnp.int32)
    col_hot = jnp.zeros((1, 128), jnp.int32)
    for c in range(COLS):
        col_mask = jnp.where(lane == c, mask_sm[hid * COLS + c], col_mask)
        col_hot = jnp.where(lane == c, hot_sm[hid * COLS + c], col_hot)
    rows_ref[...] = jnp.zeros((ROWS, 128), jnp.int32)
    rows_ref[:, 0:COLS] = inter_ref[...]
    for r in range(ROWS):
        at = slice(r, r + 1)
        flags = jnp.maximum(rows_ref[at, :], jnp.maximum(col_hot, hot_sm[band * ROWS + r]))
        rows_ref[at, :] = flags * col_mask * mask_sm[band * ROWS + r]
    for t in range(PACK):
        tail = pltpu.roll(jnp.broadcast_to(rows_ref[18 + t % 6 : 19 + t % 6, :], (8, 128)), 96 - 32 * (t // 6), 1)
        edge_ref[t : t + 1, :] = jnp.where(lane < COLS, rows_ref[t : t + 1, :], tail[0:1, :]).astype(F32)


def tail_pixels(t):
    return aligned((18 + t % 6) * COLS + 32 * (t // 6), 32, 32)


def normalized(x):
    centred = x - jnp.mean(x, axis=0, keepdims=True)
    variance = jnp.mean(centred * centred, axis=0, keepdims=True)
    high, low = split_bf16(centred * lax.rsqrt(variance + EPS))
    return jnp.concatenate([high, high, low], axis=0)


def project(state_ref, w_cat, edge_ref, norm_ref, mix_ref, send_ref, normalize=None):
    def prepare(i, carry):
        for half in range(2):
            norm_ref[i, :, 128 * half : 128 * half + 128] = normalized(state_ref[2 * i + half])
        return carry

    lax.fori_loop(0, PACK // 2, normalize or prepare, 0, unroll=3)

    def pair(i, carry):
        values = matmul(w_cat, norm_ref[i], ((1,), (0,)))
        for half in range(2):
            t = 2 * i + half
            part = values[:, 128 * half : 128 * half + 128]
            edge = edge_ref[pl.ds(t, 1), :]
            left = edge * jax.nn.sigmoid(part[CH : 2 * CH]) * part[:CH]
            right = edge * jax.nn.sigmoid(part[3 * CH :]) * part[2 * CH : 3 * CH]
            mix_ref[pl.ds(t, CH, stride=2 * PACK), :] = left
            mix_ref[pl.ds(t + PACK, CH, stride=2 * PACK), :] = right
        return carry

    lax.fori_loop(0, PACK // 2, pair, 0, unroll=3)

    def convert(i, carry):
        at = aligned(i * 256, 256, 256)
        send_ref[at, :] = mix_ref[at, :].astype(BF16)
        return carry

    lax.fori_loop(0, 18, convert, 0)


def first_kernel(mask_hbm, hot_hbm, inter_hbm, pair_hbm, proj_hbm, send_ref, edge_ref, state_ref, mask_sm, hot_sm,
                 inter_ref, rows_ref, pair_ref, proj_ref, sems, norm_ref, mix_ref):
    copies = [
        pltpu.make_async_copy(source, target, sems.at[n])
        for n, (source, target) in enumerate((
            (mask_hbm, mask_sm), (hot_hbm, hot_sm), (inter_hbm, inter_ref), (proj_hbm.at[0], proj_ref),
            (pair_hbm, pair_ref),
        ))
    ]
    for copy in copies:
        copy.start()
    for copy in copies[:3]:
        copy.wait()
    packed_edge(mask_sm, hot_sm, inter_ref, edge_ref, rows_ref)
    copies[3].wait()
    w_cat = stacked(proj_ref[...].T, 1)
    copies[4].wait()

    def prepare(i, carry):
        for half in range(2):
            t = 2 * i + half
            x = jnp.concatenate([pair_ref[aligned(t * COLS, COLS, COLS), :], pair_ref[tail_pixels(t), :]], axis=0).T
            state_ref[t] = x
            norm_ref[i, :, 128 * half : 128 * half + 128] = normalized(x)
        return carry

    project(state_ref, w_cat, edge_ref, norm_ref, mix_ref, send_ref, prepare)


def gate_kernel(layer):
    def body(state_ref, gatew_ref, outw_ref, *refs):
        if layer == 0:
            proj_ref, gate_ref, outcat_ref, projcat_ref = refs
            projcat_ref[...] = stacked(proj_ref[1].T, 1)
        else:
            gate_ref, outcat_ref = refs
        outcat_ref[...] = stacked(outw_ref[layer].T, 1)
        cat = stacked(gatew_ref[layer].T, 1)

        def step(t, carry):
            gate_ref[t] = jax.nn.sigmoid(matmul(cat, normalized(state_ref[t]), ((1,), (0,))))
            return carry

        lax.fori_loop(0, PACK, step, 0, unroll=3)

    return body


PAD = 8


def widen(source_ref, wide_ref):
    def step(i, carry):
        wide_ref[aligned(PAD + i * 256, 256, 8), :] = source_ref[aligned(i * 256, 256, 256), :].astype(F32)
        return carry

    lax.fori_loop(0, 18, step, 0)


def unpack(wide_ref, base):
    lane = lanes((8, 128))
    sub = lax.broadcasted_iota(jnp.int32, (8, 128), 0)

    def rows(at):
        return wide_ref[pl.ds(base + at, 8), :]

    third = jnp.where(lane < 64, pltpu.roll(rows(4), 64, 1), pltpu.roll(rows(10), 96, 1))
    third = jnp.where(lane < 32, pltpu.roll(rows(-2), 32, 1), third)
    return rows(0), rows(8), jnp.where(sub < 2, rows(16), third)


def place(wide_ref, base, target_ref, start, column, clear):
    lane = lanes((8, 128))
    for n, part in enumerate(unpack(wide_ref, base)):
        if clear:
            part = jnp.where(lane < COLS, part, 0.0)
        target_ref[aligned(start + 8 * n, 8, 8), column] = part


def tail_slot(half, g):
    return 8 + (half * 8 + g) * 24


def send_tri(tri_ref, mix_ref, tail_ref, ready_ref, out_hbm, sems):
    lane = lanes((8, 128))

    def send(i, carry):
        blocks = [(half, g, (2 * i + half) * 24) for half in range(2) for g in range(8)]
        for half, g, base in blocks:
            slot = tail_slot(half, g)
            value = tri_ref[g, aligned(base + 16, 8, 8), :]
            tail_ref[slot + 10 : slot + 18, :] = pltpu.roll(value, 32, 1)
            tail_ref[slot + 4 : slot + 12, :] = pltpu.roll(value, 64, 1)
            tail_ref[slot - 2 : slot + 6, :] = pltpu.roll(value, 96, 1)
        for half, g, base in blocks:
            slot = tail_slot(half, g)
            target = ((2 * i + half) * 8 + g) * PACK
            for n in range(3):
                tail = tail_ref[slot + 8 * n : slot + 8 * n + 8, :]
                value = jnp.where(lane < COLS, tri_ref[g, aligned(base + 8 * n, 8, 8), :], tail)
                if n < 2:
                    mix_ref[pl.ds(target + 8 * n, 8), :] = value
                else:
                    mix_ref[pl.ds(target + 16, 2), :] = value[0:2]
        at = aligned(i * 288, 288, 288)
        ready_ref[at, :] = mix_ref[at, :].astype(BF16)
        return carry

    copies = []
    for n in range(4):
        lax.fori_loop(2 * n, 2 * n + 2, send, 0)
        at = pl.ds(576 * n, 576)
        copies.append(pltpu.make_async_copy(ready_ref.at[at], out_hbm.at[at], sems.at[n]))
        copies[-1].start()
    for copy in copies:
        copy.wait()


def outgoing_own(own_ref, left_ref, right_ref, wide_ref, keep_ref):
    core = lax.axis_index("core")
    widen(own_ref, wide_ref)

    def step(b, carry):
        start = (b // 2) * 128 + (b % 2) * 48 + core * 24
        for g in range(8):
            at = slice(128 * g, 128 * g + 128)
            message = PAD + (b * 8 + g) * 2 * PACK
            place(wide_ref, message, keep_ref, b * 24, at, False)
            place(wide_ref, message + PACK, right_ref, start, at, True)
        return carry

    lax.fori_loop(0, 16, step, 0, unroll=2)
    for z in range(8):
        right_ref[128 * z + 96 : 128 * z + 128, :] = jnp.zeros((32, 1024), F32)
    left_ref[...] = keep_ref[...].astype(BF16)


def outgoing_kernel(left_ref, _, other_ref, out_hbm, right_ref, wide_ref, tri_ref, *scratch):
    core = lax.axis_index("core")
    widen(other_ref, wide_ref)

    def step(b, carry):
        start = (b // 2) * 128 + (b % 2) * 48 + 24 - core * 24
        for g in range(8):
            message = PAD + (b * 8 + g) * 2 * PACK
            place(wide_ref, message + PACK, right_ref, start, slice(128 * g, 128 * g + 128), True)
        return carry

    lax.fori_loop(0, 16, step, 0, unroll=2)
    left = left_ref[...]
    for n in range(4):
        tri = matmul(left, right_ref[256 * n : 256 * n + 256, :].astype(BF16), ((1,), (1,)))
        tri_ref[2 * n, 0:384, :] = tri[:, 0:128]
        tri_ref[2 * n + 1, 0:384, :] = tri[:, 128:256]
    mix_ref, tail_ref, ready_ref, sems = scratch
    send_tri(tri_ref, mix_ref, tail_ref, ready_ref, out_hbm, sems)


def incoming_half(source_ref, wide_ref, left_ref, right_ref, turn_ref, turned_ref):
    core = lax.axis_index("core")
    widen(source_ref, wide_ref)

    def step(b, carry):
        for g in range(8):
            at = slice(128 * g, 128 * g + 128)
            message = PAD + (b * 8 + g) * 2 * PACK
            place(wide_ref, message, left_ref, b * 24, at, False)
            place(wide_ref, message + PACK, right_ref, b * 24, at, False)
        return carry

    lax.fori_loop(0, 16, step, 0, unroll=2)
    for z in range(8):
        turn_ref[z % 2] = left_ref[:, 128 * z : 128 * z + 128].T
        for y in range(2):
            rows = slice(48 * z + 24 * y, 48 * z + 24 * y + 24)
            turned_ref[rows, :] = turn_ref[z % 2, aligned(48 * y + 24 * core, 24, 8), :]
    left = turned_ref[...].astype(BF16)
    for n in range(4):
        tri = matmul(left, right_ref[:, 256 * n : 256 * n + 256].astype(BF16), ((1,), (0,)))
        yield 2 * n, tri[:, 0:128]
        yield 2 * n + 1, tri[:, 128:256]


def incoming_own(own_ref, part_ref, *scratch):
    for g, tri in incoming_half(own_ref, *scratch):
        part_ref[g] = tri


def incoming_kernel(part_ref, other_ref, out_hbm, wide_ref, left_ref, right_ref, turn_ref, turned_ref, tri_ref,
                    mix_ref, tail_ref, ready_ref, sems):
    for g, tri in incoming_half(other_ref, wide_ref, left_ref, right_ref, turn_ref, turned_ref):
        tri_ref[g, 0:384, :] = part_ref[g] + tri
    send_tri(tri_ref, mix_ref, tail_ref, ready_ref, out_hbm, sems)


def finish(tri_ref, state_ref, gate_hbm, outcat_hbm, next_ref, scaled_ref, stat_ref, gate_ref, outcat_ref, fetch_sems,
           done=None, after=None):
    fetches = [
        pltpu.make_async_copy(outcat_hbm, outcat_ref, fetch_sems.at[0]),
        pltpu.make_async_copy(gate_hbm, gate_ref, fetch_sems.at[1]),
    ]
    for fetch in fetches + ([after] if after is not None else []):
        fetch.start()

    def stats(i, carry):
        total, square = carry
        t = tri_ref[aligned(i * 144, 144, 144), :].astype(F32)
        first, second = t[0:72], t[72:144]
        return total + first + second, square + first * first + second * second

    zero = jnp.zeros((72, 128), F32)
    total, square = lax.fori_loop(0, 16, stats, (zero, zero))
    stat_ref[0, 0:72, :] = total
    stat_ref[1, 0:72, :] = square

    def gather(n):
        return sum(stat_ref[n, 18 * q : 18 * q + 18, :] for q in range(4)) * (1.0 / CH)

    average = gather(0)
    scale = lax.rsqrt(gather(1) - average * average + EPS)
    for q in range(4):
        stat_ref[0, 18 * q : 18 * q + 18, :] = average
        stat_ref[1, 18 * q : 18 * q + 18, :] = scale

    def rescale(i, carry):
        t = tri_ref[aligned(i * 144, 144, 144), :].astype(F32)
        for half in range(2):
            part = (t[72 * half : 72 * half + 72] - stat_ref[0, 0:72, :]) * stat_ref[1, 0:72, :]
            scaled_ref[aligned(i * 144 + 72 * half, 72, 72), :] = part
        return carry

    lax.fori_loop(0, 16, rescale, 0)
    for fetch in fetches:
        fetch.wait()
    w_cat = outcat_ref[...]

    def combine(i, carry):
        pieces = [split_bf16(scaled_ref[pl.ds(2 * i + half, CH, stride=PACK), :]) for half in range(2)]
        high = jnp.concatenate([pieces[0][0], pieces[1][0]], axis=1)
        low = jnp.concatenate([pieces[0][1], pieces[1][1]], axis=1)
        values = matmul(w_cat, jnp.concatenate([high, high, low], axis=0), ((1,), (0,)))
        for half in range(2):
            t = 2 * i + half
            value = state_ref[t] + gate_ref[t] * values[:, 128 * half : 128 * half + 128]
            if done is None:
                next_ref[t] = value
            else:
                value = value.T
                next_ref[aligned(t * COLS, COLS, COLS), :] = value[:COLS]
                next_ref[tail_pixels(t), :] = value[COLS:]
        return carry

    if done is None:
        lax.fori_loop(0, PACK // 2, combine, 0, unroll=3)
    else:
        for n in range(3):
            for i in range(3):
                combine(3 * n + i, 0)
            done(n)
        done(3)


def middle_kernel(edge_ref, tri_ref, state_ref, gate_hbm, outcat_hbm, projcat_hbm, next_ref, send_ref,
                  projcat_ref, sems, norm_ref, mix_ref, *scratch):
    fetch = pltpu.make_async_copy(projcat_hbm, projcat_ref, sems.at[0])
    finish(tri_ref, state_ref, gate_hbm, outcat_hbm, next_ref, *scratch, after=fetch)
    fetch.wait()
    project(next_ref, projcat_ref[...], edge_ref, norm_ref, mix_ref, send_ref)


def last_kernel(tri_ref, state_ref, gate_hbm, outcat_hbm, out_hbm, next_ref, sems, *scratch):
    copies = []

    def done(n):
        at = pl.ds(n * PIX // 4, PIX // 4)
        copies.append(pltpu.make_async_copy(next_ref.at[at], out_hbm.at[at], sems.at[n]))
        copies[-1].start()

    finish(tri_ref, state_ref, gate_hbm, outcat_hbm, next_ref, *scratch, done=done)
    for copy in copies:
        copy.wait()


VM = pl.BlockSpec(memory_space=pltpu.VMEM)
SM = pl.BlockSpec(memory_space=pltpu.SMEM)
HB = pl.BlockSpec(memory_space=pltpu.HBM)
STATE = pltpu.VMEM((PACK, CH, 128), F32)
SEND = pltpu.VMEM((CH * 2 * PACK, 128), BF16)
TRI = pltpu.HBM((CH * PACK, 128), BF16)
GATE = pltpu.HBM((PACK, CH, 128), F32)
EDGE = pltpu.VMEM((PACK, 128), F32)
OUTCAT = pltpu.HBM((CH, 3 * CH), BF16)
PROJCAT = pltpu.HBM((4 * CH, 3 * CH), BF16)
PROJECT_SCRATCH = [pltpu.VMEM((PACK // 2, 384, 256), BF16), pltpu.VMEM((CH * 2 * PACK, 128), F32)]
FINISH_SCRATCH = [
    pltpu.VMEM((CH * PACK, 128), F32), pltpu.VMEM((2, 72, 128), F32), pltpu.VMEM((PACK, CH, 128), F32),
    pltpu.VMEM((CH, 3 * CH), BF16), pltpu.SemaphoreType.DMA((2,)),
]
SEND_SCRATCH = [
    pltpu.VMEM((8, 384, 128), F32), pltpu.VMEM((CH * PACK, 128), F32), pltpu.VMEM((400, 128), F32),
    pltpu.VMEM((CH * PACK, 128), BF16), pltpu.SemaphoreType.DMA((4,)),
]
WIDE = pltpu.VMEM((CH * 2 * PACK + 16, 128), F32)
HALF = pltpu.VMEM((384, 1024), F32)
RIGHT = pltpu.VMEM((1024, 1024), F32)
HALF_SCRATCH = [WIDE, HALF, HALF, pltpu.VMEM((2, 128, 384), F32), pltpu.VMEM((384, 384), F32)]
PART = pltpu.VMEM((8, 384, 128), F32)


def call(kernel, out_shape, operands, scratch=(), specs=None, out_specs=None, mib=16, **options):
    outs = out_shape if isinstance(out_shape, tuple) else None
    return pl.pallas_call(
        kernel,
        out_shape=out_shape,
        in_specs=specs or [VM] * len(operands),
        out_specs=out_specs or (VM if outs is None else (VM,) * len(outs)),
        scratch_shapes=list(scratch),
        compiler_params=pltpu.CompilerParams(vmem_limit_bytes=mib * 1024 * 1024),
        **options,
    )(*operands)


def near(value):
    return pltpu.with_memory_space_constraint(value, pltpu.VMEM)


def far(value):
    return pltpu.with_memory_space_constraint(value, pltpu.HBM)


def exchange(message, rows):
    moved = lax.all_to_all(message.reshape(CH, rows // 2, 2, 128), CHIPS, split_axis=0, concat_axis=0, tiled=True)
    return moved.reshape(CH * rows, 128)


def partner(value):
    return lax.ppermute(value, "core", [(0, 1), (1, 0)])


def gating(layer, outs, *operands):
    cost = pl.CostEstimate(flops=3 * 2 * PIX * CH * CH, transcendentals=PIX * CH, bytes_accessed=8 * PIX * CH)
    return call(gate_kernel(layer), outs, operands, cost_estimate=cost)


def on_device(pair, residue_mask, hotspot, interface, proj_weight, gate_weight, out_weight):
    send, edge, state = call(
        first_kernel, (SEND, EDGE, STATE),
        (far(residue_mask), far(hotspot), far(interface), far(pair.reshape(PIX, CH)), far(proj_weight)),
        [pltpu.SMEM((768,), jnp.int32), pltpu.SMEM((768,), jnp.int32), pltpu.VMEM((ROWS, COLS), jnp.int32),
         pltpu.VMEM((ROWS, 128), jnp.int32), pltpu.VMEM((PIX, CH), F32), pltpu.VMEM((CH, 4 * CH), F32),
         pltpu.SemaphoreType.DMA((5,))] + PROJECT_SCRATCH,
        [HB] * 5,
    )
    own = exchange(send, 2 * PACK)
    other = partner(own)
    left, right = call(outgoing_own, (pltpu.VMEM((384, 1024), BF16), RIGHT), (near(own),), [WIDE, HALF])
    tri, _ = call(
        outgoing_kernel, (TRI, RIGHT), (near(left), near(right), near(other)), [WIDE] + SEND_SCRATCH,
        out_specs=(HB, VM), input_output_aliases={1: 1},
    )
    tri = exchange(tri, PACK)
    gate, outcat, projcat = gating(0, (GATE, OUTCAT, PROJCAT), near(state), gate_weight, out_weight, proj_weight)
    state, send = call(
        middle_kernel, (STATE, SEND),
        (near(edge), near(tri), near(state), far(gate), far(outcat), far(projcat)),
        [pltpu.VMEM((4 * CH, 3 * CH), BF16), pltpu.SemaphoreType.DMA((1,))] + PROJECT_SCRATCH + FINISH_SCRATCH,
        [VM, VM, VM, HB, HB, HB],
    )
    own = exchange(send, 2 * PACK)
    other = partner(own)
    part = call(incoming_own, PART, (near(own),), HALF_SCRATCH)
    tri = call(incoming_kernel, TRI, (near(part), near(other)), HALF_SCRATCH + SEND_SCRATCH, out_specs=HB)
    tri = exchange(tri, PACK)
    gate, outcat = gating(1, (GATE, OUTCAT), near(state), gate_weight, out_weight)
    state = call(
        last_kernel, jax.ShapeDtypeStruct((PIX, CH), F32), (near(tri), near(state), far(gate), far(outcat)),
        [pltpu.VMEM((PIX, CH), F32), pltpu.SemaphoreType.DMA((4,))] + FINISH_SCRATCH, [VM, VM, HB, HB], out_specs=HB,
    )
    return state.reshape(ROWS, COLS, CH)


def solution(mesh):
    grid = Mesh(mesh.devices.reshape(8, 2, 2, 4, 2), ("z", "yl", "core", "x", "yh"))
    rows = ("z", "yl", "core")
    cols = ("x", "yh")
    return jax.shard_map(
        on_device,
        mesh=grid,
        in_specs=(P(rows, cols, None), P(), P(), P(rows, cols), P(), P(), P()),
        out_specs=P(rows, cols, None),
        check_vma=False,
    )
```

```python
import jax
import jax.numpy as jnp
from jax import lax
from jax.experimental import pallas as pl
from jax.experimental.pallas import tpu as pltpu
from jax.sharding import Mesh, PartitionSpec as P

EPS = 1e-05
F32 = jnp.float32
BF16 = jnp.bfloat16
ROWS = 24
COLS = 96
PIX = ROWS * COLS
CH = 128
PACK = 18
CHIPS = ("z", "yl", "x", "yh")


def split_bf16(value):
    high = value.astype(BF16)
    low = (value - high.astype(F32)).astype(BF16)
    return high, low


def lanes(shape):
    return lax.broadcasted_iota(jnp.int32, shape, len(shape) - 1)


def matmul(a, b, dims):
    return lax.dot_general(a, b, (dims, ((), ())), preferred_element_type=F32)


def stacked(weight, axis):
    high, low = split_bf16(weight)
    return jnp.concatenate([high, low, high], axis=axis)


def aligned(start, size, unit):
    return pl.ds(pl.multiple_of(start, unit), size)


def packed_edge(mask_sm, hot_sm, inter_ref, edge_ref, rows_ref):
    band = (lax.axis_index("z") * 2 + lax.axis_index("yl")) * 2 + lax.axis_index("core")
    hid = lax.axis_index("x") * 2 + lax.axis_index("yh")
    lane = lanes((1, 128))
    col_mask = jnp.zeros((1, 128), jnp.int32)
    col_hot = jnp.zeros((1, 128), jnp.int32)
    for c in range(COLS):
        col_mask = jnp.where(lane == c, mask_sm[hid * COLS + c], col_mask)
        col_hot = jnp.where(lane == c, hot_sm[hid * COLS + c], col_hot)
    rows_ref[...] = jnp.zeros((ROWS, 128), jnp.int32)
    rows_ref[:, 0:COLS] = inter_ref[...]
    for r in range(ROWS):
        at = slice(r, r + 1)
        flags = jnp.maximum(rows_ref[at, :], jnp.maximum(col_hot, hot_sm[band * ROWS + r]))
        rows_ref[at, :] = flags * col_mask * mask_sm[band * ROWS + r]
    for t in range(PACK):
        tail = pltpu.roll(jnp.broadcast_to(rows_ref[18 + t % 6 : 19 + t % 6, :], (8, 128)), 96 - 32 * (t // 6), 1)
        edge_ref[t : t + 1, :] = jnp.where(lane < COLS, rows_ref[t : t + 1, :], tail[0:1, :]).astype(F32)


def tail_pixels(t):
    return aligned((18 + t % 6) * COLS + 32 * (t // 6), 32, 32)


def normalized(x):
    centred = x - jnp.mean(x, axis=0, keepdims=True)
    variance = jnp.mean(centred * centred, axis=0, keepdims=True)
    high, low = split_bf16(centred * lax.rsqrt(variance + EPS))
    return jnp.concatenate([high, high, low], axis=0)


def project(state_ref, w_cat, edge_ref, norm_ref, mix_ref, send_ref, normalize=None):
    def prepare(i, carry):
        for half in range(2):
            norm_ref[i, :, 128 * half : 128 * half + 128] = normalized(state_ref[2 * i + half])
        return carry

    lax.fori_loop(0, PACK // 2, normalize or prepare, 0, unroll=3)

    w_value = jnp.concatenate([w_cat[:CH], w_cat[2 * CH : 3 * CH]], axis=0)
    w_gate = jnp.concatenate([w_cat[CH : 2 * CH, : 2 * CH], w_cat[3 * CH :, : 2 * CH]], axis=0)

    def pair(i, carry):
        values = matmul(w_value, norm_ref[i], ((1,), (0,)))
        gates = matmul(w_gate, norm_ref[i, 0 : 2 * CH, :], ((1,), (0,)))
        for half in range(2):
            t = 2 * i + half
            at = slice(128 * half, 128 * half + 128)
            edge = edge_ref[pl.ds(t, 1), :]
            left = edge * jax.nn.sigmoid(gates[:CH, at]) * values[:CH, at]
            right = edge * jax.nn.sigmoid(gates[CH:, at]) * values[CH:, at]
            mix_ref[pl.ds(t, CH, stride=2 * PACK), :] = left
            mix_ref[pl.ds(t + PACK, CH, stride=2 * PACK), :] = right
        return carry

    lax.fori_loop(0, PACK // 2, pair, 0, unroll=3)

    def convert(i, carry):
        at = aligned(i * 256, 256, 256)
        send_ref[at, :] = mix_ref[at, :].astype(BF16)
        return carry

    lax.fori_loop(0, 18, convert, 0)


def first_kernel(mask_hbm, hot_hbm, inter_hbm, pair_hbm, proj_hbm, send_ref, edge_ref, state_ref, mask_sm, hot_sm,
                 inter_ref, rows_ref, pair_ref, proj_ref, sems, norm_ref, mix_ref):
    copies = [
        pltpu.make_async_copy(source, target, sems.at[n])
        for n, (source, target) in enumerate((
            (mask_hbm, mask_sm), (hot_hbm, hot_sm), (inter_hbm, inter_ref), (proj_hbm.at[0], proj_ref),
            (pair_hbm, pair_ref),
        ))
    ]
    for copy in copies:
        copy.start()
    for copy in copies[:3]:
        copy.wait()
    packed_edge(mask_sm, hot_sm, inter_ref, edge_ref, rows_ref)
    copies[3].wait()
    w_cat = stacked(proj_ref[...].T, 1)
    copies[4].wait()

    def prepare(i, carry):
        for half in range(2):
            t = 2 * i + half
            x = jnp.concatenate([pair_ref[aligned(t * COLS, COLS, COLS), :], pair_ref[tail_pixels(t), :]], axis=0).T
            state_ref[t] = x
            norm_ref[i, :, 128 * half : 128 * half + 128] = normalized(x)
        return carry

    project(state_ref, w_cat, edge_ref, norm_ref, mix_ref, send_ref, prepare)


def gate_kernel(layer):
    def body(state_ref, gatew_ref, outw_ref, *refs):
        if layer == 0:
            proj_ref, gate_ref, outcat_ref, projcat_ref = refs
            projcat_ref[...] = stacked(proj_ref[1].T, 1)
        else:
            gate_ref, outcat_ref = refs
        outcat_ref[...] = stacked(outw_ref[layer].T, 1)
        cat = stacked(gatew_ref[layer].T, 1)

        def step(t, carry):
            gate_ref[t] = jax.nn.sigmoid(matmul(cat, normalized(state_ref[t]), ((1,), (0,))))
            return carry

        lax.fori_loop(0, PACK, step, 0, unroll=3)

    return body


PAD = 8


def widen(source_ref, wide_ref):
    def step(i, carry):
        wide_ref[aligned(PAD + i * 256, 256, 8), :] = source_ref[aligned(i * 256, 256, 256), :].astype(F32)
        return carry

    lax.fori_loop(0, 18, step, 0)


def unpack(wide_ref, base):
    lane = lanes((8, 128))
    sub = lax.broadcasted_iota(jnp.int32, (8, 128), 0)

    def rows(at):
        return wide_ref[pl.ds(base + at, 8), :]

    third = jnp.where(lane < 64, pltpu.roll(rows(4), 64, 1), pltpu.roll(rows(10), 96, 1))
    third = jnp.where(lane < 32, pltpu.roll(rows(-2), 32, 1), third)
    return rows(0), rows(8), jnp.where(sub < 2, rows(16), third)


def place(wide_ref, base, target_ref, start, column, clear):
    lane = lanes((8, 128))
    for n, part in enumerate(unpack(wide_ref, base)):
        if clear:
            part = jnp.where(lane < COLS, part, 0.0)
        target_ref[aligned(start + 8 * n, 8, 8), column] = part


def tail_slot(half, g):
    return 8 + (half * 8 + g) * 24


def send_tri(tri_ref, mix_ref, tail_ref, ready_ref, out_hbm, sems):
    lane = lanes((8, 128))

    def send(i, carry):
        blocks = [(half, g, (2 * i + half) * 24) for half in range(2) for g in range(8)]
        for half, g, base in blocks:
            slot = tail_slot(half, g)
            value = tri_ref[g, aligned(base + 16, 8, 8), :]
            tail_ref[slot + 10 : slot + 18, :] = pltpu.roll(value, 32, 1)
            tail_ref[slot + 4 : slot + 12, :] = pltpu.roll(value, 64, 1)
            tail_ref[slot - 2 : slot + 6, :] = pltpu.roll(value, 96, 1)
        for half, g, base in blocks:
            slot = tail_slot(half, g)
            target = ((2 * i + half) * 8 + g) * PACK
            for n in range(3):
                tail = tail_ref[slot + 8 * n : slot + 8 * n + 8, :]
                value = jnp.where(lane < COLS, tri_ref[g, aligned(base + 8 * n, 8, 8), :], tail)
                if n < 2:
                    mix_ref[pl.ds(target + 8 * n, 8), :] = value
                else:
                    mix_ref[pl.ds(target + 16, 2), :] = value[0:2]
        at = aligned(i * 288, 288, 288)
        ready_ref[at, :] = mix_ref[at, :].astype(BF16)
        return carry

    copies = []
    for n in range(4):
        lax.fori_loop(2 * n, 2 * n + 2, send, 0)
        at = pl.ds(576 * n, 576)
        copies.append(pltpu.make_async_copy(ready_ref.at[at], out_hbm.at[at], sems.at[n]))
        copies[-1].start()
    for copy in copies:
        copy.wait()


def outgoing_own(own_ref, left_ref, right_ref, wide_ref, keep_ref):
    core = lax.axis_index("core")
    widen(own_ref, wide_ref)

    def step(b, carry):
        start = (b // 2) * 128 + (b % 2) * 48 + core * 24
        for g in range(8):
            at = slice(128 * g, 128 * g + 128)
            message = PAD + (b * 8 + g) * 2 * PACK
            place(wide_ref, message, keep_ref, b * 24, at, False)
            place(wide_ref, message + PACK, right_ref, start, at, True)
        return carry

    lax.fori_loop(0, 16, step, 0, unroll=2)
    for z in range(8):
        right_ref[128 * z + 96 : 128 * z + 128, :] = jnp.zeros((32, 1024), F32)
    left_ref[...] = keep_ref[...].astype(BF16)


def outgoing_kernel(left_ref, _, other_ref, out_hbm, right_ref, wide_ref, tri_ref, *scratch):
    core = lax.axis_index("core")
    widen(other_ref, wide_ref)

    def step(b, carry):
        start = (b // 2) * 128 + (b % 2) * 48 + 24 - core * 24
        for g in range(8):
            message = PAD + (b * 8 + g) * 2 * PACK
            place(wide_ref, message + PACK, right_ref, start, slice(128 * g, 128 * g + 128), True)
        return carry

    lax.fori_loop(0, 16, step, 0, unroll=2)
    left = left_ref[...]
    for n in range(4):
        tri = matmul(left, right_ref[256 * n : 256 * n + 256, :].astype(BF16), ((1,), (1,)))
        tri_ref[2 * n, 0:384, :] = tri[:, 0:128]
        tri_ref[2 * n + 1, 0:384, :] = tri[:, 128:256]
    mix_ref, tail_ref, ready_ref, sems = scratch
    send_tri(tri_ref, mix_ref, tail_ref, ready_ref, out_hbm, sems)


def incoming_half(source_ref, wide_ref, left_ref, right_ref, turn_ref, turned_ref):
    core = lax.axis_index("core")
    widen(source_ref, wide_ref)
    lane = lanes((8, 128))
    keep = lax.broadcasted_iota(jnp.int32, (8, 128), 0) < 6

    def step(b, carry):
        at = aligned(8 * b, 8, 8)
        for g in range(8):
            column = slice(128 * g, 128 * g + 128)
            message = PAD + (b * 8 + g) * 2 * PACK
            for p in range(3):
                left_ref[g, p, at, :] = wide_ref[pl.ds(message + 6 * p, 8), :]
            right = [wide_ref[pl.ds(message + PACK + 6 * p, 8), :] for p in range(3)]
            tail = jnp.where(lane < 64, pltpu.roll(right[1], 64, 1), pltpu.roll(right[2], 96, 1))
            right.append(jnp.where(lane < 32, pltpu.roll(right[0], 32, 1), tail))
            for p in range(4):
                right_ref[p, at, column] = jnp.where(keep, right[p], 0.0)
        return carry

    lax.fori_loop(0, 16, step, 0, unroll=2)
    for z in range(8):
        slot = z % 2
        for p in range(3):
            turned = left_ref[z, p].T
            turn_ref[slot, p] = turned
            turn_ref[slot, 3, 32 * p : 32 * p + 32, :] = turned[COLS:]
        for y in range(2):
            rows = slice(48 * z + 24 * y, 48 * z + 24 * y + 24)
            for p in range(4):
                turned_ref[rows, 128 * p : 128 * p + 128] = turn_ref[slot, p, aligned(48 * y + 24 * core, 24, 8), :]
    left = turned_ref[...].astype(BF16)
    for n in range(4):
        right = right_ref[:, :, 256 * n : 256 * n + 256].reshape(512, 256).astype(BF16)
        tri = matmul(left, right, ((1,), (0,)))
        yield 2 * n, tri[:, 0:128]
        yield 2 * n + 1, tri[:, 128:256]


def incoming_own(own_ref, part_ref, *scratch):
    for g, tri in incoming_half(own_ref, *scratch):
        part_ref[g] = tri


def incoming_kernel(part_ref, other_ref, out_hbm, wide_ref, left_ref, right_ref, turn_ref, turned_ref, tri_ref,
                    mix_ref, tail_ref, ready_ref, sems):
    for g, tri in incoming_half(other_ref, wide_ref, left_ref, right_ref, turn_ref, turned_ref):
        tri_ref[g, 0:384, :] = part_ref[g] + tri
    send_tri(tri_ref, mix_ref, tail_ref, ready_ref, out_hbm, sems)


def finish(tri_ref, state_ref, gate_hbm, outcat_hbm, next_ref, scaled_ref, stat_ref, gate_ref, outcat_ref, fetch_sems,
           done=None, after=None):
    fetches = [
        pltpu.make_async_copy(outcat_hbm, outcat_ref, fetch_sems.at[0]),
        pltpu.make_async_copy(gate_hbm, gate_ref, fetch_sems.at[1]),
    ]
    for fetch in fetches + ([after] if after is not None else []):
        fetch.start()

    def stats(i, carry):
        total, square = carry
        at = aligned(i * 144, 144, 144)
        t = tri_ref[at, :].astype(F32)
        scaled_ref[at, :] = t
        first, second = t[0:72], t[72:144]
        return total + first + second, square + first * first + second * second

    zero = jnp.zeros((72, 128), F32)
    total, square = lax.fori_loop(0, 16, stats, (zero, zero))
    stat_ref[0, 0:72, :] = total
    stat_ref[1, 0:72, :] = square

    def gather(n):
        return sum(stat_ref[n, 18 * q : 18 * q + 18, :] for q in range(4)) * (1.0 / CH)

    average = gather(0)
    scale = lax.rsqrt(gather(1) - average * average + EPS)
    stat_ref[0, 0:18, :] = average
    stat_ref[1, 0:18, :] = scale
    for fetch in fetches:
        fetch.wait()
    w_cat = outcat_ref[...]

    def combine(i, carry):
        pieces = []
        for half in range(2):
            t = 2 * i + half
            centred = scaled_ref[pl.ds(t, CH, stride=PACK), :] - stat_ref[0, pl.ds(t, 1), :]
            pieces.append(split_bf16(centred * stat_ref[1, pl.ds(t, 1), :]))
        high = jnp.concatenate([pieces[0][0], pieces[1][0]], axis=1)
        low = jnp.concatenate([pieces[0][1], pieces[1][1]], axis=1)
        values = matmul(w_cat, jnp.concatenate([high, high, low], axis=0), ((1,), (0,)))
        for half in range(2):
            t = 2 * i + half
            value = state_ref[t] + gate_ref[t] * values[:, 128 * half : 128 * half + 128]
            if done is None:
                next_ref[t] = value
            else:
                value = value.T
                next_ref[aligned(t * COLS, COLS, COLS), :] = value[:COLS]
                next_ref[tail_pixels(t), :] = value[COLS:]
        return carry

    if done is None:
        lax.fori_loop(0, PACK // 2, combine, 0, unroll=3)
    else:
        for n in range(3):
            for i in range(3):
                combine(3 * n + i, 0)
            done(n)
        done(3)


def middle_kernel(edge_ref, tri_ref, state_ref, gate_hbm, outcat_hbm, projcat_hbm, next_ref, send_ref,
                  projcat_ref, sems, norm_ref, mix_ref, *scratch):
    fetch = pltpu.make_async_copy(projcat_hbm, projcat_ref, sems.at[0])
    finish(tri_ref, state_ref, gate_hbm, outcat_hbm, next_ref, *scratch, after=fetch)
    fetch.wait()
    project(next_ref, projcat_ref[...], edge_ref, norm_ref, mix_ref, send_ref)


def last_kernel(tri_ref, state_ref, gate_hbm, outcat_hbm, out_hbm, next_ref, sems, *scratch):
    copies = []

    def done(n):
        at = pl.ds(n * PIX // 4, PIX // 4)
        copies.append(pltpu.make_async_copy(next_ref.at[at], out_hbm.at[at], sems.at[n]))
        copies[-1].start()

    finish(tri_ref, state_ref, gate_hbm, outcat_hbm, next_ref, *scratch, done=done)
    for copy in copies:
        copy.wait()


VM = pl.BlockSpec(memory_space=pltpu.VMEM)
SM = pl.BlockSpec(memory_space=pltpu.SMEM)
HB = pl.BlockSpec(memory_space=pltpu.HBM)
STATE = pltpu.VMEM((PACK, CH, 128), F32)
SEND = pltpu.VMEM((CH * 2 * PACK, 128), BF16)
TRI = pltpu.HBM((CH * PACK, 128), BF16)
GATE = pltpu.HBM((PACK, CH, 128), F32)
EDGE = pltpu.VMEM((PACK, 128), F32)
OUTCAT = pltpu.HBM((CH, 3 * CH), BF16)
PROJCAT = pltpu.HBM((4 * CH, 3 * CH), BF16)
PROJECT_SCRATCH = [pltpu.VMEM((PACK // 2, 384, 256), BF16), pltpu.VMEM((CH * 2 * PACK, 128), F32)]
FINISH_SCRATCH = [
    pltpu.VMEM((CH * PACK, 128), F32), pltpu.VMEM((2, 72, 128), F32), pltpu.VMEM((PACK, CH, 128), F32),
    pltpu.VMEM((CH, 3 * CH), BF16), pltpu.SemaphoreType.DMA((2,)),
]
SEND_SCRATCH = [
    pltpu.VMEM((8, 384, 128), F32), pltpu.VMEM((CH * PACK, 128), F32), pltpu.VMEM((400, 128), F32),
    pltpu.VMEM((CH * PACK, 128), BF16), pltpu.SemaphoreType.DMA((4,)),
]
WIDE = pltpu.VMEM((CH * 2 * PACK + 16, 128), F32)
HALF = pltpu.VMEM((384, 1024), F32)
RIGHT = pltpu.VMEM((1024, 1024), F32)
HALF_SCRATCH = [
    WIDE, pltpu.VMEM((8, 3, 128, 128), F32), pltpu.VMEM((4, 128, 1024), F32), pltpu.VMEM((2, 4, 128, 128), F32),
    pltpu.VMEM((384, 512), F32),
]
PART = pltpu.VMEM((8, 384, 128), F32)


def call(kernel, out_shape, operands, scratch=(), specs=None, out_specs=None, mib=16, **options):
    outs = out_shape if isinstance(out_shape, tuple) else None
    return pl.pallas_call(
        kernel,
        out_shape=out_shape,
        in_specs=specs or [VM] * len(operands),
        out_specs=out_specs or (VM if outs is None else (VM,) * len(outs)),
        scratch_shapes=list(scratch),
        compiler_params=pltpu.CompilerParams(vmem_limit_bytes=mib * 1024 * 1024),
        **options,
    )(*operands)


def near(value):
    return pltpu.with_memory_space_constraint(value, pltpu.VMEM)


def far(value):
    return pltpu.with_memory_space_constraint(value, pltpu.HBM)


def exchange(message, rows):
    moved = lax.all_to_all(message.reshape(CH, rows // 2, 2, 128), CHIPS, split_axis=0, concat_axis=0, tiled=True)
    return moved.reshape(CH * rows, 128)


def partner(value):
    return lax.ppermute(value, "core", [(0, 1), (1, 0)])


def gating(layer, outs, *operands):
    cost = pl.CostEstimate(flops=3 * 2 * PIX * CH * CH, transcendentals=PIX * CH, bytes_accessed=8 * PIX * CH)
    return call(gate_kernel(layer), outs, operands, cost_estimate=cost)


def on_device(pair, residue_mask, hotspot, interface, proj_weight, gate_weight, out_weight):
    send, edge, state = call(
        first_kernel, (SEND, EDGE, STATE),
        (far(residue_mask), far(hotspot), far(interface), far(pair.reshape(PIX, CH)), far(proj_weight)),
        [pltpu.SMEM((768,), jnp.int32), pltpu.SMEM((768,), jnp.int32), pltpu.VMEM((ROWS, COLS), jnp.int32),
         pltpu.VMEM((ROWS, 128), jnp.int32), pltpu.VMEM((PIX, CH), F32), pltpu.VMEM((CH, 4 * CH), F32),
         pltpu.SemaphoreType.DMA((5,))] + PROJECT_SCRATCH,
        [HB] * 5,
    )
    own = exchange(send, 2 * PACK)
    other = partner(own)
    left, right = call(outgoing_own, (pltpu.VMEM((384, 1024), BF16), RIGHT), (near(own),), [WIDE, HALF])
    tri, _ = call(
        outgoing_kernel, (TRI, RIGHT), (near(left), near(right), near(other)), [WIDE] + SEND_SCRATCH,
        out_specs=(HB, VM), input_output_aliases={1: 1},
    )
    tri = exchange(tri, PACK)
    gate, outcat, projcat = gating(0, (GATE, OUTCAT, PROJCAT), near(state), gate_weight, out_weight, proj_weight)
    state, send = call(
        middle_kernel, (STATE, SEND),
        (near(edge), near(tri), near(state), far(gate), far(outcat), far(projcat)),
        [pltpu.VMEM((4 * CH, 3 * CH), BF16), pltpu.SemaphoreType.DMA((1,))] + PROJECT_SCRATCH + FINISH_SCRATCH,
        [VM, VM, VM, HB, HB, HB],
    )
    own = exchange(send, 2 * PACK)
    other = partner(own)
    part = call(incoming_own, PART, (near(own),), HALF_SCRATCH)
    tri = call(incoming_kernel, TRI, (near(part), near(other)), HALF_SCRATCH + SEND_SCRATCH, out_specs=HB)
    tri = exchange(tri, PACK)
    gate, outcat = gating(1, (GATE, OUTCAT), near(state), gate_weight, out_weight)
    state = call(
        last_kernel, jax.ShapeDtypeStruct((PIX, CH), F32), (near(tri), near(state), far(gate), far(outcat)),
        [pltpu.VMEM((PIX, CH), F32), pltpu.SemaphoreType.DMA((4,))] + FINISH_SCRATCH, [VM, VM, HB, HB], out_specs=HB,
    )
    return state.reshape(ROWS, COLS, CH)


def solution(mesh):
    grid = Mesh(mesh.devices.reshape(8, 2, 2, 4, 2), ("z", "yl", "core", "x", "yh"))
    rows = ("z", "yl", "core")
    cols = ("x", "yh")
    return jax.shard_map(
        on_device,
        mesh=grid,
        in_specs=(P(rows, cols, None), P(), P(), P(rows, cols), P(), P(), P()),
        out_specs=P(rows, cols, None),
        check_vma=False,
    )
```

```python
import jax
import jax.numpy as jnp
from jax import lax
from jax.experimental import pallas as pl
from jax.experimental.pallas import tpu as pltpu
from jax.sharding import Mesh, PartitionSpec as P

EPS = 1e-05
F32 = jnp.float32
BF16 = jnp.bfloat16
ROWS = 24
COLS = 96
PIX = ROWS * COLS
CH = 128
PACK = 18
CHIPS = ("z", "yl", "x", "yh")


def split_bf16(value):
    high = value.astype(BF16)
    low = (value - high.astype(F32)).astype(BF16)
    return high, low


def lanes(shape):
    return lax.broadcasted_iota(jnp.int32, shape, len(shape) - 1)


def matmul(a, b, dims):
    return lax.dot_general(a, b, (dims, ((), ())), preferred_element_type=F32)


def stacked(weight, axis):
    high, low = split_bf16(weight)
    return jnp.concatenate([high, low, high], axis=axis)


def aligned(start, size, unit):
    return pl.ds(pl.multiple_of(start, unit), size)


def packed_edge(mask_sm, hot_sm, inter_ref, edge_ref, rows_ref):
    band = (lax.axis_index("z") * 2 + lax.axis_index("yl")) * 2 + lax.axis_index("core")
    hid = lax.axis_index("x") * 2 + lax.axis_index("yh")
    lane = lanes((1, 128))
    col_mask = jnp.zeros((1, 128), jnp.int32)
    col_hot = jnp.zeros((1, 128), jnp.int32)
    for c in range(COLS):
        col_mask = jnp.where(lane == c, mask_sm[hid * COLS + c], col_mask)
        col_hot = jnp.where(lane == c, hot_sm[hid * COLS + c], col_hot)
    rows_ref[...] = jnp.zeros((ROWS, 128), jnp.int32)
    rows_ref[:, 0:COLS] = inter_ref[...]
    for r in range(ROWS):
        at = slice(r, r + 1)
        flags = jnp.maximum(rows_ref[at, :], jnp.maximum(col_hot, hot_sm[band * ROWS + r]))
        rows_ref[at, :] = flags * col_mask * mask_sm[band * ROWS + r]
    for t in range(PACK):
        tail = pltpu.roll(jnp.broadcast_to(rows_ref[18 + t % 6 : 19 + t % 6, :], (8, 128)), 96 - 32 * (t // 6), 1)
        edge_ref[t : t + 1, :] = jnp.where(lane < COLS, rows_ref[t : t + 1, :], tail[0:1, :]).astype(F32)


def tail_pixels(t):
    return aligned((18 + t % 6) * COLS + 32 * (t // 6), 32, 32)


def normalized(x):
    centred = x - jnp.mean(x, axis=0, keepdims=True)
    variance = jnp.mean(centred * centred, axis=0, keepdims=True)
    high, low = split_bf16(centred * lax.rsqrt(variance + EPS))
    return jnp.concatenate([high, high, low], axis=0)


def project(source, w_cat, edge_ref, mix_ref, send_ref):
    def group(i, carry):
        values = matmul(w_cat, jnp.concatenate([normalized(x) for x in source(i)], axis=1), ((1,), (0,)))
        for half in range(2):
            t = 2 * i + half
            part = values[:, 128 * half : 128 * half + 128]
            edge = edge_ref[pl.ds(t, 1), :]
            left = edge * jax.nn.sigmoid(part[CH : 2 * CH]) * part[:CH]
            right = edge * jax.nn.sigmoid(part[3 * CH :]) * part[2 * CH : 3 * CH]
            mix_ref[pl.ds(t, CH, stride=2 * PACK), :] = left
            mix_ref[pl.ds(t + PACK, CH, stride=2 * PACK), :] = right
        return carry

    lax.fori_loop(0, PACK // 2, group, 0, unroll=True)

    def convert(i, carry):
        at = aligned(i * 256, 256, 256)
        send_ref[at, :] = mix_ref[at, :].astype(BF16)
        return carry

    lax.fori_loop(0, 18, convert, 0, unroll=2)


def first_kernel(mask_hbm, hot_hbm, inter_hbm, pair_hbm, proj_hbm, send_ref, edge_ref, state_ref, mask_sm, hot_sm,
                 inter_ref, rows_ref, pair_ref, proj_ref, sems, mix_ref):
    copies = [
        pltpu.make_async_copy(source, target, sems.at[n])
        for n, (source, target) in enumerate((
            (mask_hbm, mask_sm), (hot_hbm, hot_sm), (inter_hbm, inter_ref), (proj_hbm.at[0], proj_ref),
            (pair_hbm, pair_ref),
        ))
    ]
    for copy in copies:
        copy.start()
    for copy in copies[:3]:
        copy.wait()
    packed_edge(mask_sm, hot_sm, inter_ref, edge_ref, rows_ref)
    copies[3].wait()
    w_cat = stacked(proj_ref[...].T, 1)
    copies[4].wait()

    def source(i):
        for half in range(2):
            t = 2 * i + half
            rows = (pair_ref[aligned(t * COLS, COLS, COLS), :], pair_ref[tail_pixels(t), :])
            x = jnp.concatenate(rows, axis=0).T
            state_ref[t] = x
            yield x

    project(source, w_cat, edge_ref, mix_ref, send_ref)


def gate_kernel(layer):
    def body(state_ref, gatew_ref, outw_ref, *refs):
        if layer == 0:
            proj_ref, gate_ref, outcat_ref, projcat_ref = refs
            projcat_ref[...] = stacked(proj_ref[1].T, 1)
        else:
            gate_ref, outcat_ref = refs
        outcat_ref[...] = stacked(outw_ref[layer].T, 1)
        cat = stacked(gatew_ref[layer].T, 1)

        def step(t, carry):
            gate_ref[t] = jax.nn.sigmoid(matmul(cat, normalized(state_ref[t]), ((1,), (0,))))
            return carry

        lax.fori_loop(0, PACK, step, 0, unroll=3)

    return body


PAD = 8


def widen(source_ref, wide_ref):
    def step(i, carry):
        wide_ref[aligned(PAD + i * 256, 256, 8), :] = source_ref[aligned(i * 256, 256, 256), :].astype(F32)
        return carry

    lax.fori_loop(0, 18, step, 0, unroll=2)


def unpack(wide_ref, base):
    lane = lanes((8, 128))
    sub = lax.broadcasted_iota(jnp.int32, (8, 128), 0)

    def rows(at):
        return wide_ref[pl.ds(base + at, 8), :]

    third = jnp.where(lane < 64, pltpu.roll(rows(4), 64, 1), pltpu.roll(rows(10), 96, 1))
    third = jnp.where(lane < 32, pltpu.roll(rows(-2), 32, 1), third)
    return rows(0), rows(8), jnp.where(sub < 2, rows(16), third)


def place(wide_ref, base, target_ref, start, column, clear):
    lane = lanes((8, 128))
    for n, part in enumerate(unpack(wide_ref, base)):
        if clear:
            part = jnp.where(lane < COLS, part, 0.0)
        target_ref[aligned(start + 8 * n, 8, 8), column] = part


def tail_slot(half, g):
    return 8 + (half * 8 + g) * 24


def send_tri(tri_ref, mix_ref, tail_ref, ready_ref, out_hbm, sems):
    lane = lanes((8, 128))

    def send(i, carry):
        blocks = [(half, g, (2 * i + half) * 24) for half in range(2) for g in range(8)]
        for half, g, base in blocks:
            slot = tail_slot(half, g)
            value = tri_ref[g, aligned(base + 16, 8, 8), :]
            tail_ref[slot + 10 : slot + 18, :] = pltpu.roll(value, 32, 1)
            tail_ref[slot + 4 : slot + 12, :] = pltpu.roll(value, 64, 1)
            tail_ref[slot - 2 : slot + 6, :] = pltpu.roll(value, 96, 1)
        for half, g, base in blocks:
            slot = tail_slot(half, g)
            target = ((2 * i + half) * 8 + g) * PACK
            for n in range(3):
                tail = tail_ref[slot + 8 * n : slot + 8 * n + 8, :]
                value = jnp.where(lane < COLS, tri_ref[g, aligned(base + 8 * n, 8, 8), :], tail)
                if n < 2:
                    mix_ref[pl.ds(target + 8 * n, 8), :] = value
                else:
                    mix_ref[pl.ds(target + 16, 2), :] = value[0:2]
        at = aligned(i * 288, 288, 288)
        ready_ref[at, :] = mix_ref[at, :].astype(BF16)
        return carry

    copies = []
    for n in range(4):
        lax.fori_loop(2 * n, 2 * n + 2, send, 0)
        at = pl.ds(576 * n, 576)
        copies.append(pltpu.make_async_copy(ready_ref.at[at], out_hbm.at[at], sems.at[n]))
        copies[-1].start()
    for copy in copies:
        copy.wait()


def outgoing_own(own_ref, left_ref, *refs):
    right_refs, (wide_ref, keep_ref) = refs[:4], refs[4:]
    core = lax.axis_index("core")
    widen(own_ref, wide_ref)
    for n, right_ref in enumerate(right_refs):
        for z in range(2):
            right_ref[128 * z + 96 : 128 * z + 128, :] = jnp.zeros((32, 1024), F32)

        def step(c, carry):
            b = 4 * n + c
            start = (c // 2) * 128 + (c % 2) * 48 + core * 24
            for g in range(8):
                at = slice(128 * g, 128 * g + 128)
                message = PAD + (b * 8 + g) * 2 * PACK
                place(wide_ref, message, keep_ref, b * 24, at, False)
                place(wide_ref, message + PACK, right_ref, start, at, True)
            return carry

        lax.fori_loop(0, 4, step, 0, unroll=2)
    left_ref[...] = keep_ref[...].astype(BF16)


def outgoing_kernel(left_ref, _0, _1, _2, _3, other_ref, out_hbm, *refs):
    right_refs, (wide_ref, tri_ref, *scratch) = refs[:4], refs[4:]
    core = lax.axis_index("core")
    widen(other_ref, wide_ref)
    left = left_ref[...]

    def fill(n):
        for c in range(4):
            for g in range(8):
                message = PAD + ((4 * n + c) * 8 + g) * 2 * PACK
                start = (c // 2) * 128 + (c % 2) * 48 + 24 - core * 24
                place(wide_ref, message + PACK, right_refs[n], start, slice(128 * g, 128 * g + 128), True)

    fill(0)
    for n in range(4):
        tri = matmul(left, right_refs[n][...].astype(BF16), ((1,), (1,)))
        if n < 3:
            fill(n + 1)
        tri_ref[2 * n] = tri[:, 0:128]
        tri_ref[2 * n + 1] = tri[:, 128:256]
    mix_ref, tail_ref, ready_ref, sems = scratch
    send_tri(tri_ref, mix_ref, tail_ref, ready_ref, out_hbm, sems)


def incoming_half(source_ref, wide_ref, left_ref, right_ref, turn_ref, turned_ref):
    core = lax.axis_index("core")
    widen(source_ref, wide_ref)
    lane = lanes((8, 128))
    keep = lax.broadcasted_iota(jnp.int32, (8, 128), 0) < 6

    def step(b, carry):
        at = aligned(8 * b, 8, 8)
        for g in range(8):
            column = slice(128 * g, 128 * g + 128)
            message = PAD + (b * 8 + g) * 2 * PACK
            for p in range(3):
                left_ref[g, p, at, :] = wide_ref[pl.ds(message + 6 * p, 8), :]
            right = [wide_ref[pl.ds(message + PACK + 6 * p, 8), :] for p in range(3)]
            tail = jnp.where(lane < 64, pltpu.roll(right[1], 64, 1), pltpu.roll(right[2], 96, 1))
            right.append(jnp.where(lane < 32, pltpu.roll(right[0], 32, 1), tail))
            for p in range(4):
                right_ref[p, at, column] = jnp.where(keep, right[p], 0.0)
        return carry

    lax.fori_loop(0, 16, step, 0, unroll=2)
    for z in range(8):
        slot = z % 2
        for p in range(3):
            turned = left_ref[z, p].T
            turn_ref[slot, p] = turned
            turn_ref[slot, 3, 32 * p : 32 * p + 32, :] = turned[COLS:]
        for y in range(2):
            rows = slice(48 * z + 24 * y, 48 * z + 24 * y + 24)
            for p in range(4):
                turned_ref[rows, 128 * p : 128 * p + 128] = turn_ref[slot, p, aligned(48 * y + 24 * core, 24, 8), :]
    left = turned_ref[...].astype(BF16)
    for n in range(4):
        right = right_ref[:, :, 256 * n : 256 * n + 256].reshape(512, 256).astype(BF16)
        tri = matmul(left, right, ((1,), (0,)))
        yield 2 * n, tri[:, 0:128]
        yield 2 * n + 1, tri[:, 128:256]


def incoming_own(own_ref, part_ref, *scratch):
    for g, tri in incoming_half(own_ref, *scratch):
        part_ref[g] = tri


def incoming_kernel(part_ref, other_ref, out_hbm, wide_ref, left_ref, right_ref, turn_ref, turned_ref, tri_ref,
                    mix_ref, tail_ref, ready_ref, sems):
    for g, tri in incoming_half(other_ref, wide_ref, left_ref, right_ref, turn_ref, turned_ref):
        tri_ref[g] = part_ref[g] + tri
    send_tri(tri_ref, mix_ref, tail_ref, ready_ref, out_hbm, sems)


def finish(tri_ref, state_ref, gate_hbm, outcat_hbm, scaled_ref, stat_ref, gate_ref, outcat_ref, fetch_sems, after=()):
    fetches = [
        pltpu.make_async_copy(outcat_hbm, outcat_ref, fetch_sems.at[0]),
        pltpu.make_async_copy(gate_hbm, gate_ref, fetch_sems.at[1]),
    ]
    for fetch in fetches + list(after):
        fetch.start()

    def stats(i, carry):
        total, square = carry
        at = aligned(i * 144, 144, 144)
        t = tri_ref[at, :].astype(F32)
        scaled_ref[at, :] = t
        first, second = t[0:72], t[72:144]
        return total + first + second, square + first * first + second * second

    zero = jnp.zeros((72, 128), F32)
    total, square = lax.fori_loop(0, 16, stats, (zero, zero), unroll=2)
    stat_ref[0, 0:72, :] = total
    stat_ref[1, 0:72, :] = square

    def gather(n):
        return sum(stat_ref[n, 18 * q : 18 * q + 18, :] for q in range(4)) * (1.0 / CH)

    average = gather(0)
    scale = lax.rsqrt(gather(1) - average * average + EPS)
    stat_ref[0, 0:18, :] = average
    stat_ref[1, 0:18, :] = scale
    for fetch in fetches:
        fetch.wait()
    w_cat = outcat_ref[...]

    def updated(i):
        pieces = []
        for half in range(2):
            t = 2 * i + half
            centred = scaled_ref[pl.ds(t, CH, stride=PACK), :] - stat_ref[0, pl.ds(t, 1), :]
            pieces.append(split_bf16(centred * stat_ref[1, pl.ds(t, 1), :]))
        high = jnp.concatenate([pieces[0][0], pieces[1][0]], axis=1)
        low = jnp.concatenate([pieces[0][1], pieces[1][1]], axis=1)
        values = matmul(w_cat, jnp.concatenate([high, high, low], axis=0), ((1,), (0,)))
        for half in range(2):
            t = 2 * i + half
            yield state_ref[t] + gate_ref[t] * values[:, 128 * half : 128 * half + 128]

    return updated


def middle_kernel(edge_ref, tri_ref, state_ref, gate_hbm, outcat_hbm, projcat_hbm, next_ref, send_ref,
                  projcat_ref, sems, mix_ref, *scratch):
    fetch = pltpu.make_async_copy(projcat_hbm, projcat_ref, sems.at[0])
    updated = finish(tri_ref, state_ref, gate_hbm, outcat_hbm, *scratch, after=(fetch,))
    fetch.wait()

    def source(i):
        for half, value in enumerate(updated(i)):
            next_ref[2 * i + half] = value
            yield value

    project(source, projcat_ref[...], edge_ref, mix_ref, send_ref)


def last_kernel(tri_ref, state_ref, gate_hbm, outcat_hbm, out_hbm, next_ref, sems, *scratch):
    updated = finish(tri_ref, state_ref, gate_hbm, outcat_hbm, *scratch)
    copies = []

    def done(n):
        at = pl.ds(n * PIX // 4, PIX // 4)
        copies.append(pltpu.make_async_copy(next_ref.at[at], out_hbm.at[at], sems.at[n]))
        copies[-1].start()

    for i in range(PACK // 2):
        for half, value in enumerate(updated(i)):
            t = 2 * i + half
            value = value.T
            next_ref[t * COLS : t * COLS + COLS, :] = value[:COLS]
            next_ref[tail_pixels(t), :] = value[COLS:]
        if i % 3 == 2:
            done(i // 3)
    done(3)
    for copy in copies:
        copy.wait()


VM = pl.BlockSpec(memory_space=pltpu.VMEM)
SM = pl.BlockSpec(memory_space=pltpu.SMEM)
HB = pl.BlockSpec(memory_space=pltpu.HBM)
STATE = pltpu.VMEM((PACK, CH, 128), F32)
SEND = pltpu.VMEM((CH * 2 * PACK, 128), BF16)
TRI = pltpu.HBM((CH * PACK, 128), BF16)
GATE = pltpu.HBM((PACK, CH, 128), F32)
EDGE = pltpu.VMEM((PACK, 128), F32)
OUTCAT = pltpu.HBM((CH, 3 * CH), BF16)
PROJCAT = pltpu.HBM((4 * CH, 3 * CH), BF16)
PROJECT_SCRATCH = [pltpu.VMEM((CH * 2 * PACK, 128), F32)]
FINISH_SCRATCH = [
    pltpu.VMEM((CH * PACK, 128), F32), pltpu.VMEM((2, 72, 128), F32), pltpu.VMEM((PACK, CH, 128), F32),
    pltpu.VMEM((CH, 3 * CH), BF16), pltpu.SemaphoreType.DMA((2,)),
]
SEND_SCRATCH = [
    pltpu.VMEM((8, 384, 128), F32), pltpu.VMEM((CH * PACK, 128), F32), pltpu.VMEM((400, 128), F32),
    pltpu.VMEM((CH * PACK, 128), BF16), pltpu.SemaphoreType.DMA((4,)),
]
WIDE = pltpu.VMEM((CH * 2 * PACK + 16, 128), F32)
HALF = pltpu.VMEM((384, 1024), F32)
RIGHT = (pltpu.VMEM((256, 1024), F32),) * 4
HALF_SCRATCH = [
    WIDE, pltpu.VMEM((8, 3, 128, 128), F32), pltpu.VMEM((4, 128, 1024), F32), pltpu.VMEM((2, 4, 128, 128), F32),
    pltpu.VMEM((384, 512), F32),
]
PART = pltpu.VMEM((8, 384, 128), F32)


def call(kernel, out_shape, operands, scratch=(), specs=None, out_specs=None, mib=16, **options):
    outs = out_shape if isinstance(out_shape, tuple) else None
    return pl.pallas_call(
        kernel,
        out_shape=out_shape,
        in_specs=specs or [VM] * len(operands),
        out_specs=out_specs or (VM if outs is None else (VM,) * len(outs)),
        scratch_shapes=list(scratch),
        compiler_params=pltpu.CompilerParams(vmem_limit_bytes=mib * 1024 * 1024),
        **options,
    )(*operands)


def near(value):
    return pltpu.with_memory_space_constraint(value, pltpu.VMEM)


def far(value):
    return pltpu.with_memory_space_constraint(value, pltpu.HBM)


def exchange(message, rows):
    moved = lax.all_to_all(message.reshape(CH, rows // 2, 2, 128), CHIPS, split_axis=0, concat_axis=0, tiled=True)
    return moved.reshape(CH * rows, 128)


def partner(value):
    return lax.ppermute(value, "core", [(0, 1), (1, 0)])


def gating(layer, outs, *operands):
    cost = pl.CostEstimate(flops=3 * 2 * PIX * CH * CH, transcendentals=PIX * CH, bytes_accessed=8 * PIX * CH)
    return call(gate_kernel(layer), outs, operands, cost_estimate=cost)


def on_device(pair, residue_mask, hotspot, interface, proj_weight, gate_weight, out_weight):
    send, edge, state = call(
        first_kernel, (SEND, EDGE, STATE),
        (far(residue_mask), far(hotspot), far(interface), far(pair.reshape(PIX, CH)), far(proj_weight)),
        [pltpu.SMEM((768,), jnp.int32), pltpu.SMEM((768,), jnp.int32), pltpu.VMEM((ROWS, COLS), jnp.int32),
         pltpu.VMEM((ROWS, 128), jnp.int32), pltpu.VMEM((PIX, CH), F32), pltpu.VMEM((CH, 4 * CH), F32),
         pltpu.SemaphoreType.DMA((5,))] + PROJECT_SCRATCH,
        [HB] * 5,
    )
    own = exchange(send, 2 * PACK)
    other = partner(own)
    left, *right = call(outgoing_own, (pltpu.VMEM((384, 1024), BF16),) + RIGHT, (near(own),), [WIDE, HALF])
    tri, *_ = call(
        outgoing_kernel, (TRI,) + RIGHT, (near(left), *map(near, right), near(other)), [WIDE] + SEND_SCRATCH,
        out_specs=(HB, VM, VM, VM, VM), input_output_aliases={1: 1, 2: 2, 3: 3, 4: 4},
    )
    tri = exchange(tri, PACK)
    gate, outcat, projcat = gating(0, (GATE, OUTCAT, PROJCAT), near(state), gate_weight, out_weight, proj_weight)
    state, send = call(
        middle_kernel, (STATE, SEND),
        (near(edge), near(tri), near(state), far(gate), far(outcat), far(projcat)),
        [pltpu.VMEM((4 * CH, 3 * CH), BF16), pltpu.SemaphoreType.DMA((1,))] + PROJECT_SCRATCH + FINISH_SCRATCH,
        [VM, VM, VM, HB, HB, HB],
    )
    own = exchange(send, 2 * PACK)
    other = partner(own)
    part = call(incoming_own, PART, (near(own),), HALF_SCRATCH)
    tri = call(incoming_kernel, TRI, (near(part), near(other)), HALF_SCRATCH + SEND_SCRATCH, out_specs=HB)
    tri = exchange(tri, PACK)
    gate, outcat = gating(1, (GATE, OUTCAT), near(state), gate_weight, out_weight)
    state = call(
        last_kernel, jax.ShapeDtypeStruct((PIX, CH), F32), (near(tri), near(state), far(gate), far(outcat)),
        [pltpu.VMEM((PIX, CH), F32), pltpu.SemaphoreType.DMA((4,))] + FINISH_SCRATCH, [VM, VM, HB, HB], out_specs=HB,
    )
    return state.reshape(ROWS, COLS, CH)


def solution(mesh):
    grid = Mesh(mesh.devices.reshape(8, 2, 2, 4, 2), ("z", "yl", "core", "x", "yh"))
    rows = ("z", "yl", "core")
    cols = ("x", "yh")
    return jax.shard_map(
        on_device,
        mesh=grid,
        in_specs=(P(rows, cols, None), P(), P(), P(rows, cols), P(), P(), P()),
        out_specs=P(rows, cols, None),
        check_vma=False,
    )
```

```python
import jax
import jax.numpy as jnp
from jax import lax
from jax.experimental import pallas as pl
from jax.experimental.pallas import tpu as pltpu
from jax.sharding import Mesh, PartitionSpec as P

EPS = 1e-05
F32 = jnp.float32
BF16 = jnp.bfloat16
ROWS = 24
COLS = 96
PIX = ROWS * COLS
CH = 128
PACK = 18
CHIPS = ("z", "yl", "x", "yh")


def split_bf16(value):
    high = value.astype(BF16)
    low = (value - high.astype(F32)).astype(BF16)
    return high, low


def lanes(shape):
    return lax.broadcasted_iota(jnp.int32, shape, len(shape) - 1)


def matmul(a, b, dims):
    return lax.dot_general(a, b, (dims, ((), ())), preferred_element_type=F32)


def stacked(weight, axis):
    high, low = split_bf16(weight)
    return jnp.concatenate([high, low, high], axis=axis)


def aligned(start, size, unit):
    return pl.ds(pl.multiple_of(start, unit), size)


def packed_edge(mask_sm, hot_sm, inter_ref, edge_ref, rows_ref):
    band = (lax.axis_index("z") * 2 + lax.axis_index("yl")) * 2 + lax.axis_index("core")
    hid = lax.axis_index("x") * 2 + lax.axis_index("yh")
    lane = lanes((1, 128))
    col_mask = jnp.zeros((1, 128), jnp.int32)
    col_hot = jnp.zeros((1, 128), jnp.int32)
    for c in range(COLS):
        col_mask = jnp.where(lane == c, mask_sm[hid * COLS + c], col_mask)
        col_hot = jnp.where(lane == c, hot_sm[hid * COLS + c], col_hot)
    rows_ref[...] = jnp.zeros((ROWS, 128), jnp.int32)
    rows_ref[:, 0:COLS] = inter_ref[...]
    for r in range(ROWS):
        at = slice(r, r + 1)
        flags = jnp.maximum(rows_ref[at, :], jnp.maximum(col_hot, hot_sm[band * ROWS + r]))
        rows_ref[at, :] = flags * col_mask * mask_sm[band * ROWS + r]
    for t in range(PACK):
        tail = pltpu.roll(jnp.broadcast_to(rows_ref[18 + t % 6 : 19 + t % 6, :], (8, 128)), 96 - 32 * (t // 6), 1)
        edge_ref[t : t + 1, :] = jnp.where(lane < COLS, rows_ref[t : t + 1, :], tail[0:1, :]).astype(F32)


def tail_pixels(t):
    return aligned((18 + t % 6) * COLS + 32 * (t // 6), 32, 32)


def normalized(x):
    centred = x - jnp.mean(x, axis=0, keepdims=True)
    variance = jnp.mean(centred * centred, axis=0, keepdims=True)
    high, low = split_bf16(centred * lax.rsqrt(variance + EPS))
    return jnp.concatenate([high, high, low], axis=0)


def project(source, w_cat, edge_ref, mix_ref, send_ref):
    def group(i, carry):
        values = matmul(w_cat, jnp.concatenate([normalized(x) for x in source(i)], axis=1), ((1,), (0,)))
        for half in range(2):
            t = 2 * i + half
            part = values[:, 128 * half : 128 * half + 128]
            edge = edge_ref[pl.ds(t, 1), :]
            left = edge * jax.nn.sigmoid(part[CH : 2 * CH]) * part[:CH]
            right = edge * jax.nn.sigmoid(part[3 * CH :]) * part[2 * CH : 3 * CH]
            mix_ref[pl.ds(t, CH, stride=2 * PACK), :] = left
            mix_ref[pl.ds(t + PACK, CH, stride=2 * PACK), :] = right
        return carry

    lax.fori_loop(0, PACK // 2, group, 0, unroll=True)

    def convert(i, carry):
        at = aligned(i * 256, 256, 256)
        send_ref[at, :] = mix_ref[at, :].astype(BF16)
        return carry

    lax.fori_loop(0, 18, convert, 0, unroll=2)


def first_kernel(mask_hbm, hot_hbm, inter_hbm, pair_hbm, proj_hbm, send_ref, edge_ref, state_ref, mask_sm, hot_sm,
                 inter_ref, rows_ref, pair_ref, proj_ref, sems, mix_ref):
    copies = [
        pltpu.make_async_copy(source, target, sems.at[n])
        for n, (source, target) in enumerate((
            (mask_hbm, mask_sm), (hot_hbm, hot_sm), (inter_hbm, inter_ref), (proj_hbm.at[0], proj_ref),
            (pair_hbm, pair_ref),
        ))
    ]
    for copy in copies:
        copy.start()
    for copy in copies[:3]:
        copy.wait()
    packed_edge(mask_sm, hot_sm, inter_ref, edge_ref, rows_ref)
    copies[3].wait()
    w_cat = stacked(proj_ref[...].T, 1)
    copies[4].wait()

    def source(i):
        for half in range(2):
            t = 2 * i + half
            rows = (pair_ref[aligned(t * COLS, COLS, COLS), :], pair_ref[tail_pixels(t), :])
            x = jnp.concatenate(rows, axis=0).T
            state_ref[t] = x
            yield x

    project(source, w_cat, edge_ref, mix_ref, send_ref)


def gate_kernel(layer):
    def body(state_ref, gatew_ref, outw_ref, *refs):
        if layer == 0:
            proj_ref, gate_ref, outcat_ref, projcat_ref = refs
            projcat_ref[...] = stacked(proj_ref[1].T, 1)
        else:
            gate_ref, outcat_ref = refs
        outcat_ref[...] = stacked(outw_ref[layer].T, 1)
        cat = stacked(gatew_ref[layer].T, 1)

        def step(t, carry):
            gate_ref[t] = jax.nn.sigmoid(matmul(cat, normalized(state_ref[t]), ((1,), (0,))))
            return carry

        lax.fori_loop(0, PACK, step, 0, unroll=3)

    return body


PAD = 8


def widen(source_ref, wide_ref):
    def step(i, carry):
        wide_ref[aligned(PAD + i * 256, 256, 8), :] = source_ref[aligned(i * 256, 256, 256), :].astype(F32)
        return carry

    lax.fori_loop(0, 18, step, 0, unroll=2)


def unpack(wide_ref, base):
    lane = lanes((8, 128))
    sub = lax.broadcasted_iota(jnp.int32, (8, 128), 0)

    def rows(at):
        return wide_ref[pl.ds(base + at, 8), :]

    third = jnp.where(lane < 64, pltpu.roll(rows(4), 64, 1), pltpu.roll(rows(10), 96, 1))
    third = jnp.where(lane < 32, pltpu.roll(rows(-2), 32, 1), third)
    return rows(0), rows(8), jnp.where(sub < 2, rows(16), third)


def place(wide_ref, base, target_ref, start, column, clear):
    lane = lanes((8, 128))
    for n, part in enumerate(unpack(wide_ref, base)):
        if clear:
            part = jnp.where(lane < COLS, part, 0.0)
        target_ref[aligned(start + 8 * n, 8, 8), column] = part


def tail_slot(half, g):
    return 8 + (half * 8 + g) * 24


def send_tri(tri_ref, mix_ref, tail_ref, ready_ref, out_hbm, sems):
    lane = lanes((8, 128))

    def send(i, carry):
        blocks = [(half, g, (2 * i + half) * 24) for half in range(2) for g in range(8)]
        for half, g, base in blocks:
            slot = tail_slot(half, g)
            value = tri_ref[g, aligned(base + 16, 8, 8), :]
            tail_ref[slot + 10 : slot + 18, :] = pltpu.roll(value, 32, 1)
            tail_ref[slot + 4 : slot + 12, :] = pltpu.roll(value, 64, 1)
            tail_ref[slot - 2 : slot + 6, :] = pltpu.roll(value, 96, 1)
        for half, g, base in blocks:
            slot = tail_slot(half, g)
            target = ((2 * i + half) * 8 + g) * PACK
            for n in range(3):
                tail = tail_ref[slot + 8 * n : slot + 8 * n + 8, :]
                value = jnp.where(lane < COLS, tri_ref[g, aligned(base + 8 * n, 8, 8), :], tail)
                if n < 2:
                    mix_ref[pl.ds(target + 8 * n, 8), :] = value
                else:
                    mix_ref[pl.ds(target + 16, 2), :] = value[0:2]
        at = aligned(i * 288, 288, 288)
        ready_ref[at, :] = mix_ref[at, :].astype(BF16)
        return carry

    copies = []
    for n in range(4):
        lax.fori_loop(2 * n, 2 * n + 2, send, 0)
        at = pl.ds(576 * n, 576)
        copies.append(pltpu.make_async_copy(ready_ref.at[at], out_hbm.at[at], sems.at[n]))
        copies[-1].start()
    for copy in copies:
        copy.wait()


def outgoing_own(own_ref, left_ref, *refs):
    right_refs, (wide_ref, keep_ref) = refs[:4], refs[4:]
    core = lax.axis_index("core")
    widen(own_ref, wide_ref)
    for n, right_ref in enumerate(right_refs):
        for z in range(2):
            right_ref[128 * z + 96 : 128 * z + 128, :] = jnp.zeros((32, 1024), F32)

        def step(c, carry):
            b = 4 * n + c
            start = (c // 2) * 128 + (c % 2) * 48 + core * 24
            for g in range(8):
                at = slice(128 * g, 128 * g + 128)
                message = PAD + (b * 8 + g) * 2 * PACK
                place(wide_ref, message, keep_ref, b * 24, at, False)
                place(wide_ref, message + PACK, right_ref, start, at, True)
            return carry

        lax.fori_loop(0, 4, step, 0, unroll=2)
    left_ref[...] = keep_ref[...].astype(BF16)


def outgoing_kernel(left_ref, _0, _1, _2, _3, other_ref, out_hbm, *refs):
    right_refs, (wide_ref, tri_ref, *scratch) = refs[:4], refs[4:]
    core = lax.axis_index("core")
    widen(other_ref, wide_ref)
    left = left_ref[...]

    def fill(n):
        for c in range(4):
            for g in range(8):
                message = PAD + ((4 * n + c) * 8 + g) * 2 * PACK
                start = (c // 2) * 128 + (c % 2) * 48 + 24 - core * 24
                place(wide_ref, message + PACK, right_refs[n], start, slice(128 * g, 128 * g + 128), True)

    fill(0)
    for n in range(4):
        tri = matmul(left, right_refs[n][...].astype(BF16), ((1,), (1,)))
        if n < 3:
            fill(n + 1)
        tri_ref[2 * n] = tri[:, 0:128]
        tri_ref[2 * n + 1] = tri[:, 128:256]
    mix_ref, tail_ref, ready_ref, sems = scratch
    send_tri(tri_ref, mix_ref, tail_ref, ready_ref, out_hbm, sems)


def incoming_half(source_ref, wide_ref, left_ref, right_ref, turn_ref, turned_ref):
    core = lax.axis_index("core")
    widen(source_ref, wide_ref)
    lane = lanes((8, 128))
    keep = lax.broadcasted_iota(jnp.int32, (8, 128), 0) < 6

    def step(b, carry):
        at = aligned(8 * b, 8, 8)
        for g in range(8):
            column = slice(128 * g, 128 * g + 128)
            message = PAD + (b * 8 + g) * 2 * PACK
            for p in range(3):
                left_ref[g, p, at, :] = wide_ref[pl.ds(message + 6 * p, 8), :]
            right = [wide_ref[pl.ds(message + PACK + 6 * p, 8), :] for p in range(3)]
            tail = jnp.where(lane < 64, pltpu.roll(right[1], 64, 1), pltpu.roll(right[2], 96, 1))
            right.append(jnp.where(lane < 32, pltpu.roll(right[0], 32, 1), tail))
            for p in range(4):
                right_ref[p, at, column] = jnp.where(keep, right[p], 0.0)
        return carry

    lax.fori_loop(0, 16, step, 0, unroll=2)
    for z in range(8):
        slot = z % 2
        for p in range(3):
            turned = left_ref[z, p].T
            turn_ref[slot, p] = turned
            turn_ref[slot, 3, 32 * p : 32 * p + 32, :] = turned[COLS:]
        for y in range(2):
            rows = slice(48 * z + 24 * y, 48 * z + 24 * y + 24)
            for p in range(4):
                turned_ref[rows, 128 * p : 128 * p + 128] = turn_ref[slot, p, aligned(48 * y + 24 * core, 24, 8), :]
    left = turned_ref[...].astype(BF16)
    for n in range(4):
        right = right_ref[:, :, 256 * n : 256 * n + 256].reshape(512, 256).astype(BF16)
        tri = matmul(left, right, ((1,), (0,)))
        yield 2 * n, tri[:, 0:128]
        yield 2 * n + 1, tri[:, 128:256]


def incoming_own(own_ref, part_ref, *scratch):
    for g, tri in incoming_half(own_ref, *scratch):
        part_ref[g] = tri


def incoming_kernel(part_ref, other_ref, out_hbm, wide_ref, left_ref, right_ref, turn_ref, turned_ref, tri_ref,
                    mix_ref, tail_ref, ready_ref, sems):
    for g, tri in incoming_half(other_ref, wide_ref, left_ref, right_ref, turn_ref, turned_ref):
        tri_ref[g] = part_ref[g] + tri
    send_tri(tri_ref, mix_ref, tail_ref, ready_ref, out_hbm, sems)


def finish(tri_ref, state_ref, gate_ref, outcat_hbm, scaled_ref, stat_ref, outcat_ref, fetch_sems, gate_hbm=None, after=()):
    fetches = [pltpu.make_async_copy(outcat_hbm, outcat_ref, fetch_sems.at[3])]
    for n in range(0 if gate_hbm is None else 3):
        at = pl.ds(6 * n, 6)
        fetches.append(pltpu.make_async_copy(gate_hbm.at[at], gate_ref.at[at], fetch_sems.at[n]))
    for fetch in fetches + list(after):
        fetch.start()

    def stats(i, carry):
        total, square = carry
        at = aligned(i * 144, 144, 144)
        t = tri_ref[at, :].astype(F32)
        scaled_ref[at, :] = t
        first, second = t[0:72], t[72:144]
        return total + first + second, square + first * first + second * second

    zero = jnp.zeros((72, 128), F32)
    total, square = lax.fori_loop(0, 16, stats, (zero, zero), unroll=2)
    stat_ref[0, 0:72, :] = total
    stat_ref[1, 0:72, :] = square

    def gather(n):
        return sum(stat_ref[n, 18 * q : 18 * q + 18, :] for q in range(4)) * (1.0 / CH)

    average = gather(0)
    scale = lax.rsqrt(gather(1) - average * average + EPS)
    stat_ref[0, 0:18, :] = average
    stat_ref[1, 0:18, :] = scale
    fetches[0].wait()
    w_cat = outcat_ref[...]

    def updated(i):
        pieces = []
        for half in range(2):
            t = 2 * i + half
            centred = scaled_ref[pl.ds(t, CH, stride=PACK), :] - stat_ref[0, pl.ds(t, 1), :]
            pieces.append(split_bf16(centred * stat_ref[1, pl.ds(t, 1), :]))
        high = jnp.concatenate([pieces[0][0], pieces[1][0]], axis=1)
        low = jnp.concatenate([pieces[0][1], pieces[1][1]], axis=1)
        values = matmul(w_cat, jnp.concatenate([high, high, low], axis=0), ((1,), (0,)))
        for half in range(2):
            t = 2 * i + half
            yield state_ref[t] + gate_ref[t] * values[:, 128 * half : 128 * half + 128]

    return updated, fetches[1:]


def middle_kernel(edge_ref, tri_ref, state_ref, gate_hbm, outcat_hbm, projcat_hbm, next_ref, send_ref,
                  projcat_ref, sems, mix_ref, gate_ref, *scratch):
    fetch = pltpu.make_async_copy(projcat_hbm, projcat_ref, sems.at[0])
    updated, parts = finish(tri_ref, state_ref, gate_ref, outcat_hbm, *scratch, gate_hbm=gate_hbm, after=(fetch,))

    def combine(i, carry):
        for half, value in enumerate(updated(i)):
            next_ref[2 * i + half] = value
        return carry

    for n, part in enumerate(parts):
        part.wait()
        lax.fori_loop(3 * n, 3 * n + 3, combine, 0, unroll=True)
    fetch.wait()
    project(lambda i: (next_ref[2 * i], next_ref[2 * i + 1]), projcat_ref[...], edge_ref, mix_ref, send_ref)


def last_kernel(tri_ref, state_ref, gate_ref, outcat_hbm, out_hbm, next_ref, sems, *scratch):
    updated, _ = finish(tri_ref, state_ref, gate_ref, outcat_hbm, *scratch)
    copies = []

    def done(n):
        at = pl.ds(n * PIX // 4, PIX // 4)
        copies.append(pltpu.make_async_copy(next_ref.at[at], out_hbm.at[at], sems.at[n]))
        copies[-1].start()

    for i in range(PACK // 2):
        for half, value in enumerate(updated(i)):
            t = 2 * i + half
            value = value.T
            next_ref[t * COLS : t * COLS + COLS, :] = value[:COLS]
            next_ref[tail_pixels(t), :] = value[COLS:]
        if i % 3 == 2:
            done(i // 3)
    done(3)
    for copy in copies:
        copy.wait()


VM = pl.BlockSpec(memory_space=pltpu.VMEM)
SM = pl.BlockSpec(memory_space=pltpu.SMEM)
HB = pl.BlockSpec(memory_space=pltpu.HBM)
STATE = pltpu.VMEM((PACK, CH, 128), F32)
SEND = pltpu.VMEM((CH * 2 * PACK, 128), BF16)
TRI = pltpu.HBM((CH * PACK, 128), BF16)
GATE = pltpu.HBM((PACK, CH, 128), F32)
EDGE = pltpu.VMEM((PACK, 128), F32)
OUTCAT = pltpu.HBM((CH, 3 * CH), BF16)
PROJCAT = pltpu.HBM((4 * CH, 3 * CH), BF16)
PROJECT_SCRATCH = [pltpu.VMEM((CH * 2 * PACK, 128), F32)]
FINISH_SCRATCH = [
    pltpu.VMEM((CH * PACK, 128), F32), pltpu.VMEM((2, 72, 128), F32), pltpu.VMEM((CH, 3 * CH), BF16),
    pltpu.SemaphoreType.DMA((4,)),
]
SEND_SCRATCH = [
    pltpu.VMEM((8, 384, 128), F32), pltpu.VMEM((CH * PACK, 128), F32), pltpu.VMEM((400, 128), F32),
    pltpu.VMEM((CH * PACK, 128), BF16), pltpu.SemaphoreType.DMA((4,)),
]
WIDE = pltpu.VMEM((CH * 2 * PACK + 16, 128), F32)
HALF = pltpu.VMEM((384, 1024), F32)
RIGHT = (pltpu.VMEM((256, 1024), F32),) * 4
HALF_SCRATCH = [
    WIDE, pltpu.VMEM((8, 3, 128, 128), F32), pltpu.VMEM((4, 128, 1024), F32), pltpu.VMEM((2, 4, 128, 128), F32),
    pltpu.VMEM((384, 512), F32),
]
PART = pltpu.VMEM((8, 384, 128), F32)


def call(kernel, out_shape, operands, scratch=(), specs=None, out_specs=None, mib=16, **options):
    outs = out_shape if isinstance(out_shape, tuple) else None
    return pl.pallas_call(
        kernel,
        out_shape=out_shape,
        in_specs=specs or [VM] * len(operands),
        out_specs=out_specs or (VM if outs is None else (VM,) * len(outs)),
        scratch_shapes=list(scratch),
        compiler_params=pltpu.CompilerParams(vmem_limit_bytes=mib * 1024 * 1024),
        **options,
    )(*operands)


def near(value):
    return pltpu.with_memory_space_constraint(value, pltpu.VMEM)


def far(value):
    return pltpu.with_memory_space_constraint(value, pltpu.HBM)


def exchange(message, rows):
    moved = lax.all_to_all(message.reshape(CH, rows // 2, 2, 128), CHIPS, split_axis=0, concat_axis=0, tiled=True)
    return moved.reshape(CH * rows, 128)


def partner(value):
    return lax.ppermute(value, "core", [(0, 1), (1, 0)])


def gating(layer, outs, *operands):
    cost = pl.CostEstimate(flops=3 * 2 * PIX * CH * CH, transcendentals=PIX * CH, bytes_accessed=8 * PIX * CH)
    return call(gate_kernel(layer), outs, operands, cost_estimate=cost)


def on_device(pair, residue_mask, hotspot, interface, proj_weight, gate_weight, out_weight):
    send, edge, state = call(
        first_kernel, (SEND, EDGE, STATE),
        (far(residue_mask), far(hotspot), far(interface), far(pair.reshape(PIX, CH)), far(proj_weight)),
        [pltpu.SMEM((768,), jnp.int32), pltpu.SMEM((768,), jnp.int32), pltpu.VMEM((ROWS, COLS), jnp.int32),
         pltpu.VMEM((ROWS, 128), jnp.int32), pltpu.VMEM((PIX, CH), F32), pltpu.VMEM((CH, 4 * CH), F32),
         pltpu.SemaphoreType.DMA((5,))] + PROJECT_SCRATCH,
        [HB] * 5,
    )
    own = exchange(send, 2 * PACK)
    other = partner(own)
    left, *right = call(outgoing_own, (pltpu.VMEM((384, 1024), BF16),) + RIGHT, (near(own),), [WIDE, HALF])
    tri, *_ = call(
        outgoing_kernel, (TRI,) + RIGHT, (near(left), *map(near, right), near(other)), [WIDE] + SEND_SCRATCH,
        out_specs=(HB, VM, VM, VM, VM), input_output_aliases={1: 1, 2: 2, 3: 3, 4: 4},
    )
    tri = exchange(tri, PACK)
    gate, outcat, projcat = gating(0, (GATE, OUTCAT, PROJCAT), near(state), gate_weight, out_weight, proj_weight)
    state, send = call(
        middle_kernel, (STATE, SEND),
        (near(edge), near(tri), near(state), far(gate), far(outcat), far(projcat)),
        [pltpu.VMEM((4 * CH, 3 * CH), BF16), pltpu.SemaphoreType.DMA((1,))] + PROJECT_SCRATCH
        + [pltpu.VMEM((PACK, CH, 128), F32)] + FINISH_SCRATCH,
        [VM, VM, VM, HB, HB, HB],
    )
    own = exchange(send, 2 * PACK)
    other = partner(own)
    part = call(incoming_own, PART, (near(own),), HALF_SCRATCH)
    tri = call(incoming_kernel, TRI, (near(part), near(other)), HALF_SCRATCH + SEND_SCRATCH, out_specs=HB)
    tri = exchange(tri, PACK)
    gate, outcat = gating(1, (STATE, OUTCAT), near(state), gate_weight, out_weight)
    state = call(
        last_kernel, jax.ShapeDtypeStruct((PIX, CH), F32), (near(tri), near(state), near(gate), far(outcat)),
        [pltpu.VMEM((PIX, CH), F32), pltpu.SemaphoreType.DMA((4,))] + FINISH_SCRATCH, [VM, VM, VM, HB], out_specs=HB,
    )
    return state.reshape(ROWS, COLS, CH)


def solution(mesh):
    grid = Mesh(mesh.devices.reshape(8, 2, 2, 4, 2), ("z", "yl", "core", "x", "yh"))
    rows = ("z", "yl", "core")
    cols = ("x", "yh")
    return jax.shard_map(
        on_device,
        mesh=grid,
        in_specs=(P(rows, cols, None), P(), P(), P(rows, cols), P(), P(), P()),
        out_specs=P(rows, cols, None),
        check_vma=False,
    )
```

```python
import jax
import jax.numpy as jnp
from jax import lax
from jax.experimental import pallas as pl
from jax.experimental.pallas import tpu as pltpu
from jax.sharding import Mesh, PartitionSpec as P

EPS = 1e-05
F32 = jnp.float32
BF16 = jnp.bfloat16
ROWS = 24
COLS = 96
PIX = ROWS * COLS
CH = 128
PACK = 18
CHIPS = ("z", "yl", "x", "yh")


def split_bf16(value):
    high = value.astype(BF16)
    low = (value - high.astype(F32)).astype(BF16)
    return high, low


def lanes(shape):
    return lax.broadcasted_iota(jnp.int32, shape, len(shape) - 1)


def matmul(a, b, dims):
    return lax.dot_general(a, b, (dims, ((), ())), preferred_element_type=F32)


def stacked(weight, axis):
    high, low = split_bf16(weight)
    return jnp.concatenate([high, low, high], axis=axis)


def aligned(start, size, unit):
    return pl.ds(pl.multiple_of(start, unit), size)


def packed_edge(mask_sm, hot_sm, inter_ref, edge_ref, rows_ref):
    band = (lax.axis_index("z") * 2 + lax.axis_index("yl")) * 2 + lax.axis_index("core")
    hid = lax.axis_index("x") * 2 + lax.axis_index("yh")
    lane = lanes((1, 128))
    col_mask = jnp.zeros((1, 128), jnp.int32)
    col_hot = jnp.zeros((1, 128), jnp.int32)
    for c in range(COLS):
        col_mask = jnp.where(lane == c, mask_sm[hid * COLS + c], col_mask)
        col_hot = jnp.where(lane == c, hot_sm[hid * COLS + c], col_hot)
    rows_ref[...] = jnp.zeros((ROWS, 128), jnp.int32)
    rows_ref[:, 0:COLS] = inter_ref[...]
    for r in range(ROWS):
        at = slice(r, r + 1)
        flags = jnp.maximum(rows_ref[at, :], jnp.maximum(col_hot, hot_sm[band * ROWS + r]))
        rows_ref[at, :] = flags * col_mask * mask_sm[band * ROWS + r]
    for t in range(PACK):
        tail = pltpu.roll(jnp.broadcast_to(rows_ref[18 + t % 6 : 19 + t % 6, :], (8, 128)), 96 - 32 * (t // 6), 1)
        edge_ref[t : t + 1, :] = jnp.where(lane < COLS, rows_ref[t : t + 1, :], tail[0:1, :]).astype(F32)


def tail_pixels(t):
    return aligned((18 + t % 6) * COLS + 32 * (t // 6), 32, 32)


def normalized(x):
    centred = x - jnp.mean(x, axis=0, keepdims=True)
    variance = jnp.mean(centred * centred, axis=0, keepdims=True)
    high, low = split_bf16(centred * lax.rsqrt(variance + EPS))
    return jnp.concatenate([high, high, low], axis=0)


def project(source, w_cat, edge_ref, mix_ref, send_ref):
    def group(i, carry):
        values = matmul(w_cat, jnp.concatenate([normalized(x) for x in source(i)], axis=1), ((1,), (0,)))
        for half in range(2):
            t = 2 * i + half
            part = values[:, 128 * half : 128 * half + 128]
            edge = edge_ref[pl.ds(t, 1), :]
            left = edge * jax.nn.sigmoid(part[CH : 2 * CH]) * part[:CH]
            right = edge * jax.nn.sigmoid(part[3 * CH :]) * part[2 * CH : 3 * CH]
            mix_ref[pl.ds(t, CH, stride=2 * PACK), :] = left
            mix_ref[pl.ds(t + PACK, CH, stride=2 * PACK), :] = right
        return carry

    lax.fori_loop(0, PACK // 2, group, 0, unroll=True)

    def convert(i, carry):
        at = aligned(i * 256, 256, 256)
        send_ref[at, :] = mix_ref[at, :].astype(BF16)
        return carry

    lax.fori_loop(0, 18, convert, 0, unroll=2)


def first_kernel(mask_hbm, hot_hbm, inter_hbm, pair_hbm, proj_hbm, send_ref, edge_ref, state_ref, mask_sm, hot_sm,
                 inter_ref, rows_ref, pair_ref, proj_ref, sems, mix_ref):
    copies = [
        pltpu.make_async_copy(source, target, sems.at[n])
        for n, (source, target) in enumerate((
            (mask_hbm, mask_sm), (hot_hbm, hot_sm), (inter_hbm, inter_ref), (proj_hbm.at[0], proj_ref),
            (pair_hbm, pair_ref),
        ))
    ]
    for copy in copies:
        copy.start()
    for copy in copies[:3]:
        copy.wait()
    packed_edge(mask_sm, hot_sm, inter_ref, edge_ref, rows_ref)
    copies[3].wait()
    w_cat = stacked(proj_ref[...].T, 1)
    copies[4].wait()

    def source(i):
        for half in range(2):
            t = 2 * i + half
            rows = (pair_ref[aligned(t * COLS, COLS, COLS), :], pair_ref[tail_pixels(t), :])
            x = jnp.concatenate(rows, axis=0).T
            state_ref[t] = x
            yield x

    project(source, w_cat, edge_ref, mix_ref, send_ref)


def gate_kernel(layer):
    def body(state_ref, gatew_ref, outw_ref, *refs):
        if layer == 0:
            proj_ref, gate_ref, outcat_ref, projcat_ref = refs
            projcat_ref[...] = stacked(proj_ref[1].T, 1)
        else:
            gate_ref, outcat_ref = refs
        outcat_ref[...] = stacked(outw_ref[layer].T, 1)
        cat = stacked(gatew_ref[layer].T, 1)

        def step(t, carry):
            gate_ref[t] = jax.nn.sigmoid(matmul(cat, normalized(state_ref[t]), ((1,), (0,))))
            return carry

        lax.fori_loop(0, PACK, step, 0, unroll=3)

    return body


PAD = 8


def widen(source_ref, wide_ref):
    def step(i, carry):
        wide_ref[aligned(PAD + i * 256, 256, 8), :] = source_ref[aligned(i * 256, 256, 256), :].astype(F32)
        return carry

    lax.fori_loop(0, 18, step, 0, unroll=2)


def unpack(wide_ref, base):
    lane = lanes((8, 128))
    sub = lax.broadcasted_iota(jnp.int32, (8, 128), 0)

    def rows(at):
        return wide_ref[pl.ds(base + at, 8), :]

    third = jnp.where(lane < 64, pltpu.roll(rows(4), 64, 1), pltpu.roll(rows(10), 96, 1))
    third = jnp.where(lane < 32, pltpu.roll(rows(-2), 32, 1), third)
    return rows(0), rows(8), jnp.where(sub < 2, rows(16), third)


def place(wide_ref, base, target_ref, start, column, clear):
    lane = lanes((8, 128))
    for n, part in enumerate(unpack(wide_ref, base)):
        if clear:
            part = jnp.where(lane < COLS, part, 0.0)
        target_ref[aligned(start + 8 * n, 8, 8), column] = part


def turned_pair(first, second, shift):
    both = pltpu.roll(jnp.concatenate([first, second], axis=0).astype(BF16), shift, 1).astype(F32)
    return both[0:8], both[8:16]


def tail_slot(half, g):
    return 8 + (half * 8 + g) * 24


def send_tri(tri_ref, mix_ref, tail_ref, ready_ref, out_hbm, sems):
    lane = lanes((8, 128))

    def send(i, carry):
        blocks = [(half, g, (2 * i + half) * 24) for half in range(2) for g in range(8)]
        for n in range(0, 16, 2):
            slots = [tail_slot(half, g) for half, g, _ in blocks[n : n + 2]]
            pair = [tri_ref[g, aligned(base + 16, 8, 8), :] for _, g, base in blocks[n : n + 2]]
            for shift, start in ((32, 10), (64, 4), (96, -2)):
                for slot, value in zip(slots, turned_pair(*pair, shift)):
                    tail_ref[slot + start : slot + start + 8, :] = value
        for half, g, base in blocks:
            slot = tail_slot(half, g)
            target = ((2 * i + half) * 8 + g) * PACK
            for n in range(3):
                tail = tail_ref[slot + 8 * n : slot + 8 * n + 8, :]
                value = jnp.where(lane < COLS, tri_ref[g, aligned(base + 8 * n, 8, 8), :], tail)
                if n < 2:
                    mix_ref[pl.ds(target + 8 * n, 8), :] = value
                else:
                    mix_ref[pl.ds(target + 16, 2), :] = value[0:2]
        at = aligned(i * 288, 288, 288)
        ready_ref[at, :] = mix_ref[at, :].astype(BF16)
        return carry

    copies = []
    for n in range(4):
        lax.fori_loop(2 * n, 2 * n + 2, send, 0)
        at = pl.ds(576 * n, 576)
        copies.append(pltpu.make_async_copy(ready_ref.at[at], out_hbm.at[at], sems.at[n]))
        copies[-1].start()
    for copy in copies:
        copy.wait()


def outgoing_own(own_ref, left_ref, *refs):
    right_refs, (wide_ref, keep_ref) = refs[:4], refs[4:]
    core = lax.axis_index("core")
    widen(own_ref, wide_ref)
    for n, right_ref in enumerate(right_refs):
        for z in range(2):
            right_ref[128 * z + 96 : 128 * z + 128, :] = jnp.zeros((32, 1024), F32)

        def step(c, carry):
            b = 4 * n + c
            start = (c // 2) * 128 + (c % 2) * 48 + core * 24
            for g in range(8):
                at = slice(128 * g, 128 * g + 128)
                message = PAD + (b * 8 + g) * 2 * PACK
                place(wide_ref, message, keep_ref, b * 24, at, False)
                place(wide_ref, message + PACK, right_ref, start, at, True)
            return carry

        lax.fori_loop(0, 4, step, 0, unroll=2)
    left_ref[...] = keep_ref[...].astype(BF16)


def outgoing_kernel(left_ref, _0, _1, _2, _3, other_ref, out_hbm, *refs):
    right_refs, (wide_ref, tri_ref, *scratch) = refs[:4], refs[4:]
    core = lax.axis_index("core")
    widen(other_ref, wide_ref)
    left = left_ref[...]

    def fill(n):
        for c in range(4):
            for g in range(8):
                message = PAD + ((4 * n + c) * 8 + g) * 2 * PACK
                start = (c // 2) * 128 + (c % 2) * 48 + 24 - core * 24
                place(wide_ref, message + PACK, right_refs[n], start, slice(128 * g, 128 * g + 128), True)

    fill(0)
    for n in range(4):
        tri = matmul(left, right_refs[n][...].astype(BF16), ((1,), (1,)))
        if n < 3:
            fill(n + 1)
        tri_ref[2 * n] = tri[:, 0:128]
        tri_ref[2 * n + 1] = tri[:, 128:256]
    mix_ref, tail_ref, ready_ref, sems = scratch
    send_tri(tri_ref, mix_ref, tail_ref, ready_ref, out_hbm, sems)


def incoming_half(source_ref, wide_ref, left_ref, right_ref, turn_ref, turned_ref):
    core = lax.axis_index("core")
    widen(source_ref, wide_ref)
    lane = lanes((8, 128))
    keep = lax.broadcasted_iota(jnp.int32, (8, 128), 0) < 6

    def step(b, carry):
        at = aligned(8 * b, 8, 8)
        for g in range(0, 8, 2):
            right = []
            for h in range(2):
                message = PAD + (b * 8 + g + h) * 2 * PACK
                for p in range(3):
                    left_ref[g + h, p, at, :] = wide_ref[pl.ds(message + 6 * p, 8), :]
                right.append([wide_ref[pl.ds(message + PACK + 6 * p, 8), :] for p in range(3)])
            moved = [turned_pair(right[0][p], right[1][p], 32 + 32 * p) for p in range(3)]
            for h in range(2):
                column = slice(128 * (g + h), 128 * (g + h) + 128)
                tail = jnp.where(lane < 64, moved[1][h], moved[2][h])
                right[h].append(jnp.where(lane < 32, moved[0][h], tail))
                for p in range(4):
                    right_ref[p, at, column] = jnp.where(keep, right[h][p], 0.0)
        return carry

    lax.fori_loop(0, 16, step, 0, unroll=2)
    for z in range(8):
        slot = z % 2
        for p in range(3):
            turned = left_ref[z, p].astype(BF16).T.astype(F32)
            turn_ref[slot, p] = turned
            turn_ref[slot, 3, 32 * p : 32 * p + 32, :] = turned[COLS:]
        for y in range(2):
            rows = slice(48 * z + 24 * y, 48 * z + 24 * y + 24)
            for p in range(4):
                turned_ref[rows, 128 * p : 128 * p + 128] = turn_ref[slot, p, aligned(48 * y + 24 * core, 24, 8), :]
    left = turned_ref[...].astype(BF16)
    for n in range(4):
        right = right_ref[:, :, 256 * n : 256 * n + 256].reshape(512, 256).astype(BF16)
        tri = matmul(left, right, ((1,), (0,)))
        yield 2 * n, tri[:, 0:128]
        yield 2 * n + 1, tri[:, 128:256]


def incoming_own(own_ref, part_ref, *scratch):
    for g, tri in incoming_half(own_ref, *scratch):
        part_ref[g] = tri


def incoming_kernel(part_ref, other_ref, out_hbm, wide_ref, left_ref, right_ref, turn_ref, turned_ref, tri_ref,
                    mix_ref, tail_ref, ready_ref, sems):
    for g, tri in incoming_half(other_ref, wide_ref, left_ref, right_ref, turn_ref, turned_ref):
        tri_ref[g] = part_ref[g] + tri
    send_tri(tri_ref, mix_ref, tail_ref, ready_ref, out_hbm, sems)


def finish(tri_ref, state_ref, gate_ref, outcat_hbm, scaled_ref, stat_ref, outcat_ref, fetch_sems, gate_hbm=None, after=()):
    fetches = [pltpu.make_async_copy(outcat_hbm, outcat_ref, fetch_sems.at[3])]
    for n in range(0 if gate_hbm is None else 3):
        at = pl.ds(6 * n, 6)
        fetches.append(pltpu.make_async_copy(gate_hbm.at[at], gate_ref.at[at], fetch_sems.at[n]))
    for fetch in fetches + list(after):
        fetch.start()

    def stats(i, carry):
        total, square = carry
        at = aligned(i * 144, 144, 144)
        t = tri_ref[at, :].astype(F32)
        scaled_ref[at, :] = t
        first, second = t[0:72], t[72:144]
        return total + first + second, square + first * first + second * second

    zero = jnp.zeros((72, 128), F32)
    total, square = lax.fori_loop(0, 16, stats, (zero, zero), unroll=2)
    stat_ref[0, 0:72, :] = total
    stat_ref[1, 0:72, :] = square

    def gather(n):
        return sum(stat_ref[n, 18 * q : 18 * q + 18, :] for q in range(4)) * (1.0 / CH)

    average = gather(0)
    scale = lax.rsqrt(gather(1) - average * average + EPS)
    stat_ref[0, 0:18, :] = average
    stat_ref[1, 0:18, :] = scale
    fetches[0].wait()
    w_cat = outcat_ref[...]

    def updated(i):
        pieces = []
        for half in range(2):
            t = 2 * i + half
            centred = scaled_ref[pl.ds(t, CH, stride=PACK), :] - stat_ref[0, pl.ds(t, 1), :]
            pieces.append(split_bf16(centred * stat_ref[1, pl.ds(t, 1), :]))
        high = jnp.concatenate([pieces[0][0], pieces[1][0]], axis=1)
        low = jnp.concatenate([pieces[0][1], pieces[1][1]], axis=1)
        values = matmul(w_cat, jnp.concatenate([high, high, low], axis=0), ((1,), (0,)))
        for half in range(2):
            t = 2 * i + half
            yield state_ref[t] + gate_ref[t] * values[:, 128 * half : 128 * half + 128]

    return updated, fetches[1:]


def middle_kernel(edge_ref, tri_ref, state_ref, gate_hbm, outcat_hbm, projcat_hbm, next_ref, send_ref,
                  projcat_ref, sems, mix_ref, gate_ref, *scratch):
    fetch = pltpu.make_async_copy(projcat_hbm, projcat_ref, sems.at[0])
    updated, parts = finish(tri_ref, state_ref, gate_ref, outcat_hbm, *scratch, gate_hbm=gate_hbm, after=(fetch,))

    def combine(i, carry):
        for half, value in enumerate(updated(i)):
            next_ref[2 * i + half] = value
        return carry

    for n, part in enumerate(parts):
        part.wait()
        lax.fori_loop(3 * n, 3 * n + 3, combine, 0, unroll=True)
    fetch.wait()
    project(lambda i: (next_ref[2 * i], next_ref[2 * i + 1]), projcat_ref[...], edge_ref, mix_ref, send_ref)


def last_kernel(tri_ref, state_ref, gate_ref, outcat_hbm, out_hbm, next_ref, sems, *scratch):
    updated, _ = finish(tri_ref, state_ref, gate_ref, outcat_hbm, *scratch)
    copies = []

    def done(n):
        at = pl.ds(n * PIX // 4, PIX // 4)
        copies.append(pltpu.make_async_copy(next_ref.at[at], out_hbm.at[at], sems.at[n]))
        copies[-1].start()

    for i in range(PACK // 2):
        for half, value in enumerate(updated(i)):
            t = 2 * i + half
            value = value.T
            next_ref[t * COLS : t * COLS + COLS, :] = value[:COLS]
            next_ref[tail_pixels(t), :] = value[COLS:]
        if i % 3 == 2:
            done(i // 3)
    done(3)
    for copy in copies:
        copy.wait()


VM = pl.BlockSpec(memory_space=pltpu.VMEM)
SM = pl.BlockSpec(memory_space=pltpu.SMEM)
HB = pl.BlockSpec(memory_space=pltpu.HBM)
STATE = pltpu.VMEM((PACK, CH, 128), F32)
SEND = pltpu.VMEM((CH * 2 * PACK, 128), BF16)
TRI = pltpu.HBM((CH * PACK, 128), BF16)
GATE = pltpu.HBM((PACK, CH, 128), F32)
EDGE = pltpu.VMEM((PACK, 128), F32)
OUTCAT = pltpu.HBM((CH, 3 * CH), BF16)
PROJCAT = pltpu.HBM((4 * CH, 3 * CH), BF16)
PROJECT_SCRATCH = [pltpu.VMEM((CH * 2 * PACK, 128), F32)]
FINISH_SCRATCH = [
    pltpu.VMEM((CH * PACK, 128), F32), pltpu.VMEM((2, 72, 128), F32), pltpu.VMEM((CH, 3 * CH), BF16),
    pltpu.SemaphoreType.DMA((4,)),
]
SEND_SCRATCH = [
    pltpu.VMEM((8, 384, 128), F32), pltpu.VMEM((CH * PACK, 128), F32), pltpu.VMEM((400, 128), F32),
    pltpu.VMEM((CH * PACK, 128), BF16), pltpu.SemaphoreType.DMA((4,)),
]
WIDE = pltpu.VMEM((CH * 2 * PACK + 16, 128), F32)
HALF = pltpu.VMEM((384, 1024), F32)
RIGHT = (pltpu.VMEM((256, 1024), F32),) * 4
HALF_SCRATCH = [
    WIDE, pltpu.VMEM((8, 3, 128, 128), F32), pltpu.VMEM((4, 128, 1024), F32), pltpu.VMEM((2, 4, 128, 128), F32),
    pltpu.VMEM((384, 512), F32),
]
PART = pltpu.VMEM((8, 384, 128), F32)


def call(kernel, out_shape, operands, scratch=(), specs=None, out_specs=None, mib=16, **options):
    outs = out_shape if isinstance(out_shape, tuple) else None
    return pl.pallas_call(
        kernel,
        out_shape=out_shape,
        in_specs=specs or [VM] * len(operands),
        out_specs=out_specs or (VM if outs is None else (VM,) * len(outs)),
        scratch_shapes=list(scratch),
        compiler_params=pltpu.CompilerParams(vmem_limit_bytes=mib * 1024 * 1024),
        **options,
    )(*operands)


def near(value):
    return pltpu.with_memory_space_constraint(value, pltpu.VMEM)


def far(value):
    return pltpu.with_memory_space_constraint(value, pltpu.HBM)


def exchange(message, rows):
    moved = lax.all_to_all(message.reshape(CH, rows // 2, 2, 128), CHIPS, split_axis=0, concat_axis=0, tiled=True)
    return moved.reshape(CH * rows, 128)


def partner(value):
    return lax.ppermute(value, "core", [(0, 1), (1, 0)])


def gating(layer, outs, *operands):
    cost = pl.CostEstimate(flops=3 * 2 * PIX * CH * CH, transcendentals=PIX * CH, bytes_accessed=8 * PIX * CH)
    return call(gate_kernel(layer), outs, operands, cost_estimate=cost)


def on_device(pair, residue_mask, hotspot, interface, proj_weight, gate_weight, out_weight):
    send, edge, state = call(
        first_kernel, (SEND, EDGE, STATE),
        (far(residue_mask), far(hotspot), far(interface), far(pair.reshape(PIX, CH)), far(proj_weight)),
        [pltpu.SMEM((768,), jnp.int32), pltpu.SMEM((768,), jnp.int32), pltpu.VMEM((ROWS, COLS), jnp.int32),
         pltpu.VMEM((ROWS, 128), jnp.int32), pltpu.VMEM((PIX, CH), F32), pltpu.VMEM((CH, 4 * CH), F32),
         pltpu.SemaphoreType.DMA((5,))] + PROJECT_SCRATCH,
        [HB] * 5,
    )
    own = exchange(send, 2 * PACK)
    other = partner(own)
    left, *right = call(outgoing_own, (pltpu.VMEM((384, 1024), BF16),) + RIGHT, (near(own),), [WIDE, HALF])
    tri, *_ = call(
        outgoing_kernel, (TRI,) + RIGHT, (near(left), *map(near, right), near(other)), [WIDE] + SEND_SCRATCH,
        out_specs=(HB, VM, VM, VM, VM), input_output_aliases={1: 1, 2: 2, 3: 3, 4: 4},
    )
    tri = exchange(tri, PACK)
    gate, outcat, projcat = gating(0, (GATE, OUTCAT, PROJCAT), near(state), gate_weight, out_weight, proj_weight)
    state, send = call(
        middle_kernel, (STATE, SEND),
        (near(edge), near(tri), near(state), far(gate), far(outcat), far(projcat)),
        [pltpu.VMEM((4 * CH, 3 * CH), BF16), pltpu.SemaphoreType.DMA((1,))] + PROJECT_SCRATCH
        + [pltpu.VMEM((PACK, CH, 128), F32)] + FINISH_SCRATCH,
        [VM, VM, VM, HB, HB, HB],
    )
    own = exchange(send, 2 * PACK)
    other = partner(own)
    part = call(incoming_own, PART, (near(own),), HALF_SCRATCH)
    tri = call(incoming_kernel, TRI, (near(part), near(other)), HALF_SCRATCH + SEND_SCRATCH, out_specs=HB)
    tri = exchange(tri, PACK)
    gate, outcat = gating(1, (STATE, OUTCAT), near(state), gate_weight, out_weight)
    state = call(
        last_kernel, jax.ShapeDtypeStruct((PIX, CH), F32), (near(tri), near(state), near(gate), far(outcat)),
        [pltpu.VMEM((PIX, CH), F32), pltpu.SemaphoreType.DMA((4,))] + FINISH_SCRATCH, [VM, VM, VM, HB], out_specs=HB,
    )
    return state.reshape(ROWS, COLS, CH)


def solution(mesh):
    grid = Mesh(mesh.devices.reshape(8, 2, 2, 4, 2), ("z", "yl", "core", "x", "yh"))
    rows = ("z", "yl", "core")
    cols = ("x", "yh")
    return jax.shard_map(
        on_device,
        mesh=grid,
        in_specs=(P(rows, cols, None), P(), P(), P(rows, cols), P(), P(), P()),
        out_specs=P(rows, cols, None),
        check_vma=False,
    )
```

```python
import jax
import jax.numpy as jnp
from jax import lax
from jax.experimental import pallas as pl
from jax.experimental.pallas import tpu as pltpu
from jax.sharding import Mesh, PartitionSpec as P

EPS = 1e-05
F32 = jnp.float32
BF16 = jnp.bfloat16
ROWS = 24
COLS = 96
PIX = ROWS * COLS
CH = 128
PACK = 18
CHIPS = ("z", "yl", "x", "yh")


def split_bf16(value):
    high = value.astype(BF16)
    low = (value - high.astype(F32)).astype(BF16)
    return high, low


def lanes(shape):
    return lax.broadcasted_iota(jnp.int32, shape, len(shape) - 1)


def matmul(a, b, dims):
    return lax.dot_general(a, b, (dims, ((), ())), preferred_element_type=F32)


def stacked(weight, axis):
    high, low = split_bf16(weight)
    return jnp.concatenate([high, low, high], axis=axis)


def aligned(start, size, unit):
    return pl.ds(pl.multiple_of(start, unit), size)


def packed_edge(mask_sm, hot_sm, inter_ref, edge_ref, rows_ref):
    band = (lax.axis_index("z") * 2 + lax.axis_index("yl")) * 2 + lax.axis_index("core")
    hid = lax.axis_index("x") * 2 + lax.axis_index("yh")
    lane = lanes((1, 128))
    col_mask = jnp.zeros((1, 128), jnp.int32)
    col_hot = jnp.zeros((1, 128), jnp.int32)
    for c in range(COLS):
        col_mask = jnp.where(lane == c, mask_sm[hid * COLS + c], col_mask)
        col_hot = jnp.where(lane == c, hot_sm[hid * COLS + c], col_hot)
    rows_ref[...] = jnp.zeros((ROWS, 128), jnp.int32)
    rows_ref[:, 0:COLS] = inter_ref[...]
    for r in range(ROWS):
        at = slice(r, r + 1)
        flags = jnp.maximum(rows_ref[at, :], jnp.maximum(col_hot, hot_sm[band * ROWS + r]))
        rows_ref[at, :] = flags * col_mask * mask_sm[band * ROWS + r]
    for t in range(PACK):
        tail = pltpu.roll(jnp.broadcast_to(rows_ref[18 + t % 6 : 19 + t % 6, :], (8, 128)), 96 - 32 * (t // 6), 1)
        edge_ref[t : t + 1, :] = jnp.where(lane < COLS, rows_ref[t : t + 1, :], tail[0:1, :]).astype(F32)


def tail_pixels(t):
    return aligned((18 + t % 6) * COLS + 32 * (t // 6), 32, 32)


def normalized(x):
    centred = x - jnp.mean(x, axis=0, keepdims=True)
    variance = jnp.mean(centred * centred, axis=0, keepdims=True)
    high, low = split_bf16(centred * lax.rsqrt(variance + EPS))
    return jnp.concatenate([high, high, low], axis=0)


def project(source, w_cat, edge_ref, mix_ref, send_ref):
    def group(i, carry):
        values = matmul(w_cat, jnp.concatenate([normalized(x) for x in source(i)], axis=1), ((1,), (0,)))
        for half in range(2):
            t = 2 * i + half
            part = values[:, 128 * half : 128 * half + 128]
            edge = edge_ref[pl.ds(t, 1), :]
            left = edge * jax.nn.sigmoid(part[CH : 2 * CH]) * part[:CH]
            right = edge * jax.nn.sigmoid(part[3 * CH :]) * part[2 * CH : 3 * CH]
            mix_ref[pl.ds(t, CH, stride=2 * PACK), :] = left
            mix_ref[pl.ds(t + PACK, CH, stride=2 * PACK), :] = right
        return carry

    lax.fori_loop(0, PACK // 2, group, 0, unroll=True)

    def convert(i, carry):
        at = aligned(i * 256, 256, 256)
        send_ref[at, :] = mix_ref[at, :].astype(BF16)
        return carry

    lax.fori_loop(0, 18, convert, 0, unroll=2)


def first_kernel(mask_hbm, hot_hbm, inter_hbm, pair_hbm, proj_hbm, send_ref, edge_ref, state_ref, mask_sm, hot_sm,
                 inter_ref, rows_ref, pair_ref, proj_ref, sems, mix_ref):
    copies = [
        pltpu.make_async_copy(source, target, sems.at[n])
        for n, (source, target) in enumerate((
            (mask_hbm, mask_sm), (hot_hbm, hot_sm), (inter_hbm, inter_ref), (proj_hbm.at[0], proj_ref),
            (pair_hbm, pair_ref),
        ))
    ]
    for copy in copies:
        copy.start()
    for copy in copies[:3]:
        copy.wait()
    packed_edge(mask_sm, hot_sm, inter_ref, edge_ref, rows_ref)
    copies[3].wait()
    w_cat = stacked(proj_ref[...].T, 1)
    copies[4].wait()

    def source(i):
        for half in range(2):
            t = 2 * i + half
            rows = (pair_ref[aligned(t * COLS, COLS, COLS), :], pair_ref[tail_pixels(t), :])
            x = jnp.concatenate(rows, axis=0).T
            state_ref[t] = x
            yield x

    project(source, w_cat, edge_ref, mix_ref, send_ref)


def gate_kernel(layer):
    def body(state_ref, gatew_ref, outw_ref, *refs):
        if layer == 0:
            proj_ref, gate_ref, outcat_ref, projcat_ref = refs
            projcat_ref[...] = stacked(proj_ref[1].T, 1)
        else:
            gate_ref, outcat_ref = refs
        outcat_ref[...] = stacked(outw_ref[layer].T, 1)
        cat = stacked(gatew_ref[layer].T, 1)

        def step(t, carry):
            gate_ref[t] = jax.nn.sigmoid(matmul(cat, normalized(state_ref[t]), ((1,), (0,))))
            return carry

        lax.fori_loop(0, PACK, step, 0, unroll=3)

    return body


PAD = 8


def widen(source_ref, wide_ref):
    def step(i, carry):
        wide_ref[aligned(PAD + i * 256, 256, 8), :] = source_ref[aligned(i * 256, 256, 256), :].astype(F32)
        return carry

    lax.fori_loop(0, 18, step, 0, unroll=2)


def unpack(wide_ref, base):
    lane = lanes((8, 128))
    sub = lax.broadcasted_iota(jnp.int32, (8, 128), 0)

    def rows(at):
        return wide_ref[pl.ds(base + at, 8), :]

    third = jnp.where(lane < 64, pltpu.roll(rows(4), 64, 1), pltpu.roll(rows(10), 96, 1))
    third = jnp.where(lane < 32, pltpu.roll(rows(-2), 32, 1), third)
    return rows(0), rows(8), jnp.where(sub < 2, rows(16), third)


def place(wide_ref, base, target_ref, start, column, clear):
    lane = lanes((8, 128))
    for n, part in enumerate(unpack(wide_ref, base)):
        if clear:
            part = jnp.where(lane < COLS, part, 0.0)
        target_ref[aligned(start + 8 * n, 8, 8), column] = part


def turned_pair(first, second, shift):
    both = pltpu.roll(jnp.concatenate([first, second], axis=0).astype(BF16), shift, 1).astype(F32)
    return both[0:8], both[8:16]


def tail_slot(half, g):
    return 8 + (half * 8 + g) * 24


def send_tri(tri_ref, mix_ref, tail_ref, ready_ref, out_hbm, sems):
    lane = lanes((8, 128))

    def send(i, carry):
        blocks = [(half, g, (2 * i + half) * 24) for half in range(2) for g in range(8)]
        for n in range(0, 16, 2):
            slots = [tail_slot(half, g) for half, g, _ in blocks[n : n + 2]]
            pair = [tri_ref[g, aligned(base + 16, 8, 8), :] for _, g, base in blocks[n : n + 2]]
            for shift, start in ((32, 10), (64, 4), (96, -2)):
                for slot, value in zip(slots, turned_pair(*pair, shift)):
                    tail_ref[slot + start : slot + start + 8, :] = value
        for half, g, base in blocks:
            slot = tail_slot(half, g)
            target = ((2 * i + half) * 8 + g) * PACK
            for n in range(3):
                tail = tail_ref[slot + 8 * n : slot + 8 * n + 8, :]
                value = jnp.where(lane < COLS, tri_ref[g, aligned(base + 8 * n, 8, 8), :], tail)
                if n < 2:
                    mix_ref[pl.ds(target + 8 * n, 8), :] = value
                else:
                    mix_ref[pl.ds(target + 16, 2), :] = value[0:2]
        at = aligned(i * 288, 288, 288)
        ready_ref[at, :] = mix_ref[at, :].astype(BF16)
        return carry

    copies = []
    for n in range(4):
        lax.fori_loop(2 * n, 2 * n + 2, send, 0)
        at = pl.ds(576 * n, 576)
        copies.append(pltpu.make_async_copy(ready_ref.at[at], out_hbm.at[at], sems.at[n]))
        copies[-1].start()
    for copy in copies:
        copy.wait()


def outgoing_own(own_ref, left_ref, *refs):
    right_refs, (wide_ref, keep_ref) = refs[:4], refs[4:]
    core = lax.axis_index("core")
    widen(own_ref, wide_ref)
    for n, right_ref in enumerate(right_refs):
        for z in range(2):
            right_ref[128 * z + 96 : 128 * z + 128, :] = jnp.zeros((32, 1024), F32)

        def step(c, carry):
            b = 4 * n + c
            start = (c // 2) * 128 + (c % 2) * 48 + core * 24
            for g in range(8):
                at = slice(128 * g, 128 * g + 128)
                message = PAD + (b * 8 + g) * 2 * PACK
                place(wide_ref, message, keep_ref, b * 24, at, False)
                place(wide_ref, message + PACK, right_ref, start, at, True)
            return carry

        lax.fori_loop(0, 4, step, 0, unroll=2)
    left_ref[...] = keep_ref[...].astype(BF16)


def outgoing_kernel(left_ref, _0, _1, _2, _3, other_ref, out_hbm, *refs):
    right_refs, (wide_ref, tri_ref, *scratch) = refs[:4], refs[4:]
    core = lax.axis_index("core")
    widen(other_ref, wide_ref)
    left = left_ref[...]

    lane = lanes((8, 128))
    sub = lax.broadcasted_iota(jnp.int32, (8, 128), 0)

    def fill(n):
        for c in range(4):
            start = (c // 2) * 128 + (c % 2) * 48 + 24 - core * 24
            for g in range(0, 8, 2):
                bases = [PAD + ((4 * n + c) * 8 + g + h) * 2 * PACK + PACK for h in range(2)]

                def moved(at, shift):
                    return turned_pair(*(wide_ref[base + at : base + at + 8, :] for base in bases), shift)

                pieces = moved(-2, 32), moved(4, 64), moved(10, 96)
                for h, base in enumerate(bases):
                    third = jnp.where(lane < 64, pieces[1][h], pieces[2][h])
                    third = jnp.where(lane < 32, pieces[0][h], third)
                    third = jnp.where(sub < 2, wide_ref[base + 16 : base + 24, :], third)
                    column = slice(128 * (g + h), 128 * (g + h) + 128)
                    for m, part in enumerate((wide_ref[base : base + 8, :], wide_ref[base + 8 : base + 16, :], third)):
                        right_refs[n][aligned(start + 8 * m, 8, 8), column] = jnp.where(lane < COLS, part, 0.0)

    fill(0)
    for n in range(4):
        tri = matmul(left, right_refs[n][...].astype(BF16), ((1,), (1,)))
        if n < 3:
            fill(n + 1)
        tri_ref[2 * n] = tri[:, 0:128]
        tri_ref[2 * n + 1] = tri[:, 128:256]
    mix_ref, tail_ref, ready_ref, sems = scratch
    send_tri(tri_ref, mix_ref, tail_ref, ready_ref, out_hbm, sems)


def incoming_half(source_ref, wide_ref, left_ref, right_ref, turn_ref, turned_ref):
    core = lax.axis_index("core")
    widen(source_ref, wide_ref)
    lane = lanes((8, 128))
    keep = lax.broadcasted_iota(jnp.int32, (8, 128), 0) < 6

    def step(b, carry):
        at = aligned(8 * b, 8, 8)
        for g in range(0, 8, 2):
            right = []
            for h in range(2):
                message = PAD + (b * 8 + g + h) * 2 * PACK
                for p in range(3):
                    left_ref[g + h, p, at, :] = wide_ref[pl.ds(message + 6 * p, 8), :]
                right.append([wide_ref[pl.ds(message + PACK + 6 * p, 8), :] for p in range(3)])
            moved = [turned_pair(right[0][p], right[1][p], 32 + 32 * p) for p in range(3)]
            for h in range(2):
                column = slice(128 * (g + h), 128 * (g + h) + 128)
                tail = jnp.where(lane < 64, moved[1][h], moved[2][h])
                right[h].append(jnp.where(lane < 32, moved[0][h], tail))
                for p in range(4):
                    right_ref[p, at, column] = jnp.where(keep, right[h][p], 0.0)
        return carry

    lax.fori_loop(0, 16, step, 0, unroll=2)
    for z in range(8):
        slot = z % 2
        for p in range(3):
            turned = left_ref[z, p].astype(BF16).T.astype(F32)
            turn_ref[slot, p] = turned
            turn_ref[slot, 3, 32 * p : 32 * p + 32, :] = turned[COLS:]
        for y in range(2):
            rows = slice(48 * z + 24 * y, 48 * z + 24 * y + 24)
            for p in range(4):
                turned_ref[rows, 128 * p : 128 * p + 128] = turn_ref[slot, p, aligned(48 * y + 24 * core, 24, 8), :]
    left = turned_ref[...].astype(BF16)
    for n in range(4):
        right = right_ref[:, :, 256 * n : 256 * n + 256].reshape(512, 256).astype(BF16)
        tri = matmul(left, right, ((1,), (0,)))
        yield 2 * n, tri[:, 0:128]
        yield 2 * n + 1, tri[:, 128:256]


def incoming_own(own_ref, part_ref, *scratch):
    for g, tri in incoming_half(own_ref, *scratch):
        part_ref[g] = tri


def incoming_kernel(part_ref, other_ref, out_hbm, wide_ref, left_ref, right_ref, turn_ref, turned_ref, tri_ref,
                    mix_ref, tail_ref, ready_ref, sems):
    for g, tri in incoming_half(other_ref, wide_ref, left_ref, right_ref, turn_ref, turned_ref):
        tri_ref[g] = part_ref[g] + tri
    send_tri(tri_ref, mix_ref, tail_ref, ready_ref, out_hbm, sems)


def finish(tri_ref, state_ref, gate_ref, outcat_hbm, scaled_ref, stat_ref, outcat_ref, fetch_sems, gate_hbm=None, after=()):
    fetches = [] if gate_hbm is None else [pltpu.make_async_copy(outcat_hbm, outcat_ref, fetch_sems.at[3])]
    for n in range(0 if gate_hbm is None else 3):
        at = pl.ds(6 * n, 6)
        fetches.append(pltpu.make_async_copy(gate_hbm.at[at], gate_ref.at[at], fetch_sems.at[n]))
    for fetch in fetches + list(after):
        fetch.start()

    def stats(i, carry):
        total, square = carry
        at = aligned(i * 144, 144, 144)
        t = tri_ref[at, :].astype(F32)
        scaled_ref[at, :] = t
        first, second = t[0:72], t[72:144]
        return total + first + second, square + first * first + second * second

    zero = jnp.zeros((72, 128), F32)
    total, square = lax.fori_loop(0, 16, stats, (zero, zero), unroll=2)
    stat_ref[0, 0:72, :] = total
    stat_ref[1, 0:72, :] = square

    def gather(n):
        return sum(stat_ref[n, 18 * q : 18 * q + 18, :] for q in range(4)) * (1.0 / CH)

    average = gather(0)
    scale = lax.rsqrt(gather(1) - average * average + EPS)
    stat_ref[0, 0:18, :] = average
    stat_ref[1, 0:18, :] = scale
    for fetch in fetches[:1]:
        fetch.wait()
    w_cat = outcat_ref[...]

    def updated(i):
        pieces = []
        for half in range(2):
            t = 2 * i + half
            centred = scaled_ref[pl.ds(t, CH, stride=PACK), :] - stat_ref[0, pl.ds(t, 1), :]
            pieces.append(split_bf16(centred * stat_ref[1, pl.ds(t, 1), :]))
        high = jnp.concatenate([pieces[0][0], pieces[1][0]], axis=1)
        low = jnp.concatenate([pieces[0][1], pieces[1][1]], axis=1)
        values = matmul(w_cat, jnp.concatenate([high, high, low], axis=0), ((1,), (0,)))
        for half in range(2):
            t = 2 * i + half
            yield state_ref[t] + gate_ref[t] * values[:, 128 * half : 128 * half + 128]

    return updated, fetches[1:]


def middle_kernel(edge_ref, tri_ref, state_ref, gate_hbm, outcat_hbm, projcat_hbm, next_ref, send_ref,
                  projcat_ref, sems, mix_ref, gate_ref, *scratch):
    fetch = pltpu.make_async_copy(projcat_hbm, projcat_ref, sems.at[0])
    updated, parts = finish(tri_ref, state_ref, gate_ref, outcat_hbm, *scratch, gate_hbm=gate_hbm, after=(fetch,))

    def combine(i, carry):
        for half, value in enumerate(updated(i)):
            next_ref[2 * i + half] = value
        return carry

    for n, part in enumerate(parts):
        part.wait()
        lax.fori_loop(3 * n, 3 * n + 3, combine, 0, unroll=True)
    fetch.wait()
    project(lambda i: (next_ref[2 * i], next_ref[2 * i + 1]), projcat_ref[...], edge_ref, mix_ref, send_ref)


def last_kernel(tri_ref, state_ref, gate_ref, outcat_ref, out_hbm, next_ref, sems, scaled_ref, stat_ref):
    updated, _ = finish(tri_ref, state_ref, gate_ref, None, scaled_ref, stat_ref, outcat_ref, None)
    copies = []

    def done(n):
        at = pl.ds(n * PIX // 4, PIX // 4)
        copies.append(pltpu.make_async_copy(next_ref.at[at], out_hbm.at[at], sems.at[n]))
        copies[-1].start()

    for i in range(PACK // 2):
        for half, value in enumerate(updated(i)):
            t = 2 * i + half
            value = value.T
            next_ref[t * COLS : t * COLS + COLS, :] = value[:COLS]
            next_ref[tail_pixels(t), :] = value[COLS:]
        if i % 3 == 2:
            done(i // 3)
    done(3)
    for copy in copies:
        copy.wait()


VM = pl.BlockSpec(memory_space=pltpu.VMEM)
SM = pl.BlockSpec(memory_space=pltpu.SMEM)
HB = pl.BlockSpec(memory_space=pltpu.HBM)
STATE = pltpu.VMEM((PACK, CH, 128), F32)
SEND = pltpu.VMEM((CH * 2 * PACK, 128), BF16)
TRI = pltpu.HBM((CH * PACK, 128), BF16)
GATE = pltpu.HBM((PACK, CH, 128), F32)
EDGE = pltpu.VMEM((PACK, 128), F32)
OUTCAT = pltpu.HBM((CH, 3 * CH), BF16)
PROJCAT = pltpu.HBM((4 * CH, 3 * CH), BF16)
PROJECT_SCRATCH = [pltpu.VMEM((CH * 2 * PACK, 128), F32)]
FINISH_SCRATCH = [
    pltpu.VMEM((CH * PACK, 128), F32), pltpu.VMEM((2, 72, 128), F32), pltpu.VMEM((CH, 3 * CH), BF16),
    pltpu.SemaphoreType.DMA((4,)),
]
SEND_SCRATCH = [
    pltpu.VMEM((8, 384, 128), F32), pltpu.VMEM((CH * PACK, 128), F32), pltpu.VMEM((400, 128), F32),
    pltpu.VMEM((CH * PACK, 128), BF16), pltpu.SemaphoreType.DMA((4,)),
]
WIDE = pltpu.VMEM((CH * 2 * PACK + 16, 128), F32)
HALF = pltpu.VMEM((384, 1024), F32)
RIGHT = (pltpu.VMEM((256, 1024), F32),) * 4
HALF_SCRATCH = [
    WIDE, pltpu.VMEM((8, 3, 128, 128), F32), pltpu.VMEM((4, 128, 1024), F32), pltpu.VMEM((2, 4, 128, 128), F32),
    pltpu.VMEM((384, 512), F32),
]
PART = pltpu.VMEM((8, 384, 128), F32)


def call(kernel, out_shape, operands, scratch=(), specs=None, out_specs=None, mib=16, **options):
    outs = out_shape if isinstance(out_shape, tuple) else None
    return pl.pallas_call(
        kernel,
        out_shape=out_shape,
        in_specs=specs or [VM] * len(operands),
        out_specs=out_specs or (VM if outs is None else (VM,) * len(outs)),
        scratch_shapes=list(scratch),
        compiler_params=pltpu.CompilerParams(vmem_limit_bytes=mib * 1024 * 1024),
        **options,
    )(*operands)


def near(value):
    return pltpu.with_memory_space_constraint(value, pltpu.VMEM)


def far(value):
    return pltpu.with_memory_space_constraint(value, pltpu.HBM)


def exchange(message, rows):
    moved = lax.all_to_all(message.reshape(CH, rows // 2, 2, 128), CHIPS, split_axis=0, concat_axis=0, tiled=True)
    return moved.reshape(CH * rows, 128)


def partner(value):
    return lax.ppermute(value, "core", [(0, 1), (1, 0)])


def gating(layer, outs, *operands):
    cost = pl.CostEstimate(flops=3 * 2 * PIX * CH * CH, transcendentals=PIX * CH, bytes_accessed=8 * PIX * CH)
    return call(gate_kernel(layer), outs, operands, cost_estimate=cost)


def on_device(pair, residue_mask, hotspot, interface, proj_weight, gate_weight, out_weight):
    send, edge, state = call(
        first_kernel, (SEND, EDGE, STATE),
        (far(residue_mask), far(hotspot), far(interface), far(pair.reshape(PIX, CH)), far(proj_weight)),
        [pltpu.SMEM((768,), jnp.int32), pltpu.SMEM((768,), jnp.int32), pltpu.VMEM((ROWS, COLS), jnp.int32),
         pltpu.VMEM((ROWS, 128), jnp.int32), pltpu.VMEM((PIX, CH), F32), pltpu.VMEM((CH, 4 * CH), F32),
         pltpu.SemaphoreType.DMA((5,))] + PROJECT_SCRATCH,
        [HB] * 5,
    )
    own = exchange(send, 2 * PACK)
    other = partner(own)
    left, *right = call(outgoing_own, (pltpu.VMEM((384, 1024), BF16),) + RIGHT, (near(own),), [WIDE, HALF])
    tri, *_ = call(
        outgoing_kernel, (TRI,) + RIGHT, (near(left), *map(near, right), near(other)), [WIDE] + SEND_SCRATCH,
        out_specs=(HB, VM, VM, VM, VM), input_output_aliases={1: 1, 2: 2, 3: 3, 4: 4},
    )
    tri = exchange(tri, PACK)
    gate, outcat, projcat = gating(0, (GATE, OUTCAT, PROJCAT), near(state), gate_weight, out_weight, proj_weight)
    state, send = call(
        middle_kernel, (STATE, SEND),
        (near(edge), near(tri), near(state), far(gate), far(outcat), far(projcat)),
        [pltpu.VMEM((4 * CH, 3 * CH), BF16), pltpu.SemaphoreType.DMA((1,))] + PROJECT_SCRATCH
        + [pltpu.VMEM((PACK, CH, 128), F32)] + FINISH_SCRATCH,
        [VM, VM, VM, HB, HB, HB],
    )
    own = exchange(send, 2 * PACK)
    other = partner(own)
    part = call(incoming_own, PART, (near(own),), HALF_SCRATCH)
    tri = call(incoming_kernel, TRI, (near(part), near(other)), HALF_SCRATCH + SEND_SCRATCH, out_specs=HB)
    tri = exchange(tri, PACK)
    gate, outcat = gating(1, (STATE, pltpu.VMEM((CH, 3 * CH), BF16)), near(state), gate_weight, out_weight)
    state = call(
        last_kernel, jax.ShapeDtypeStruct((PIX, CH), F32), (near(tri), near(state), near(gate), near(outcat)),
        [pltpu.VMEM((PIX, CH), F32), pltpu.SemaphoreType.DMA((4,))] + FINISH_SCRATCH[:2], out_specs=HB,
    )
    return state.reshape(ROWS, COLS, CH)


def solution(mesh):
    grid = Mesh(mesh.devices.reshape(8, 2, 2, 4, 2), ("z", "yl", "core", "x", "yh"))
    rows = ("z", "yl", "core")
    cols = ("x", "yh")
    return jax.shard_map(
        on_device,
        mesh=grid,
        in_specs=(P(rows, cols, None), P(), P(), P(rows, cols), P(), P(), P()),
        out_specs=P(rows, cols, None),
        check_vma=False,
    )
```
